32 devices in a mesh: fsdp: 32 (over z, y, x, core).
Axes of the slice: x: 2, y: 2, z: 4, core: 2. Of those that a mesh axis runs over, the one named last changes fastest.
Arguments:
- block_in: bfloat16 [8192, 768], P('fsdp'), may hold values from -6 to 6
- segment_ids: int32 [8192], P('fsdp'), may hold values from 0 to 8191, as said below
- live_count: int32 [32], P('fsdp'), may hold values from 128 to 256, as said below
- norm_gain: bfloat16 [768], P('fsdp'), may hold values from 0.099609375 to 1.8984375
- in_weight: bfloat16 [768, 3352], P('fsdp'), may hold values from -0.21875 to 0.21875
- conv_weight: bfloat16 [1792, 4], P('fsdp'), may hold values from -3 to 3
- conv_bias: bfloat16 [1792], P('fsdp'), may hold values from -3 to 3
- step_bias: float32 [24], replicated, may hold values from -6 to -3
- decay_log: float32 [24], replicated, may hold values from 0 to 2.5
- skip_gain: float32 [24], replicated, may hold values from 0.5 to 1.5
- gated_gain: bfloat16 [1536], P('fsdp'), may hold values from 0.099609375 to 1.8984375
- out_weight: bfloat16 [1536, 768], P('fsdp'), may hold values from -0.15625 to 0.15625
- out_cotangent: bfloat16 [8192, 768], P('fsdp'), may hold values from -6 to 6
Outputs:
- block_out: bfloat16 [8192, 768], P('fsdp')
- input_grad: float32 [8192, 768], P('fsdp')
- norm_gain_grad: float32 [768], P('fsdp')
- in_weight_grad: float32 [768, 3352], P('fsdp')
- conv_weight_grad: float32 [1792, 4], P('fsdp')
- conv_bias_grad: float32 [1792], P('fsdp')
- step_bias_grad: float32 [24], replicated
- decay_log_grad: float32 [24], replicated
- skip_gain_grad: float32 [24], replicated
- gated_gain_grad: float32 [1536], P('fsdp')
- out_weight_grad: float32 [1536, 768], P('fsdp')
The draws below stay inside these ranges and needn't reach their ends.
Inputs may be any that keep to these rules, and one draw needn't show every extreme that they name: `segment_ids`: segment numbers never fall inside a device's 256 slots and no segment spans two devices; a segment holds 1 to 256 slots and one holds exactly 256; a device's first padding slot starts a new segment. `live_count`: live slots come first in each device's 256 slots; one device is full in every draw.
All inputs are finite; a program needn't handle non-finite values.
Results may differ from the reference program's by a relative error of at most 0.0098.
Values may be sent and summed in bfloat16 or wider, within the bound.
A program may use at most 128 MiB of HBM per device.

```python
from functools import partial
import jax
import jax.numpy as jnp
from jax import lax

D = 768
DI = 1536
STATE = 128
HDIM = 64
KCONV = 4
SCAN_BLOCK = 128
TOK_DEV = 256
HEADS = 24
SEQMAX = 256
CONV = 1792
PROJ = 3352
TOKENS = 8192
N_FSDP = 32


def layout_draw(key):
    full_dev = jax.random.randint(jax.random.fold_in(key, 11), (), 0, N_FSDP)
    counts = jax.random.randint(jax.random.fold_in(key, 12), (N_FSDP,), TOK_DEV // 2, TOK_DEV + 1)
    device_ids = jnp.arange(N_FSDP, dtype=jnp.int32)
    counts = jnp.where(device_ids == full_dev, TOK_DEV, counts).astype(jnp.int32)
    slot_index = jnp.arange(TOK_DEV, dtype=jnp.int32)
    coin_draws = jax.random.randint(jax.random.fold_in(key, 13), (N_FSDP, TOK_DEV), 0, SEQMAX)
    protected = (device_ids[:, None] == full_dev) & (slot_index[None, :] < SEQMAX)
    starts = (slot_index[None, :] % SEQMAX == 0) | (slot_index[None, :] == counts[:, None]) | (coin_draws < 3) & jnp.logical_not(protected)
    segment_num = jnp.cumsum(starts.astype(jnp.int32), axis=1) - 1 + device_ids[:, None] * TOK_DEV
    return (counts, segment_num.reshape(-1).astype(jnp.int32))


def draw_live_count(key, part):
    return layout_draw(key)[0]


def draw_segment_ids(key, part):
    return layout_draw(key)[1]


def levels(key, dims, shards, smallest, largest):
    def one(position, parts):
        heights = jax.random.uniform(jax.random.fold_in(jax.random.fold_in(key, 6), position), (parts,), jnp.float32, smallest / len(shards), largest / len(shards))
        return jnp.repeat(jnp.exp(heights), dims[position] // parts).reshape((-1,) + (1,) * (len(dims) - position - 1))

    level = one(*shards[0])
    for cut in shards[1:]:
        level = level * one(*cut)
    return level


def bell_draw(rng, dims, scale, most, cuts=(), kind=jnp.bfloat16):
    entries = jax.random.normal(rng, dims, jnp.float32) * scale
    if len(cuts) > 0:
        entries = levels(rng, dims, cuts, -0.22, 0.18) * entries
    return jnp.clip(entries, min=-most, max=most).astype(kind)


def setup_inputs(seed: int = 0) -> dict:
    splits = jax.random.split(jax.random.key(seed), 14)
    return {
        "block_in": bell_draw(splits[0], (TOKENS, D), 1.0, 6.0, ((0, 32),)),
        "segment_ids": draw_segment_ids(jax.random.fold_in(splits[13], 71), 0),
        "live_count": draw_live_count(jax.random.fold_in(splits[13], 71), 0),
        "norm_gain": jnp.clip(1.0 + 0.18 * jax.random.normal(splits[3], (D,), jnp.float32), 0.099609375, 1.8984375).astype(jnp.bfloat16),
        "in_weight": bell_draw(splits[4], (D, PROJ), D ** -0.5, 0.21875, ((0, 32),)),
        "conv_weight": bell_draw(splits[5], (CONV, KCONV), KCONV ** -0.5, 3.0, ((0, 32),)),
        "conv_bias": bell_draw(splits[6], (CONV,), 0.5, 3.0, ((0, 32),)),
        "step_bias": jnp.clip(jax.random.uniform(splits[7], (HEADS,), jnp.float32, -6.0, -3.0), -6.0, -3.0),
        "decay_log": jnp.clip(jax.random.uniform(splits[8], (HEADS,), jnp.float32, 0.0, 2.5), 0.0, 2.5),
        "skip_gain": jnp.clip(jax.random.uniform(splits[9], (HEADS,), jnp.float32, 0.5, 1.5), 0.5, 1.5),
        "gated_gain": jnp.clip(1.0 + 0.18 * jax.random.normal(splits[10], (DI,), jnp.float32), 0.099609375, 1.8984375).astype(jnp.bfloat16),
        "out_weight": bell_draw(splits[11], (DI, D), DI ** -0.5, 0.15625, ((0, 32),)),
        "out_cotangent": bell_draw(splits[12], (TOKENS, D), 1.0, 6.0, ((0, 32),)),
    }


EPSILON = 1e-05
HIGHEST = lax.Precision.HIGHEST

def rms_scale(values, gain_vec):
    return values * lax.rsqrt(lax.optimization_barrier(jnp.mean(values * values, axis=-1, keepdims=True)) + EPSILON) * gain_vec

def convolve(inputs, kernel_w, kernel_bias, segments):
    length = inputs.shape[0]
    conv_total = kernel_bias[None, :] + kernel_w[:, KCONV - 1][None, :] * inputs
    for offset in range(1, KCONV):
        moved_in = jnp.concatenate([jnp.zeros((offset, inputs.shape[1]), inputs.dtype), inputs[:length - offset]], axis=0)
        earlier = jnp.concatenate([jnp.full((offset,), -1, jnp.int32), segments[:length - offset]], axis=0)
        same_seg = (earlier == segments).astype(inputs.dtype)
        conv_total = conv_total + kernel_w[:, KCONV - 1 - offset][None, :] * moved_in * same_seg[:, None]
    return conv_total

def block_step(carry_state, pieces):
    values, keys_in, queries, step_sizes, logdecay, group_segs, before = pieces
    positions = jnp.arange(SCAN_BLOCK)
    lower_mask = positions[:, None] >= positions[None, :]
    running = jnp.dot(lower_mask.astype(logdecay.dtype), logdecay, precision=HIGHEST)
    same_seg = lower_mask & (group_segs[:, None] == group_segs[None, :])
    spread = running.T[:, :, None] - running.T[:, None, :]
    decay_mat = jnp.where(same_seg[None], jnp.exp(jnp.where(same_seg[None], spread, 0.0)), 0.0)
    intersection = jnp.dot(queries, keys_in.T, precision=HIGHEST)
    weights_all = decay_mat * intersection[None] * step_sizes.T[:, None, :]
    intra_out = jnp.einsum('hts,shp->thp', weights_all, values, precision=HIGHEST)
    carried = (group_segs == before).astype(logdecay.dtype)
    factor = carried[:, None] * jnp.exp(running)
    inter_out = jnp.einsum('tn,hpn->thp', queries, carry_state, precision=HIGHEST) * factor[:, :, None]
    tail_mask = (group_segs == group_segs[-1]).astype(logdecay.dtype)
    towards = jnp.exp(running[-1][None, :] - running) * tail_mask[:, None] * step_sizes
    fresh_state = jnp.einsum('shp,sn->hpn', towards[:, :, None] * values, keys_in, precision=HIGHEST)
    new_state = fresh_state + (carried[-1] * jnp.exp(running[-1]))[:, None, None] * carry_state
    return (new_state, intra_out + inter_out)

def run_mixer(segments, projected, params):
    kernel_w, kernel_bias, bias_step, log_rate, skip_vec, gain_gated = params
    length = projected.shape[0]
    gating = projected[:, :DI]
    conv_in = projected[:, DI:DI + CONV]
    raw_step = projected[:, DI + CONV:]
    activated = jax.nn.silu(convolve(conv_in, kernel_w, kernel_bias, segments))
    values = activated[:, :DI].reshape(length, HEADS, HDIM)
    keys_in = activated[:, DI:DI + STATE]
    queries = activated[:, DI + STATE:]
    step_sizes = jax.nn.softplus(raw_step + bias_step[None, :])
    logdecay = -step_sizes * jnp.exp(log_rate)[None, :]
    block_count = length // SCAN_BLOCK
    group_segs = segments.reshape(block_count, SCAN_BLOCK)
    before = jnp.concatenate([jnp.full((1,), -1, jnp.int32), group_segs[:-1, -1]])
    pieces = (values.reshape(block_count, SCAN_BLOCK, HEADS, HDIM), keys_in.reshape(block_count, SCAN_BLOCK, STATE), queries.reshape(block_count, SCAN_BLOCK, STATE), step_sizes.reshape(block_count, SCAN_BLOCK, HEADS), logdecay.reshape(block_count, SCAN_BLOCK, HEADS), group_segs, before)
    initial_state = jnp.zeros((HEADS, HDIM, STATE), projected.dtype)
    _, outputs = lax.scan(jax.checkpoint(block_step), initial_state, pieces)
    scanned = outputs.reshape(length, HEADS, HDIM) + skip_vec[None, :, None] * values
    gated = scanned.reshape(length, DI) * jax.nn.silu(gating)
    return rms_scale(gated, gain_gated)

def block_pass(weights, inputs, segments, live_total, cotangent):
    in_full, out_full, gain_norm, params = weights
    source = inputs.astype(jnp.float32)
    live_rows = (jnp.arange(TOK_DEV) < live_total).astype(jnp.float32)
    normed = rms_scale(source, gain_norm).astype(jnp.bfloat16)
    projected = jnp.dot(normed, in_full, preferred_element_type=jnp.float32)
    mixer_out, mixer_vjp = jax.vjp(partial(run_mixer, segments), projected, params)
    mixer_low = mixer_out.astype(jnp.bfloat16)
    branch = jnp.dot(mixer_low, out_full, preferred_element_type=jnp.float32)
    output = (source + live_rows[:, None] * branch).astype(jnp.bfloat16)
    masked = jnp.where(live_rows[:, None] > 0, cotangent, jnp.zeros_like(cotangent))
    grad_out_w = jnp.dot(mixer_low.T, masked, preferred_element_type=jnp.float32)
    grad_mixer = jnp.dot(masked, out_full.T, preferred_element_type=jnp.float32)
    grad_proj, grad_params = mixer_vjp(grad_mixer)
    grad_low = grad_proj.astype(jnp.bfloat16)
    grad_in_w = jnp.dot(normed.T, grad_low, preferred_element_type=jnp.float32)
    grad_normed = jnp.dot(grad_low, in_full.T, preferred_element_type=jnp.float32)
    _, norm_vjp = jax.vjp(rms_scale, source, gain_norm)
    grad_source, grad_gain = norm_vjp(grad_normed)
    grad_input = cotangent.astype(jnp.float32) + grad_source
    return (output, grad_input, (grad_gain, grad_in_w, grad_params, grad_out_w))

def reference(block_in, segment_ids, live_count, norm_gain, in_weight, conv_weight, conv_bias, step_bias, decay_log, skip_gain, gated_gain, out_weight, out_cotangent):
    params = (conv_weight.astype(jnp.float32), conv_bias.astype(jnp.float32), step_bias, decay_log, skip_gain, gated_gain.astype(jnp.float32))
    weights = (in_weight, out_weight, norm_gain.astype(jnp.float32), params)

    def per_block(totals, block_items):
        output, grad_input, grads = block_pass(weights, *block_items)
        return (jax.tree.map(jnp.add, totals, grads), (output, grad_input))
    initial = (jnp.zeros((D,), jnp.float32), jnp.zeros((D, PROJ), jnp.float32), jax.tree.map(jnp.zeros_like, params), jnp.zeros((DI, D), jnp.float32))
    block_items = (block_in.reshape(N_FSDP, TOK_DEV, D), segment_ids.reshape(N_FSDP, TOK_DEV), live_count, out_cotangent.reshape(N_FSDP, TOK_DEV, D))
    totals, results = lax.scan(per_block, initial, block_items)
    gain_grad, in_grad, param_grads, out_grad = totals
    outputs, grad_inputs = results
    return (outputs.reshape(TOKENS, D), grad_inputs.reshape(TOKENS, D), gain_grad, in_grad, param_grads[0], param_grads[1], param_grads[2], param_grads[3], param_grads[4], param_grads[5], out_grad)
```

```python
import functools

import jax
import jax.numpy as jnp
from jax import lax
from jax.experimental import pallas as pl
from jax.experimental.pallas import tpu as pltpu
from jax.sharding import PartitionSpec as P

DI = 1536
STATE = 128
HDIM = 64
KCONV = 4
HEADS = 24
CONV = 1792
LANES = 128
EPSILON = 1e-05
HIGHEST = lax.Precision.HIGHEST
F32 = jnp.float32
BF16 = jnp.bfloat16
NT = (((1,), (1,)), ((), ()))
TN = (((0,), (0,)), ((), ()))
MESH = pl.DeviceIdType.MESH


def rms_scale(values, gain_vec):
    return (
        values * lax.rsqrt(jnp.mean(values * values, axis=-1, keepdims=True) + EPSILON) * gain_vec
    )


def dot(a, b, dims=(((1,), (0,)), ((), ()))):
    return lax.dot_general(a.astype(BF16), b.astype(BF16), dims, preferred_element_type=F32)


def sigmoid(v):
    return 1.0 / (1.0 + jnp.exp(-v))


def softplus(v):
    return jnp.maximum(v, 0.0) + jnp.log1p(jnp.exp(-jnp.abs(v)))


def chunk_ds(i):
    return pl.ds(pl.multiple_of(i * LANES, LANES), LANES)


def head_prelude(raw_ref, segc, segr, bias_ref, rate_ref):
    length = raw_ref.shape[0]
    rows = lax.broadcasted_iota(jnp.int32, (length, length), 0)
    cols = lax.broadcasted_iota(jnp.int32, (length, length), 1)
    mask = ((rows >= cols) & (segc == segr)).astype(F32)
    shifted = raw_ref[...] + bias_ref[...]
    step = softplus(shifted)
    decay = -step * rate_ref[...]
    running = jnp.dot(mask, decay, precision=HIGHEST, preferred_element_type=F32)
    return mask, shifted, step, decay, running


def column(values, h):
    lane = lax.broadcasted_iota(jnp.int32, values.shape, 1)
    return jnp.sum(jnp.where(lane == h, values, 0.0), axis=1, keepdims=True)


def decay_of(mask_ref, run_ref, run_t_ref, h):
    spread = column(run_ref[...], h) - run_t_ref[pl.ds(h, 1), :]
    mask = mask_ref[...]
    return jnp.where(mask > 0, jnp.exp(jnp.where(mask > 0, spread, 0.0)), 0.0)


def forward_kernel(
    proj_ref, raw_ref, segc_ref, segr_ref, shift_ref, cw_ref, bias_ref, rate_ref, skip_ref, gain_ref,
    pre_ref, scan_ref, low_ref,
    mask_s, run_s, runt_s, stept_s, inter_s, gated_s,
):
    length = proj_ref.shape[0]
    mask, _, step, _, running = head_prelude(
        raw_ref, segc_ref[...], segr_ref[...], bias_ref, rate_ref
    )
    mask_s[...] = mask
    run_s[...] = running
    runt_s[...] = running.T
    stept_s[...] = step.T

    def conv(i, _):
        ds = chunk_ds(i)
        x = proj_ref[:, chunk_ds(i + DI // LANES)]
        total = cw_ref[KCONV : KCONV + 1, ds] + cw_ref[KCONV - 1 : KCONV, ds] * x
        for j in range(1, KCONV):
            moved = pltpu.roll(x, j, 0) * shift_ref[:, j - 1 : j]
            total = total + cw_ref[KCONV - 1 - j : KCONV - j, ds] * moved
        pre_ref[:, ds] = total
        return 0

    lax.fori_loop(0, CONV // LANES, conv, 0)
    pre_k = pre_ref[:, DI : DI + STATE]
    pre_q = pre_ref[:, DI + STATE :]
    inter_s[...] = dot(pre_q * sigmoid(pre_q), pre_k * sigmoid(pre_k), NT)

    def pair(i, sumsq):
        ds = chunk_ds(i)
        pre = pre_ref[:, ds]
        values = pre * sigmoid(pre)
        low = values.astype(BF16)
        outs = []
        for side in range(2):
            h = 2 * i + side
            weights = decay_of(mask_s, run_s, runt_s, h) * inter_s[...] * stept_s[pl.ds(h, 1), :]
            outs.append(dot(weights, low))
        lane = lax.broadcasted_iota(jnp.int32, (length, LANES), 1)
        scanned = jnp.where(lane < HDIM, outs[0], outs[1]) + skip_ref[:, ds] * values
        scan_ref[:, ds] = scanned
        z = proj_ref[:, ds]
        gated = scanned * (z * sigmoid(z))
        gated_s[:, ds] = gated
        return sumsq + gated * gated

    sumsq = lax.fori_loop(0, DI // LANES, pair, jnp.zeros((length, LANES), F32))
    scale = lax.rsqrt(jnp.sum(sumsq, axis=1, keepdims=True) / DI + EPSILON)

    def finish(i, _):
        ds = chunk_ds(i)
        low_ref[:, ds] = (gated_s[:, ds] * scale * gain_ref[:, ds]).astype(BF16)
        return 0

    lax.fori_loop(0, DI // LANES, finish, 0)


def backward_kernel(
    proj_ref, raw_ref, segc_ref, segr_ref, shift_ref, cw_ref, bias_ref, rate_ref, skip_ref, gain_ref,
    pre_ref, scan_ref, gm_ref,
    glow_ref, graw_ref, gconv_ref, gdi_ref, ghead_ref,
    mask_s, run_s, runt_s, stept_s, inter_s, dinter_s, row_s, col_s,
):
    length = proj_ref.shape[0]
    mask, shifted, step, decay, running = head_prelude(
        raw_ref, segc_ref[...], segr_ref[...], bias_ref, rate_ref
    )
    mask_s[...] = mask
    run_s[...] = running
    runt_s[...] = running.T
    stept_s[...] = step.T
    pre_k = pre_ref[:, DI : DI + STATE]
    pre_q = pre_ref[:, DI + STATE :]
    keys = (pre_k * sigmoid(pre_k)).astype(BF16)
    queries = (pre_q * sigmoid(pre_q)).astype(BF16)
    inter_s[...] = dot(queries, keys, NT)
    dinter_s[...] = jnp.zeros_like(dinter_s)
    row_s[...] = jnp.zeros_like(row_s)
    col_s[...] = jnp.zeros_like(col_s)
    gconv_ref[...] = jnp.zeros_like(gconv_ref)
    gdi_ref[...] = jnp.zeros_like(gdi_ref)
    ghead_ref[...] = jnp.zeros_like(ghead_ref)

    def sums(i, carry):
        sumsq, inner = carry
        ds = chunk_ds(i)
        z = proj_ref[:, ds]
        gated = scan_ref[:, ds] * (z * sigmoid(z))
        return sumsq + gated * gated, inner + gated * gm_ref[:, ds] * gain_ref[:, ds]

    zero = jnp.zeros((length, LANES), F32)
    sumsq, inner = lax.fori_loop(0, DI // LANES, sums, (zero, zero))
    scale = lax.rsqrt(jnp.sum(sumsq, axis=1, keepdims=True) / DI + EPSILON)
    coef = scale * scale * scale * (jnp.sum(inner, axis=1, keepdims=True) / DI)

    def conv_back(i, grad_act):
        ds = chunk_ds(i)
        wide = chunk_ds(i + DI // LANES)
        pre = pre_ref[:, ds]
        sg = sigmoid(pre)
        gpre = grad_act * (sg * (1.0 + pre * (1.0 - sg)))
        x = proj_ref[:, wide]
        total = cw_ref[KCONV - 1 : KCONV, ds] * gpre
        gconv_ref[KCONV : KCONV + 1, ds] = jnp.sum(gpre, axis=0, keepdims=True)
        gconv_ref[KCONV - 1 : KCONV, ds] = jnp.sum(gpre * x, axis=0, keepdims=True)
        for j in range(1, KCONV):
            live = gpre * shift_ref[:, j - 1 : j]
            back = pltpu.roll(live, length - j, 0)
            total = total + cw_ref[KCONV - 1 - j : KCONV - j, ds] * back
            gconv_ref[KCONV - 1 - j : KCONV - j, ds] = jnp.sum(back * x, axis=0, keepdims=True)
        glow_ref[:, wide] = total.astype(BF16)

    def pair(i, _):
        ds = chunk_ds(i)
        z = proj_ref[:, ds]
        sz = sigmoid(z)
        silu_z = z * sz
        scanned = scan_ref[:, ds]
        gated = scanned * silu_z
        grad_out = gm_ref[:, ds]
        gdi_ref[0:1, ds] = jnp.sum(grad_out * gated * scale, axis=0, keepdims=True)
        dgated = scale * (grad_out * gain_ref[:, ds]) - gated * coef
        dscan = dgated * silu_z
        glow_ref[:, ds] = (dgated * scanned * (sz * (1.0 + z * (1.0 - sz)))).astype(BF16)
        pre = pre_ref[:, ds]
        values = pre * sigmoid(pre)
        gdi_ref[1:2, ds] = jnp.sum(dscan * values, axis=0, keepdims=True)
        low = values.astype(BF16)
        dlow = dscan.astype(BF16)
        lane = lax.broadcasted_iota(jnp.int32, (length, LANES), 1)
        head_lane = lax.broadcasted_iota(jnp.int32, (length, LANES), 1)
        outs = []
        for side in range(2):
            h = 2 * i + side
            here = (lane < HDIM) if side == 0 else (lane >= HDIM)
            factor = decay_of(mask_s, run_s, runt_s, h)
            stept = stept_s[pl.ds(h, 1), :]
            inter = inter_s[...]
            scaled = factor * stept
            outs.append(dot(scaled * inter, dlow, TN))
            dweights = dot(jnp.where(here, dscan, 0.0), low, NT)
            dinter_s[...] += dweights * scaled
            pairs = dweights * factor * inter
            col_s[pl.ds(h, 1), :] = jnp.sum(pairs, axis=0, keepdims=True)
            row = jnp.sum(pairs * stept, axis=1, keepdims=True)
            row_s[...] += jnp.where(head_lane == h, row, 0.0)
        grad_values = jnp.where(lane < HDIM, outs[0], outs[1]) + skip_ref[:, ds] * dscan
        conv_back(i, grad_values)
        return 0

    lax.fori_loop(0, DI // LANES, pair, 0)
    dinter = dinter_s[...].astype(BF16)
    conv_back(DI // LANES, dot(dinter, queries, TN))
    conv_back(DI // LANES + 1, dot(dinter, keys))
    dstep = col_s[...].T
    drun = row_s[...] - dstep * step
    ddecay = lax.dot_general(
        mask_s[...], drun, TN, precision=HIGHEST, preferred_element_type=F32
    )
    dstep = dstep - ddecay * rate_ref[...]
    graw = dstep * sigmoid(shifted)
    graw_ref[...] = graw.astype(BF16)
    ghead_ref[0:1, :] = jnp.sum(graw, axis=0, keepdims=True)
    ghead_ref[1:2, :] = jnp.sum(ddecay * decay, axis=0, keepdims=True)


def forward_mixer(proj, raw, small):
    length = proj.shape[0]
    vec = pltpu.VMEM
    return pl.pallas_call(
        forward_kernel,
        out_shape=(
            jax.ShapeDtypeStruct((length, CONV), F32),
            jax.ShapeDtypeStruct((length, DI), F32),
            jax.ShapeDtypeStruct((length, DI), BF16),
        ),
        in_specs=[pl.BlockSpec(memory_space=vec)] * 10,
        out_specs=[pl.BlockSpec(memory_space=vec)] * 3,
        scratch_shapes=[
            pltpu.VMEM((length, length), F32),
            pltpu.VMEM((length, LANES), F32),
            pltpu.VMEM((LANES, length), F32),
            pltpu.VMEM((LANES, length), F32),
            pltpu.VMEM((length, length), F32),
            pltpu.VMEM((length, DI), F32),
        ],
        compiler_params=pltpu.CompilerParams(vmem_limit_bytes=40 * 2**20),
        cost_estimate=pl.CostEstimate(
            flops=HEADS * length * length * 280, bytes_accessed=length * 30000, transcendentals=0
        ),
        name="mixer_forward",
    )(proj, raw, *small)


def backward_mixer(proj, raw, small, pre, scanned, grad_mixer):
    length, width = proj.shape[0], DI + CONV
    vec = pltpu.VMEM
    return pl.pallas_call(
        backward_kernel,
        out_shape=(
            jax.ShapeDtypeStruct((length, width), BF16),
            jax.ShapeDtypeStruct((length, LANES), BF16),
            jax.ShapeDtypeStruct((8, CONV), F32),
            jax.ShapeDtypeStruct((8, DI), F32),
            jax.ShapeDtypeStruct((8, LANES), F32),
        ),
        in_specs=[pl.BlockSpec(memory_space=vec)] * 13,
        out_specs=[pl.BlockSpec(memory_space=vec)] * 5,
        scratch_shapes=[
            pltpu.VMEM((length, length), F32),
            pltpu.VMEM((length, LANES), F32),
            pltpu.VMEM((LANES, length), F32),
            pltpu.VMEM((LANES, length), F32),
            pltpu.VMEM((length, length), F32),
            pltpu.VMEM((length, length), F32),
            pltpu.VMEM((length, LANES), F32),
            pltpu.VMEM((LANES, length), F32),
        ],
        compiler_params=pltpu.CompilerParams(vmem_limit_bytes=40 * 2**20),
        cost_estimate=pl.CostEstimate(
            flops=HEADS * length * length * 800, bytes_accessed=length * 60000, transcendentals=0
        ),
        name="mixer_backward",
    )(proj, raw, *small, pre, scanned, grad_mixer)


def place(n):
    me = lax.axis_index("fsdp")
    core, chip = lax.rem(me, 2), lax.div(me, 2)
    plane, line = split(n)
    return me, core, lax.rem(chip, plane), lax.div(chip, plane)


def split(n):
    half = n // 2
    plane = 4 if half % 4 == 0 else 1
    return plane, half // plane


def loop(count, step):
    def body(k, _):
        step(k)
        return 0

    lax.fori_loop(0, count, body, 0)


def greet(n, me, core, spot, rank):
    plane, line = split(n)
    barrier = pltpu.get_barrier_semaphore()

    def signal(device):
        pl.semaphore_signal(barrier, inc=1, device_id=(device,), device_id_type=MESH)

    signal(me + 1 - 2 * core)
    for j in range(plane - 1):
        signal(2 * (rank * plane + lax.rem(spot + 1 + j, plane)) + core)
    loop(line - 1, lambda r: signal(2 * (lax.rem(rank + 1 + r, line) * plane + spot) + core))
    pl.semaphore_wait(barrier, plane + line - 1)


def gather_kernel(
    n, x0, x1, x2, o0, o1, o2, own_sem, s_line, r_line, s_plane, r_plane, s_near, r_near
):
    plane, line = split(n)
    me, core, spot, rank = place(n)
    partner = me + 1 - 2 * core
    greet(n, me, core, spot, rank)
    groups = ((x0, o0), (x1, o1), (x2, o2))

    def send(g, src, slot, sems, index, device):
        return pltpu.make_async_remote_copy(
            src_ref=src,
            dst_ref=groups[g][1].at[slot],
            send_sem=sems[0].at[g, index],
            recv_sem=sems[1].at[g, index],
            device_id=(device,),
            device_id_type=MESH,
        )

    def origin(r, j):
        from_rank = lax.rem(rank + 2 * line - 1 - r, line)
        return 2 * (from_rank * plane + lax.rem(spot + 2 * plane - 1 - j, plane))

    def along(g, r, slot):
        device = 2 * (lax.rem(rank + 1 + r, line) * plane + spot) + core
        return send(g, groups[g][0], slot, (s_line, r_line), r, device)

    def across(g, r, j, src, slot):
        device = 2 * (rank * plane + lax.rem(spot + 1 + j, plane)) + core
        return send(g, src, slot, (s_plane, r_plane), plane * r + j, device)

    def near(g, r, j, src, slot):
        return send(g, src, slot, (s_near, r_near), plane * r + j, partner)

    def start_along(r):
        for g in range(3):
            along(g, r, me).start()

    loop(line - 1, start_along)
    for g in range(3):
        x = groups[g][0]
        for j in range(plane - 1):
            across(g, line - 1, j, x, me).start()
        near(g, line - 1, plane - 1, x, me).start()
        pltpu.make_async_copy(x, groups[g][1].at[me], own_sem.at[g]).start()

    def forward(r):
        for j in range(plane - 1):
            slot = origin(r, j) + core
            for g in range(3):
                block = groups[g][1].at[slot]
                across(g, r, j, block, slot).wait_recv()
                near(g, r, j, block, slot).start()

    def spread(r):
        slot = origin(r, plane - 1) + core
        for g in range(3):
            block = groups[g][1].at[slot]
            along(g, r, slot).wait_recv()
            for j in range(plane - 1):
                across(g, r, j, block, slot).start()
            near(g, r, plane - 1, block, slot).start()
        forward(lax.rem(r + line - 1, line))

    loop(line - 1, spread)
    forward((line - 2) % line)

    def drain(r):
        for j in range(plane):
            slot, other = origin(r, j) + core, origin(r, j) + 1 - core
            for g in range(3):
                block = groups[g][1].at[slot]
                near(g, r, j, block, other).wait_recv()
                near(g, r, j, block, slot).wait_send()
                if j < plane - 1:
                    across(g, r, j, block, slot).wait_send()

    loop(line, drain)

    def drain_along(r):
        for g in range(3):
            along(g, r, me).wait_send()

    loop(line - 1, drain_along)
    for g in range(3):
        pltpu.make_async_copy(groups[g][0], groups[g][1].at[me], own_sem.at[g]).wait()


def gather_plus(n, x0, x1, x2, *refs):
    fin = refs[:10]
    gm = refs[10]
    o0, o1, o2, pre, scan, low, glow, graw, gconv, gdi, ghead = refs[11:22]
    sems = refs[22:29]
    fs = refs[29:35]
    bs = refs[35:]
    gather_kernel(n, x0, x1, x2, o0, o1, o2, *sems)
    forward_kernel(*fin, pre, scan, low, *fs)
    backward_kernel(*fin, pre, scan, gm, glow, graw, gconv, gdi, ghead, *bs)


def reduce_kernel(
    n, a0, a1, a2, o0, o1, o2, p0, p1, p2, t0, t1, t2, q0, q1, q2,
    u0, u1, u2, v0, v1, v2, w0, w1, w2,
    s_near, r_near, s_plane, r_plane, s_line, r_line,
):
    plane, line = split(n)
    me, core, spot, rank = place(n)
    partner = me + 1 - 2 * core
    greet(n, me, core, spot, rank)
    groups = (
        (a0, o0, p0, t0, q0, u0, v0, w0),
        (a1, o1, p1, t1, q1, u1, v1, w1),
        (a2, o2, p2, t2, q2, u2, v2, w2),
    )

    def send(src, dst, sems, g, index, device):
        return pltpu.make_async_remote_copy(
            src_ref=src.at[index] if not isinstance(src, tuple) else src[0].at[src[1]],
            dst_ref=dst.at[index],
            send_sem=sems[0].at[g, index],
            recv_sem=sems[1].at[g, index],
            device_id=(device,),
            device_id_type=MESH,
        )

    def owner(r, j):
        return 2 * (lax.rem(rank + 1 + r, line) * plane + lax.rem(spot + 1 + j, plane))

    def near(g, r, j):
        src = (groups[g][0], owner(r, j) + 1 - core)
        return send(src, groups[g][2], (s_near, r_near), g, plane * r + j, partner)

    def across(g, r, j):
        device = 2 * (rank * plane + lax.rem(spot + 1 + j, plane)) + core
        return send(groups[g][3], groups[g][4], (s_plane, r_plane), g, plane * r + j, device)

    def along(g, r):
        device = 2 * (lax.rem(rank + 1 + r, line) * plane + spot) + core
        return send(groups[g][6], groups[g][7], (s_line, r_line), g, r, device)

    def both(g, r, j):
        near(g, r, j).wait_recv()
        return groups[g][0][owner(r, j) + core].astype(F32) + groups[g][2][plane * r + j].astype(F32)

    def start_near(r):
        for j in range(plane):
            for g in range(3):
                near(g, r, j).start()

    loop(line, start_near)

    def pairs(r):
        for j in range(plane):
            for g in range(3):
                if j < plane - 1:
                    sums = groups[g][3]
                    sums[plane * r + j] = both(g, r, j).astype(sums.dtype)
                else:
                    groups[g][5][r] = both(g, r, j)
            if j > 0:
                for g in range(3):
                    across(g, r, j - 1).start()

    def total(g, r):
        result = groups[g][5][r]
        for j in range(plane - 1):
            across(g, r, j).wait_recv()
            result = result + groups[g][4][plane * r + j].astype(F32)
        return result

    def planes(r):
        for g in range(3):
            sums = groups[g][6]
            sums[r] = total(g, r).astype(sums.dtype)
        for g in range(3):
            along(g, r).start()

    def step(r):
        pairs(r)

        @pl.when(r > 0)
        def _():
            planes(r - 1)

    loop(line, step)
    for g in range(3):
        groups[g][1][...] = total(g, line - 1)

    def collect(r):
        for g in range(3):
            along(g, r).wait_recv()
            groups[g][1][...] += groups[g][7][r].astype(F32)

    loop(line - 1, collect)

    def drain(r):
        for g in range(3):
            for j in range(plane):
                near(g, r, j).wait_send()
                if j < plane - 1:
                    across(g, r, j).wait_send()

    loop(line, drain)

    def drain_along(r):
        for g in range(3):
            along(g, r).wait_send()

    loop(line - 1, drain_along)


def gather_all(n, shards, dummy):
    vmem = pl.BlockSpec(memory_space=pltpu.VMEM)
    half, (_, line) = n // 2, split(n)
    length = dummy[0].shape[0]
    return pl.pallas_call(
        functools.partial(gather_plus, n),
        out_shape=tuple(jax.ShapeDtypeStruct((n,) + x.shape, x.dtype) for x in shards) + (
            jax.ShapeDtypeStruct((length, CONV), F32),
            jax.ShapeDtypeStruct((length, DI), F32),
            jax.ShapeDtypeStruct((length, DI), BF16),
            jax.ShapeDtypeStruct((length, DI + CONV), BF16),
            jax.ShapeDtypeStruct((length, LANES), BF16),
            jax.ShapeDtypeStruct((8, CONV), F32),
            jax.ShapeDtypeStruct((8, DI), F32),
            jax.ShapeDtypeStruct((8, LANES), F32),
        ),
        in_specs=[vmem] * 14,
        out_specs=[vmem] * 11,
        scratch_shapes=[
            pltpu.SemaphoreType.DMA((3,)),
            pltpu.SemaphoreType.DMA((3, line)),
            pltpu.SemaphoreType.DMA((3, line)),
            pltpu.SemaphoreType.DMA((3, half)),
            pltpu.SemaphoreType.DMA((3, half)),
            pltpu.SemaphoreType.DMA((3, half)),
            pltpu.SemaphoreType.DMA((3, half)),
            pltpu.VMEM((length, length), F32),
            pltpu.VMEM((length, LANES), F32),
            pltpu.VMEM((LANES, length), F32),
            pltpu.VMEM((LANES, length), F32),
            pltpu.VMEM((length, length), F32),
            pltpu.VMEM((length, DI), F32),
            pltpu.VMEM((length, length), F32),
            pltpu.VMEM((length, LANES), F32),
            pltpu.VMEM((LANES, length), F32),
            pltpu.VMEM((LANES, length), F32),
            pltpu.VMEM((length, length), F32),
            pltpu.VMEM((length, length), F32),
            pltpu.VMEM((length, LANES), F32),
            pltpu.VMEM((LANES, length), F32),
        ],
        compiler_params=pltpu.CompilerParams(
            collective_id=0, has_side_effects=True, vmem_limit_bytes=60 * 2**20
        ),
        name="gather_all",
    )(*shards, *dummy)


def reduce_all(n, terms):
    vmem = pl.BlockSpec(memory_space=pltpu.VMEM)
    half, (_, line) = n // 2, split(n)
    slots = [pltpu.VMEM((half,) + x.shape[1:], x.dtype) for x in terms]
    partial_sums = [pltpu.VMEM((line,) + x.shape[1:], F32) for x in terms]
    lines = [pltpu.VMEM((line,) + x.shape[1:], x.dtype) for x in terms]
    return pl.pallas_call(
        functools.partial(reduce_kernel, n),
        out_shape=tuple(jax.ShapeDtypeStruct(x.shape[1:], F32) for x in terms),
        in_specs=[vmem] * 3,
        out_specs=[vmem] * 3,
        scratch_shapes=slots * 3
        + partial_sums
        + lines * 2
        + [pltpu.SemaphoreType.DMA((3, half))] * 4
        + [pltpu.SemaphoreType.DMA((3, line))] * 2,
        compiler_params=pltpu.CompilerParams(
            collective_id=1, has_side_effects=True, vmem_limit_bytes=60 * 2**20
        ),
        name="reduce_all",
    )(*terms)


def per_device(
    block_in,
    segment_ids,
    live_count,
    norm_gain,
    in_weight,
    conv_weight,
    conv_bias,
    step_bias,
    decay_log,
    skip_gain,
    gated_gain,
    out_weight,
    out_cotangent,
):
    devices = lax.axis_size("fsdp")
    length = block_in.shape[0]
    share, proj_width = in_weight.shape
    width = block_in.shape[1]
    smalls = jnp.concatenate(
        [norm_gain, conv_weight.T.reshape(-1), conv_bias, gated_gain]
    )
    small_rows = -(-smalls.shape[0] // (8 * LANES)) * 8
    smalls = jnp.pad(smalls, (0, small_rows * LANES - smalls.shape[0])).reshape(small_rows, LANES)
    z = lambda *d: jnp.zeros(d, F32) + block_in[0, 0].astype(F32)
    zi = lambda *d: jnp.zeros(d, jnp.int32) + segment_ids[0]
    dummy = (z(length, DI + CONV), z(length, LANES), zi(length, 1), zi(1, length), z(length, 8),
             z(8, CONV), z(1, LANES), z(1, LANES), z(1, DI), z(1, DI), z(length, DI))
    in_blocks, out_blocks, rest, *extra = gather_all(devices, (in_weight, out_weight, smalls), dummy)
    in_full = in_blocks.reshape(devices * share, proj_width)
    out_full = out_blocks.reshape(devices * out_weight.shape[0], width)
    rest = rest.reshape(devices, -1).astype(F32)
    a = norm_gain.shape[0]
    b = a + conv_weight.size
    c = b + conv_bias.shape[0]
    d = c + gated_gain.shape[0]
    gain_norm = rest[:, :a].reshape(-1)
    kernel_rows = jnp.moveaxis(rest[:, a:b].reshape(devices, KCONV, -1), 1, 0).reshape(KCONV, CONV)
    kernel_bias = rest[:, b:c].reshape(1, CONV)
    gated = rest[:, c:d].reshape(1, DI)
    conv_rows = jnp.concatenate([kernel_rows, kernel_bias, jnp.zeros((3, CONV), F32)], axis=0)

    def lanes(v):
        return jnp.pad(v, (0, LANES - v.shape[0])).reshape(1, LANES)

    slots = jnp.arange(length)
    shift = jnp.stack(
        [
            ((slots >= j) & (jnp.roll(segment_ids, j) == segment_ids)).astype(F32)
            for j in range(1, KCONV)
        ],
        axis=1,
    )
    shift = jnp.pad(shift, ((0, 0), (0, 8 - shift.shape[1])))
    small = (
        segment_ids.reshape(length, 1),
        segment_ids.reshape(1, length),
        shift,
        conv_rows,
        lanes(step_bias),
        lanes(jnp.exp(decay_log)),
        jnp.repeat(skip_gain, HDIM).reshape(1, DI),
        gated,
    )
    source = block_in.astype(F32)
    live_rows = (lax.iota(jnp.int32, length) < live_count[0]).astype(F32)
    masked = jnp.where(live_rows[:, None] > 0, out_cotangent, jnp.zeros_like(out_cotangent))
    normed = rms_scale(source, gain_norm).astype(BF16)
    main = DI + CONV
    projected = jnp.dot(normed, in_full[:, :main], preferred_element_type=F32)
    tail = jnp.pad(in_full[:, main:], ((0, 0), (0, LANES - HEADS)))
    raw = jnp.dot(normed, tail, preferred_element_type=F32)
    grad_mixer = lax.dot_general(masked, out_full, NT, preferred_element_type=F32)
    pre, scanned, mixer_low = forward_mixer(projected, raw, small)
    grad_out_w = lax.dot_general(mixer_low, masked, TN, preferred_element_type=F32)
    branch = jnp.dot(mixer_low, out_full, preferred_element_type=F32)
    output = (source + live_rows[:, None] * branch).astype(BF16)
    glow, graw, gconv, gdi, ghead = backward_mixer(projected, raw, small, pre, scanned, grad_mixer)
    grad_low = jnp.concatenate([glow, graw], axis=1)
    grad_in_w = lax.dot_general(normed, grad_low, TN, preferred_element_type=F32)
    grad_normed = lax.dot_general(glow, in_full[:, :main], NT, preferred_element_type=F32)
    grad_normed = grad_normed + lax.dot_general(graw, tail, NT, preferred_element_type=F32)
    _, norm_vjp = jax.vjp(rms_scale, source, gain_norm)
    grad_source, grad_gain = norm_vjp(grad_normed)
    grad_input = out_cotangent.astype(F32) + grad_source
    skip_part = gdi[1].reshape(HEADS, HDIM).sum(axis=1)
    heads = jnp.concatenate([ghead[0, :HEADS], ghead[1, :HEADS], skip_part])
    rows = jnp.concatenate(
        [
            grad_gain.reshape(devices, -1),
            jnp.moveaxis(gconv[:KCONV].reshape(KCONV, devices, -1), 0, 1).reshape(devices, -1),
            gconv[KCONV].reshape(devices, -1),
            gdi[0].reshape(devices, -1),
            jnp.broadcast_to(heads, (devices, heads.shape[0])),
        ],
        axis=1,
    )
    sum_rows = -(-rows.shape[1] // (8 * LANES)) * 8
    rows = jnp.pad(rows, ((0, 0), (0, sum_rows * LANES - rows.shape[1])))
    in_share, out_share, mine = reduce_all(
        devices,
        (
            grad_in_w.astype(BF16).reshape(devices, share, -1),
            grad_out_w.astype(BF16).reshape(devices, -1, width),
            rows.reshape(devices, sum_rows, LANES),
        ),
    )
    in_share = in_share[:, :proj_width]
    mine = mine.reshape(-1)
    head_sums = mine[d : d + 3 * HEADS].reshape(3, HEADS)
    return (
        output,
        grad_input,
        mine[:a],
        in_share,
        mine[a:b].reshape(KCONV, -1).T,
        mine[b:c],
        head_sums[0],
        head_sums[1],
        head_sums[2],
        mine[c:d],
        out_share,
    )


def solution(mesh):
    rows, vec, whole = P("fsdp", None), P("fsdp"), P()
    in_specs = (rows, vec, vec, vec, rows, rows, vec, whole, whole, whole, vec, rows, rows)
    out_specs = (rows, rows, vec, rows, rows, vec, whole, whole, whole, vec, rows)
    return jax.shard_map(
        per_device, mesh=mesh, in_specs=in_specs, out_specs=out_specs, check_vma=False
    )
```

```python
import functools

import jax
import jax.numpy as jnp
from jax import lax
from jax.experimental import pallas as pl
from jax.experimental.pallas import tpu as pltpu
from jax.sharding import PartitionSpec as P

DI = 1536
STATE = 128
HDIM = 64
KCONV = 4
HEADS = 24
CONV = 1792
LANES = 128
EPSILON = 1e-05
HIGHEST = lax.Precision.HIGHEST
F32 = jnp.float32
BF16 = jnp.bfloat16
NT = (((1,), (1,)), ((), ()))
TN = (((0,), (0,)), ((), ()))
MESH = pl.DeviceIdType.MESH


def rms_scale(values, gain_vec):
    return (
        values * lax.rsqrt(jnp.mean(values * values, axis=-1, keepdims=True) + EPSILON) * gain_vec
    )


def dot(a, b, dims=(((1,), (0,)), ((), ()))):
    return lax.dot_general(a.astype(BF16), b.astype(BF16), dims, preferred_element_type=F32)


def sigmoid(v):
    return 1.0 / (1.0 + jnp.exp(-v))


def softplus(v):
    return jnp.maximum(v, 0.0) + jnp.log1p(jnp.exp(-jnp.abs(v)))


def chunk_ds(i):
    return pl.ds(pl.multiple_of(i * LANES, LANES), LANES)


def head_prelude(raw_ref, segc, segr, bias_ref, rate_ref):
    length = raw_ref.shape[0]
    rows = lax.broadcasted_iota(jnp.int32, (length, length), 0)
    cols = lax.broadcasted_iota(jnp.int32, (length, length), 1)
    mask = ((rows >= cols) & (segc == segr)).astype(F32)
    shifted = raw_ref[...] + bias_ref[...]
    step = softplus(shifted)
    decay = -step * rate_ref[...]
    running = jnp.dot(mask, decay, precision=HIGHEST, preferred_element_type=F32)
    return mask, shifted, step, decay, running


def column(values, h):
    lane = lax.broadcasted_iota(jnp.int32, values.shape, 1)
    return jnp.sum(jnp.where(lane == h, values, 0.0), axis=1, keepdims=True)


def decay_of(mask_ref, run_ref, run_t_ref, h):
    spread = column(run_ref[...], h) - run_t_ref[pl.ds(h, 1), :]
    mask = mask_ref[...]
    return jnp.where(mask > 0, jnp.exp(jnp.where(mask > 0, spread, 0.0)), 0.0)


def forward_kernel(
    proj_ref, raw_ref, segc_ref, segr_ref, shift_ref, cw_ref, bias_ref, rate_ref, skip_ref, gain_ref,
    pre_ref, scan_ref, low_ref,
    mask_s, run_s, runt_s, stept_s, inter_s, gated_s,
):
    length = proj_ref.shape[0]
    mask, _, step, _, running = head_prelude(
        raw_ref, segc_ref[...], segr_ref[...], bias_ref, rate_ref
    )
    mask_s[...] = mask
    run_s[...] = running
    runt_s[...] = running.T
    stept_s[...] = step.T

    def conv(i, _):
        ds = chunk_ds(i)
        x = proj_ref[:, chunk_ds(i + DI // LANES)]
        total = cw_ref[KCONV : KCONV + 1, ds] + cw_ref[KCONV - 1 : KCONV, ds] * x
        for j in range(1, KCONV):
            moved = pltpu.roll(x, j, 0) * shift_ref[:, j - 1 : j]
            total = total + cw_ref[KCONV - 1 - j : KCONV - j, ds] * moved
        pre_ref[:, ds] = total
        return 0

    lax.fori_loop(0, CONV // LANES, conv, 0)
    pre_k = pre_ref[:, DI : DI + STATE]
    pre_q = pre_ref[:, DI + STATE :]
    inter_s[...] = dot(pre_q * sigmoid(pre_q), pre_k * sigmoid(pre_k), NT)

    def pair(i, sumsq):
        ds = chunk_ds(i)
        pre = pre_ref[:, ds]
        values = pre * sigmoid(pre)
        low = values.astype(BF16)
        outs = []
        for side in range(2):
            h = 2 * i + side
            weights = decay_of(mask_s, run_s, runt_s, h) * inter_s[...] * stept_s[pl.ds(h, 1), :]
            outs.append(dot(weights, low))
        lane = lax.broadcasted_iota(jnp.int32, (length, LANES), 1)
        scanned = jnp.where(lane < HDIM, outs[0], outs[1]) + skip_ref[:, ds] * values
        scan_ref[:, ds] = scanned
        z = proj_ref[:, ds]
        gated = scanned * (z * sigmoid(z))
        gated_s[:, ds] = gated
        return sumsq + gated * gated

    sumsq = lax.fori_loop(0, DI // LANES, pair, jnp.zeros((length, LANES), F32))
    scale = lax.rsqrt(jnp.sum(sumsq, axis=1, keepdims=True) / DI + EPSILON)

    def finish(i, _):
        ds = chunk_ds(i)
        low_ref[:, ds] = (gated_s[:, ds] * scale * gain_ref[:, ds]).astype(BF16)
        return 0

    lax.fori_loop(0, DI // LANES, finish, 0)


def backward_kernel(
    proj_ref, raw_ref, segc_ref, segr_ref, shift_ref, cw_ref, bias_ref, rate_ref, skip_ref, gain_ref,
    pre_ref, scan_ref, gm_ref,
    glow_ref, graw_ref, gconv_ref, gdi_ref, ghead_ref,
    mask_s, run_s, runt_s, stept_s, inter_s, dinter_s, row_s, col_s,
):
    length = proj_ref.shape[0]
    mask, shifted, step, decay, running = head_prelude(
        raw_ref, segc_ref[...], segr_ref[...], bias_ref, rate_ref
    )
    mask_s[...] = mask
    run_s[...] = running
    runt_s[...] = running.T
    stept_s[...] = step.T
    pre_k = pre_ref[:, DI : DI + STATE]
    pre_q = pre_ref[:, DI + STATE :]
    keys = (pre_k * sigmoid(pre_k)).astype(BF16)
    queries = (pre_q * sigmoid(pre_q)).astype(BF16)
    inter_s[...] = dot(queries, keys, NT)
    dinter_s[...] = jnp.zeros_like(dinter_s)
    row_s[...] = jnp.zeros_like(row_s)
    col_s[...] = jnp.zeros_like(col_s)
    gconv_ref[...] = jnp.zeros_like(gconv_ref)
    gdi_ref[...] = jnp.zeros_like(gdi_ref)
    ghead_ref[...] = jnp.zeros_like(ghead_ref)

    def sums(i, carry):
        sumsq, inner = carry
        ds = chunk_ds(i)
        z = proj_ref[:, ds]
        gated = scan_ref[:, ds] * (z * sigmoid(z))
        return sumsq + gated * gated, inner + gated * gm_ref[:, ds] * gain_ref[:, ds]

    zero = jnp.zeros((length, LANES), F32)
    sumsq, inner = lax.fori_loop(0, DI // LANES, sums, (zero, zero))
    scale = lax.rsqrt(jnp.sum(sumsq, axis=1, keepdims=True) / DI + EPSILON)
    coef = scale * scale * scale * (jnp.sum(inner, axis=1, keepdims=True) / DI)

    def conv_back(i, grad_act):
        ds = chunk_ds(i)
        wide = chunk_ds(i + DI // LANES)
        pre = pre_ref[:, ds]
        sg = sigmoid(pre)
        gpre = grad_act * (sg * (1.0 + pre * (1.0 - sg)))
        x = proj_ref[:, wide]
        total = cw_ref[KCONV - 1 : KCONV, ds] * gpre
        gconv_ref[KCONV : KCONV + 1, ds] = jnp.sum(gpre, axis=0, keepdims=True)
        gconv_ref[KCONV - 1 : KCONV, ds] = jnp.sum(gpre * x, axis=0, keepdims=True)
        for j in range(1, KCONV):
            live = gpre * shift_ref[:, j - 1 : j]
            back = pltpu.roll(live, length - j, 0)
            total = total + cw_ref[KCONV - 1 - j : KCONV - j, ds] * back
            gconv_ref[KCONV - 1 - j : KCONV - j, ds] = jnp.sum(back * x, axis=0, keepdims=True)
        glow_ref[:, wide] = total.astype(BF16)

    def pair(i, _):
        ds = chunk_ds(i)
        z = proj_ref[:, ds]
        sz = sigmoid(z)
        silu_z = z * sz
        scanned = scan_ref[:, ds]
        gated = scanned * silu_z
        grad_out = gm_ref[:, ds]
        gdi_ref[0:1, ds] = jnp.sum(grad_out * gated * scale, axis=0, keepdims=True)
        dgated = scale * (grad_out * gain_ref[:, ds]) - gated * coef
        dscan = dgated * silu_z
        glow_ref[:, ds] = (dgated * scanned * (sz * (1.0 + z * (1.0 - sz)))).astype(BF16)
        pre = pre_ref[:, ds]
        values = pre * sigmoid(pre)
        gdi_ref[1:2, ds] = jnp.sum(dscan * values, axis=0, keepdims=True)
        low = values.astype(BF16)
        dlow = dscan.astype(BF16)
        lane = lax.broadcasted_iota(jnp.int32, (length, LANES), 1)
        head_lane = lax.broadcasted_iota(jnp.int32, (length, LANES), 1)
        outs = []
        for side in range(2):
            h = 2 * i + side
            here = (lane < HDIM) if side == 0 else (lane >= HDIM)
            factor = decay_of(mask_s, run_s, runt_s, h)
            stept = stept_s[pl.ds(h, 1), :]
            inter = inter_s[...]
            scaled = factor * stept
            outs.append(dot(scaled * inter, dlow, TN))
            dweights = dot(jnp.where(here, dscan, 0.0), low, NT)
            dinter_s[...] += dweights * scaled
            pairs = dweights * factor * inter
            col_s[pl.ds(h, 1), :] = jnp.sum(pairs, axis=0, keepdims=True)
            row = jnp.sum(pairs * stept, axis=1, keepdims=True)
            row_s[...] += jnp.where(head_lane == h, row, 0.0)
        grad_values = jnp.where(lane < HDIM, outs[0], outs[1]) + skip_ref[:, ds] * dscan
        conv_back(i, grad_values)
        return 0

    lax.fori_loop(0, DI // LANES, pair, 0)
    dinter = dinter_s[...].astype(BF16)
    conv_back(DI // LANES, dot(dinter, queries, TN))
    conv_back(DI // LANES + 1, dot(dinter, keys))
    dstep = col_s[...].T
    drun = row_s[...] - dstep * step
    ddecay = lax.dot_general(
        mask_s[...], drun, TN, precision=HIGHEST, preferred_element_type=F32
    )
    dstep = dstep - ddecay * rate_ref[...]
    graw = dstep * sigmoid(shifted)
    graw_ref[...] = graw.astype(BF16)
    ghead_ref[0:1, :] = jnp.sum(graw, axis=0, keepdims=True)
    ghead_ref[1:2, :] = jnp.sum(ddecay * decay, axis=0, keepdims=True)


def forward_mixer(proj, raw, small):
    length = proj.shape[0]
    vec = pltpu.VMEM
    return pl.pallas_call(
        forward_kernel,
        out_shape=(
            jax.ShapeDtypeStruct((length, CONV), F32),
            jax.ShapeDtypeStruct((length, DI), F32),
            jax.ShapeDtypeStruct((length, DI), BF16),
        ),
        in_specs=[pl.BlockSpec(memory_space=vec)] * 10,
        out_specs=[pl.BlockSpec(memory_space=vec)] * 3,
        scratch_shapes=[
            pltpu.VMEM((length, length), F32),
            pltpu.VMEM((length, LANES), F32),
            pltpu.VMEM((LANES, length), F32),
            pltpu.VMEM((LANES, length), F32),
            pltpu.VMEM((length, length), F32),
            pltpu.VMEM((length, DI), F32),
        ],
        compiler_params=pltpu.CompilerParams(vmem_limit_bytes=40 * 2**20),
        cost_estimate=pl.CostEstimate(
            flops=HEADS * length * length * 280, bytes_accessed=length * 30000, transcendentals=0
        ),
        name="mixer_forward",
    )(proj, raw, *small)


def backward_mixer(proj, raw, small, pre, scanned, grad_mixer):
    length, width = proj.shape[0], DI + CONV
    vec = pltpu.VMEM
    return pl.pallas_call(
        backward_kernel,
        out_shape=(
            jax.ShapeDtypeStruct((length, width), BF16),
            jax.ShapeDtypeStruct((length, LANES), BF16),
            jax.ShapeDtypeStruct((8, CONV), F32),
            jax.ShapeDtypeStruct((8, DI), F32),
            jax.ShapeDtypeStruct((8, LANES), F32),
        ),
        in_specs=[pl.BlockSpec(memory_space=vec)] * 13,
        out_specs=[pl.BlockSpec(memory_space=vec)] * 5,
        scratch_shapes=[
            pltpu.VMEM((length, length), F32),
            pltpu.VMEM((length, LANES), F32),
            pltpu.VMEM((LANES, length), F32),
            pltpu.VMEM((LANES, length), F32),
            pltpu.VMEM((length, length), F32),
            pltpu.VMEM((length, length), F32),
            pltpu.VMEM((length, LANES), F32),
            pltpu.VMEM((LANES, length), F32),
        ],
        compiler_params=pltpu.CompilerParams(vmem_limit_bytes=40 * 2**20),
        cost_estimate=pl.CostEstimate(
            flops=HEADS * length * length * 800, bytes_accessed=length * 60000, transcendentals=0
        ),
        name="mixer_backward",
    )(proj, raw, *small, pre, scanned, grad_mixer)


def place(n):
    me = lax.axis_index("fsdp")
    core, chip = lax.rem(me, 2), lax.div(me, 2)
    plane, line = split(n)
    return me, core, lax.rem(chip, plane), lax.div(chip, plane)


def split(n):
    half = n // 2
    plane = 4 if half % 4 == 0 else 1
    return plane, half // plane


def loop(count, step):
    def body(k, _):
        step(k)
        return 0

    lax.fori_loop(0, count, body, 0)


def greet(n, me, core, spot, rank):
    plane, line = split(n)
    barrier = pltpu.get_barrier_semaphore()

    def signal(device):
        pl.semaphore_signal(barrier, inc=1, device_id=(device,), device_id_type=MESH)

    signal(me + 1 - 2 * core)
    for j in range(plane - 1):
        signal(2 * (rank * plane + lax.rem(spot + 1 + j, plane)) + core)
    loop(line - 1, lambda r: signal(2 * (lax.rem(rank + 1 + r, line) * plane + spot) + core))
    pl.semaphore_wait(barrier, plane + line - 1)


def gather_kernel(
    n, x0, x1, x2, o0, o1, o2, own_sem, s_line, r_line, s_plane, r_plane, s_near, r_near
):
    plane, line = split(n)
    me, core, spot, rank = place(n)
    partner = me + 1 - 2 * core
    greet(n, me, core, spot, rank)
    groups = ((x0, o0), (x1, o1), (x2, o2))

    def send(g, src, slot, sems, index, device):
        return pltpu.make_async_remote_copy(
            src_ref=src,
            dst_ref=groups[g][1].at[slot],
            send_sem=sems[0].at[g, index],
            recv_sem=sems[1].at[g, index],
            device_id=(device,),
            device_id_type=MESH,
        )

    def origin(r, j):
        from_rank = lax.rem(rank + 2 * line - 1 - r, line)
        return 2 * (from_rank * plane + lax.rem(spot + 2 * plane - 1 - j, plane))

    def along(g, r, slot):
        device = 2 * (lax.rem(rank + 1 + r, line) * plane + spot) + core
        return send(g, groups[g][0], slot, (s_line, r_line), r, device)

    def across(g, r, j, src, slot):
        device = 2 * (rank * plane + lax.rem(spot + 1 + j, plane)) + core
        return send(g, src, slot, (s_plane, r_plane), plane * r + j, device)

    def near(g, r, j, src, slot):
        return send(g, src, slot, (s_near, r_near), plane * r + j, partner)

    def start_along(r):
        for g in range(3):
            along(g, r, me).start()

    loop(line - 1, start_along)
    for g in range(3):
        x = groups[g][0]
        for j in range(plane - 1):
            across(g, line - 1, j, x, me).start()
        near(g, line - 1, plane - 1, x, me).start()
        pltpu.make_async_copy(x, groups[g][1].at[me], own_sem.at[g]).start()

    def forward(r):
        for j in range(plane - 1):
            slot = origin(r, j) + core
            for g in range(3):
                block = groups[g][1].at[slot]
                across(g, r, j, block, slot).wait_recv()
                near(g, r, j, block, slot).start()

    def spread(r):
        slot = origin(r, plane - 1) + core
        for g in range(3):
            block = groups[g][1].at[slot]
            along(g, r, slot).wait_recv()
            for j in range(plane - 1):
                across(g, r, j, block, slot).start()
            near(g, r, plane - 1, block, slot).start()
        forward(lax.rem(r + line - 1, line))

    loop(line - 1, spread)
    forward((line - 2) % line)

    def drain(r):
        for j in range(plane):
            slot, other = origin(r, j) + core, origin(r, j) + 1 - core
            for g in range(3):
                block = groups[g][1].at[slot]
                near(g, r, j, block, other).wait_recv()
                near(g, r, j, block, slot).wait_send()
                if j < plane - 1:
                    across(g, r, j, block, slot).wait_send()

    loop(line, drain)

    def drain_along(r):
        for g in range(3):
            along(g, r, me).wait_send()

    loop(line - 1, drain_along)
    for g in range(3):
        pltpu.make_async_copy(groups[g][0], groups[g][1].at[me], own_sem.at[g]).wait()


def reduce_kernel(
    n, a0, a1, a2, o0, o1, o2, p0, p1, p2, t0, t1, t2, q0, q1, q2,
    u0, u1, u2, v0, v1, v2, w0, w1, w2,
    s_near, r_near, s_plane, r_plane, s_line, r_line,
):
    plane, line = split(n)
    me, core, spot, rank = place(n)
    partner = me + 1 - 2 * core
    greet(n, me, core, spot, rank)
    groups = (
        (a0, o0, p0, t0, q0, u0, v0, w0),
        (a1, o1, p1, t1, q1, u1, v1, w1),
        (a2, o2, p2, t2, q2, u2, v2, w2),
    )

    def send(src, dst, sems, g, index, device):
        return pltpu.make_async_remote_copy(
            src_ref=src.at[index] if not isinstance(src, tuple) else src[0].at[src[1]],
            dst_ref=dst.at[index],
            send_sem=sems[0].at[g, index],
            recv_sem=sems[1].at[g, index],
            device_id=(device,),
            device_id_type=MESH,
        )

    def owner(r, j):
        return 2 * (lax.rem(rank + 1 + r, line) * plane + lax.rem(spot + 1 + j, plane))

    def near(g, r, j):
        src = (groups[g][0], owner(r, j) + 1 - core)
        return send(src, groups[g][2], (s_near, r_near), g, plane * r + j, partner)

    def across(g, r, j):
        device = 2 * (rank * plane + lax.rem(spot + 1 + j, plane)) + core
        return send(groups[g][3], groups[g][4], (s_plane, r_plane), g, plane * r + j, device)

    def along(g, r):
        device = 2 * (lax.rem(rank + 1 + r, line) * plane + spot) + core
        return send(groups[g][6], groups[g][7], (s_line, r_line), g, r, device)

    def both(g, r, j):
        near(g, r, j).wait_recv()
        return groups[g][0][owner(r, j) + core].astype(F32) + groups[g][2][plane * r + j].astype(F32)

    def start_near(r):
        for j in range(plane):
            for g in range(3):
                near(g, r, j).start()

    loop(line, start_near)

    def pairs(r):
        for j in range(plane):
            for g in range(3):
                if j < plane - 1:
                    sums = groups[g][3]
                    sums[plane * r + j] = both(g, r, j).astype(sums.dtype)
                else:
                    groups[g][5][r] = both(g, r, j)
            if j > 0:
                for g in range(3):
                    across(g, r, j - 1).start()

    def total(g, r):
        result = groups[g][5][r]
        for j in range(plane - 1):
            across(g, r, j).wait_recv()
            result = result + groups[g][4][plane * r + j].astype(F32)
        return result

    def planes(r):
        for g in range(3):
            sums = groups[g][6]
            sums[r] = total(g, r).astype(sums.dtype)
        for g in range(3):
            along(g, r).start()

    def step(r):
        pairs(r)

        @pl.when(r > 0)
        def _():
            planes(r - 1)

    loop(line, step)
    for g in range(3):
        groups[g][1][...] = total(g, line - 1)

    def collect(r):
        for g in range(3):
            along(g, r).wait_recv()
            groups[g][1][...] += groups[g][7][r].astype(F32)

    loop(line - 1, collect)

    def drain(r):
        for g in range(3):
            for j in range(plane):
                near(g, r, j).wait_send()
                if j < plane - 1:
                    across(g, r, j).wait_send()

    loop(line, drain)

    def drain_along(r):
        for g in range(3):
            along(g, r).wait_send()

    loop(line - 1, drain_along)


def gather_all(n, shards):
    vmem = pl.BlockSpec(memory_space=pltpu.VMEM)
    half, (_, line) = n // 2, split(n)
    return pl.pallas_call(
        functools.partial(gather_kernel, n),
        out_shape=tuple(jax.ShapeDtypeStruct((n,) + x.shape, x.dtype) for x in shards),
        in_specs=[vmem] * 3,
        out_specs=[vmem] * 3,
        scratch_shapes=[
            pltpu.SemaphoreType.DMA((3,)),
            pltpu.SemaphoreType.DMA((3, line)),
            pltpu.SemaphoreType.DMA((3, line)),
            pltpu.SemaphoreType.DMA((3, half)),
            pltpu.SemaphoreType.DMA((3, half)),
            pltpu.SemaphoreType.DMA((3, half)),
            pltpu.SemaphoreType.DMA((3, half)),
        ],
        compiler_params=pltpu.CompilerParams(
            collective_id=0, has_side_effects=True, vmem_limit_bytes=60 * 2**20
        ),
        name="gather_all",
    )(*shards)


def reduce_all(n, terms):
    vmem = pl.BlockSpec(memory_space=pltpu.VMEM)
    half, (_, line) = n // 2, split(n)
    slots = [pltpu.VMEM((half,) + x.shape[1:], x.dtype) for x in terms]
    partial_sums = [pltpu.VMEM((line,) + x.shape[1:], F32) for x in terms]
    lines = [pltpu.VMEM((line,) + x.shape[1:], x.dtype) for x in terms]
    return pl.pallas_call(
        functools.partial(reduce_kernel, n),
        out_shape=tuple(jax.ShapeDtypeStruct(x.shape[1:], F32) for x in terms),
        in_specs=[vmem] * 3,
        out_specs=[vmem] * 3,
        scratch_shapes=slots * 3
        + partial_sums
        + lines * 2
        + [pltpu.SemaphoreType.DMA((3, half))] * 4
        + [pltpu.SemaphoreType.DMA((3, line))] * 2,
        compiler_params=pltpu.CompilerParams(
            collective_id=1, has_side_effects=True, vmem_limit_bytes=60 * 2**20
        ),
        name="reduce_all",
    )(*terms)


def per_device(
    block_in,
    segment_ids,
    live_count,
    norm_gain,
    in_weight,
    conv_weight,
    conv_bias,
    step_bias,
    decay_log,
    skip_gain,
    gated_gain,
    out_weight,
    out_cotangent,
):
    devices = lax.axis_size("fsdp")
    length = block_in.shape[0]
    share, proj_width = in_weight.shape
    width = block_in.shape[1]
    smalls = jnp.concatenate(
        [norm_gain, conv_weight.T.reshape(-1), conv_bias, gated_gain]
    )
    small_rows = -(-smalls.shape[0] // (8 * LANES)) * 8
    smalls = jnp.pad(smalls, (0, small_rows * LANES - smalls.shape[0])).reshape(small_rows, LANES)
    in_blocks, out_blocks, rest = gather_all(devices, (in_weight, out_weight, smalls))
    in_full = in_blocks.reshape(devices * share, proj_width)
    out_full = out_blocks.reshape(devices * out_weight.shape[0], width)
    rest = rest.reshape(devices, -1).astype(F32)
    a = norm_gain.shape[0]
    b = a + conv_weight.size
    c = b + conv_bias.shape[0]
    d = c + gated_gain.shape[0]
    gain_norm = rest[:, :a].reshape(-1)
    kernel_rows = jnp.moveaxis(rest[:, a:b].reshape(devices, KCONV, -1), 1, 0).reshape(KCONV, CONV)
    kernel_bias = rest[:, b:c].reshape(1, CONV)
    gated = rest[:, c:d].reshape(1, DI)
    conv_rows = jnp.concatenate([kernel_rows, kernel_bias, jnp.zeros((3, CONV), F32)], axis=0)

    def lanes(v):
        return jnp.pad(v, (0, LANES - v.shape[0])).reshape(1, LANES)

    slots = jnp.arange(length)
    shift = jnp.stack(
        [
            ((slots >= j) & (jnp.roll(segment_ids, j) == segment_ids)).astype(F32)
            for j in range(1, KCONV)
        ],
        axis=1,
    )
    shift = jnp.pad(shift, ((0, 0), (0, 8 - shift.shape[1])))
    small = (
        segment_ids.reshape(length, 1),
        segment_ids.reshape(1, length),
        shift,
        conv_rows,
        lanes(step_bias),
        lanes(jnp.exp(decay_log)),
        jnp.repeat(skip_gain, HDIM).reshape(1, DI),
        gated,
    )
    source = block_in.astype(F32)
    live_rows = (lax.iota(jnp.int32, length) < live_count[0]).astype(F32)
    masked = jnp.where(live_rows[:, None] > 0, out_cotangent, jnp.zeros_like(out_cotangent))
    normed = rms_scale(source, gain_norm).astype(BF16)
    main = DI + CONV
    projected = jnp.dot(normed, in_full[:, :main], preferred_element_type=F32)
    tail = jnp.pad(in_full[:, main:], ((0, 0), (0, LANES - HEADS)))
    raw = jnp.dot(normed, tail, preferred_element_type=F32)
    grad_mixer = lax.dot_general(masked, out_full, NT, preferred_element_type=F32)
    pre, scanned, mixer_low = forward_mixer(projected, raw, small)
    grad_out_w = lax.dot_general(mixer_low, masked, TN, preferred_element_type=F32)
    branch = jnp.dot(mixer_low, out_full, preferred_element_type=F32)
    output = (source + live_rows[:, None] * branch).astype(BF16)
    glow, graw, gconv, gdi, ghead = backward_mixer(projected, raw, small, pre, scanned, grad_mixer)
    grad_low = jnp.concatenate([glow, graw], axis=1)
    grad_in_w = lax.dot_general(normed, grad_low, TN, preferred_element_type=F32)
    grad_normed = lax.dot_general(glow, in_full[:, :main], NT, preferred_element_type=F32)
    grad_normed = grad_normed + lax.dot_general(graw, tail, NT, preferred_element_type=F32)
    _, norm_vjp = jax.vjp(rms_scale, source, gain_norm)
    grad_source, grad_gain = norm_vjp(grad_normed)
    grad_input = out_cotangent.astype(F32) + grad_source
    skip_part = gdi[1].reshape(HEADS, HDIM).sum(axis=1)
    heads = jnp.concatenate([ghead[0, :HEADS], ghead[1, :HEADS], skip_part])
    rows = jnp.concatenate(
        [
            grad_gain.reshape(devices, -1),
            jnp.moveaxis(gconv[:KCONV].reshape(KCONV, devices, -1), 0, 1).reshape(devices, -1),
            gconv[KCONV].reshape(devices, -1),
            gdi[0].reshape(devices, -1),
            jnp.broadcast_to(heads, (devices, heads.shape[0])),
        ],
        axis=1,
    )
    sum_rows = -(-rows.shape[1] // (8 * LANES)) * 8
    rows = jnp.pad(rows, ((0, 0), (0, sum_rows * LANES - rows.shape[1])))
    in_share, out_share, mine = reduce_all(
        devices,
        (
            grad_in_w.astype(BF16).reshape(devices, share, -1),
            grad_out_w.astype(BF16).reshape(devices, -1, width),
            rows.reshape(devices, sum_rows, LANES),
        ),
    )
    in_share = in_share[:, :proj_width]
    mine = mine.reshape(-1)
    head_sums = mine[d : d + 3 * HEADS].reshape(3, HEADS)
    return (
        output,
        grad_input,
        mine[:a],
        in_share,
        mine[a:b].reshape(KCONV, -1).T,
        mine[b:c],
        head_sums[0],
        head_sums[1],
        head_sums[2],
        mine[c:d],
        out_share,
    )


SECTIONS = 16


def lower(index, length):
    return pl.ds(pl.multiple_of(index * length, length), length)


def row_of(values):
    return jnp.pad(values.astype(F32), (0, LANES - values.shape[0]))[None]


class Spot:
    def __init__(self, n):
        self.plane, self.line = split(n)
        self.me, self.core, self.spot, self.rank = place(n)
        self.partner = self.me + 1 - 2 * self.core
        bit0, bit1 = lax.rem(self.spot, 2), lax.div(self.spot, 2)
        self.x = self.spot + 1 - 2 * bit0
        self.y = self.spot + 2 - 4 * bit1
        self.d = 3 - self.spot

    def device(self, rank, spot):
        return 2 * (rank * self.plane + spot) + self.core

    def greet(self):
        barrier = pltpu.get_barrier_semaphore()

        def signal(device):
            pl.semaphore_signal(barrier, inc=1, device_id=(device,), device_id_type=MESH)

        signal(self.partner)
        signal(self.device(self.rank, self.x))
        signal(self.device(self.rank, self.y))
        for k in range(1, self.line):
            signal(self.device(lax.rem(self.rank + k, self.line), self.spot))
        pl.semaphore_wait(barrier, self.line + 2)


def remote(src, dst, send_sem, recv_sem, device):
    return pltpu.make_async_remote_copy(
        src_ref=src, dst_ref=dst, send_sem=send_sem, recv_sem=recv_sem,
        device_id=(device,), device_id_type=MESH,
    )


class Gather:
    def __init__(self, at, buf, rows, g, s_line, r_line, s_plane, r_plane, s_near, r_near):
        self.at, self.buf, self.rows, self.g = at, buf, rows, g
        self.sems = (s_line, r_line, s_plane, r_plane, s_near, r_near)

    def block(self, half, rank, spot):
        return self.buf.at[half, lower(rank * self.at.plane + spot, self.rows)]

    def move(self, half, rank, spot, send, recv, device):
        ref = self.block(half, rank, spot)
        return remote(ref, ref, send, recv, device)

    def step(self, rank, way):
        at, g = self.at, self.g
        s_line, r_line = self.sems[:2]
        device = at.device(at.rank + way, at.spot)
        side = 0 if way > 0 else 1
        return self.move(at.core, rank, at.spot, s_line.at[g, side, rank], r_line.at[g, rank], device)

    def across(self, rank, kind):
        at, g = self.at, self.g
        s_plane, r_plane = self.sems[2:4]
        spot, to = (
            (at.spot, at.x), (at.spot, at.y), (at.x, at.y), (at.y, at.x)
        )[kind]
        slot = min(kind, 2)
        return self.move(
            at.core, rank, spot, s_plane.at[g, slot, rank], r_plane.at[g, slot, rank],
            at.device(at.rank, to),
        )

    def arrived(self, rank, kind):
        at, g = self.at, self.g
        s_plane, r_plane = self.sems[2:4]
        spot = (at.x, at.y, at.d)[kind]
        self.move(
            at.core, rank, spot, s_plane.at[g, kind, rank], r_plane.at[g, kind, rank],
            at.device(at.rank, at.x),
        ).wait_recv()

    def near(self, half, rank, spot):
        at, g = self.at, self.g
        s_near, r_near = self.sems[4:]
        chip = rank * at.plane + spot
        return self.move(half, rank, spot, s_near.at[g, chip], r_near.at[g, chip], at.partner)

    def spread(self, rank):
        self.across(rank, 0).start()
        self.across(rank, 1).start()
        self.near(self.at.core, rank, self.at.spot).start()

    def own(self):
        at = self.at

        @pl.when(at.rank < at.line - 1)
        def _():
            self.step(at.rank, 1).start()

        @pl.when(at.rank > 0)
        def _():
            self.step(at.rank, -1).start()

        self.spread(at.rank)

    def line_event(self, rank, below):
        at = self.at
        self.step(rank, 1).wait_recv()
        if below:
            @pl.when(at.rank < at.line - 1)
            def _():
                self.step(rank, 1).start()
        else:
            @pl.when(at.rank > 0)
            def _():
                self.step(rank, -1).start()
        self.spread(rank)

    def plane_event(self, rank, below=None):
        at = self.at
        self.arrived(rank, 0)

        @pl.when(rank < at.line // 2)
        def _():
            self.across(rank, 2).start()

        self.near(at.core, rank, at.x).start()
        self.arrived(rank, 1)

        @pl.when(rank >= at.line // 2)
        def _():
            self.across(rank, 3).start()

        self.near(at.core, rank, at.y).start()

    def diagonal_event(self, rank, below=None):
        self.arrived(rank, 2)
        self.near(self.at.core, rank, self.at.d).start()

    def away(self, k, event):
        at = self.at

        @pl.when(at.rank >= k)
        def _():
            event(at.rank - k, True)

        @pl.when(at.rank + k < at.line)
        def _():
            event(at.rank + k, False)

    def events(self):
        at, out = self.at, []
        for k in range(at.line + 2):
            if k == 0:
                out.append(self.own)
            elif k < at.line:
                out.append(functools.partial(self.away, k, self.line_event))
            if k == 1:
                out.append(functools.partial(self.plane_event, at.rank))
            elif 1 < k <= at.line:
                out.append(functools.partial(self.away, k - 1, self.plane_event))
            if k == 2:
                out.append(functools.partial(self.diagonal_event, at.rank))
            elif k > 2:
                out.append(functools.partial(self.away, k - 2, self.diagonal_event))
        return out

    def finish(self):
        at = self.at

        def chip(i):
            rank, spot = lax.div(i, at.plane), lax.rem(i, at.plane)
            self.near(1 - at.core, rank, spot).wait_recv()

        loop(at.line * at.plane, chip)

    def drain(self):
        at = self.at

        def chip(i):
            rank, spot = lax.div(i, at.plane), lax.rem(i, at.plane)
            self.near(at.core, rank, spot).wait_send()

        loop(at.line * at.plane, chip)

        def ranks(rank):
            for kind in range(3):
                self.across(rank, kind).wait_send()

            @pl.when((at.rank < at.line - 1) & (rank <= at.rank))
            def _():
                self.step(rank, 1).wait_send()

            @pl.when((at.rank > 0) & (rank >= at.rank))
            def _():
                self.step(rank, -1).wait_send()

        loop(at.line, ranks)


class Reduce:
    def __init__(self, at, index, refs, send, recv):
        self.at, self.index = at, index
        self.part, self.near_in, self.x1, self.y1, self.x2, self.y2 = refs[:6]
        self.out, self.line_in, self.total, self.last_in = refs[6:]
        self.send, self.recv = send, recv

    def copy(self, k, src, dst, device):
        return remote(src, dst, self.send.at[self.index, k], self.recv.at[self.index, k], device)

    def near(self):
        at = self.at
        return self.copy(0, self.part.at[1 - at.core], self.near_in, at.partner)

    def first(self, side):
        at, half = self.at, self.at.line // 2
        src = self.part.at[at.core, pl.ds(side * half, half), at.d]
        to = at.device(at.rank, (at.x, at.y)[side])
        return self.copy(1 + side, src, (self.x1, self.y1)[side], to)

    def second(self, side):
        at = self.at
        spot = (at.x, at.y)[side]
        src = self.part.at[at.core, :, spot]
        return self.copy(3 + side, src, (self.x2, self.y2)[side], at.device(at.rank, spot))

    def along(self, k):
        at = self.at
        rank = lax.rem(at.rank + 1 + k, at.line)
        return self.copy(6 + k, self.out.at[rank], self.line_in.at[k], at.device(rank, at.spot))

    def last(self):
        at = self.at
        rows = self.last_in.shape[0]
        return self.copy(5, self.total.at[lower(1 - at.core, rows)], self.last_in, at.partner)

    def pairs(self):
        at = self.at
        self.near().wait_recv()

        def add(spot):
            mine = self.part[at.core, :, spot].astype(F32) + self.near_in[:, spot].astype(F32)
            self.part[at.core, :, spot] = mine.astype(BF16)

        add(at.d)
        self.first(0).start()
        self.first(1).start()
        add(at.x)
        add(at.y)
        add(at.spot)

    def planes(self):
        at, half = self.at, self.at.line // 2
        for side, spot in ((0, at.y), (1, at.x)):
            self.first(side).wait_recv()
            where = pl.ds(side * half, half)
            got = (self.x1, self.y1)[side][...].astype(F32)
            mine = self.part[at.core, where, spot].astype(F32) + got
            self.part[at.core, where, spot] = mine.astype(BF16)
        self.second(0).start()
        self.second(1).start()

    def lines(self):
        at = self.at
        self.second(0).wait_recv()
        self.second(1).wait_recv()
        mine = self.part[at.core, :, at.spot].astype(F32)
        mine = mine + self.x2[...].astype(F32) + self.y2[...].astype(F32)
        self.out[...] = mine.astype(BF16)
        for k in range(at.line - 1):
            self.along(k).start()
        mine = self.part[at.core, at.rank, at.spot].astype(F32)
        self.total[...] = mine + self.x2[at.rank].astype(F32) + self.y2[at.rank].astype(F32)

    def ends(self):
        at = self.at
        for k in range(at.line - 1):
            self.along(k).wait_recv()
        total = self.total[...]
        for k in range(at.line - 1):
            total = total + self.line_in[k].astype(F32)
        self.total[...] = total
        self.last().start()

    def halves(self):
        at = self.at
        self.last().wait_recv()
        rows = self.last_in.shape[0]
        mine, other = self.total[lower(at.core, rows), :], self.last_in[...]
        first = at.core == 0
        return jnp.where(first, mine, other), jnp.where(first, other, mine)

    def drain(self):
        self.near().wait_send()
        for side in range(2):
            self.first(side).wait_send()
            self.second(side).wait_send()
        for k in range(self.at.line - 1):
            self.along(k).wait_send()
        self.last().wait_send()


def owner_mask(n, count):
    share = count // n
    rows = lax.broadcasted_iota(jnp.int32, (n, count), 0) * share
    cols = lax.broadcasted_iota(jnp.int32, (n, count), 1)
    return (cols >= rows) & (cols < rows + share)


def lane_pick(share, count):
    lane = lax.broadcasted_iota(jnp.int32, (LANES, count), 0).astype(F32)
    col = lax.broadcasted_iota(jnp.int32, (LANES, count), 1).astype(F32)
    owner = jnp.floor((col + 0.5) * (1.0 / share))
    return jnp.where(col - owner * share == lane, 1.0, 0.0)


def fused_scratch(n, length, width, share, rows, chunks):
    _, line = split(n)
    wide, half_out = CONV, width // 2
    shapes = dict(
        stage=((2, share, wide), F32), staged=((share, wide), F32), own=((2, rows, half_out), BF16),
        win=((2, n * share, wide), BF16), wout=((2, n * rows, half_out), BF16),
        mask=((length, length), F32), neg=((length, length), F32),
        shift=((KCONV - 1, length, LANES), F32), unit=((length, width), F32),
        inv=((length, LANES), F32), masked=((length, width), BF16),
        normed=((length, width), BF16), normt=((width, length), BF16),
        enorm=((LANES, width), BF16), econv=((LANES, CONV), BF16), egate=((LANES, DI), BF16),
        eskip=((LANES, DI), F32), psel=((SECTIONS * n, n * share), BF16),
        cw=((8, CONV), F32), gate=((8, DI), F32), skip=((8, DI), F32), gain=((8, width), F32),
        proj=((length, 2 * wide), F32), pre=((length, CONV), F32), scan=((length, DI), F32),
        gated=((length, DI), F32), low=((length, DI), BF16), gm=((length, DI), F32),
        glow=((length, 2 * wide), BF16),
        run=((length, LANES), F32), runt=((LANES, length), F32), stept=((LANES, length), F32),
        inter=((length, length), F32), dinter=((length, length), F32),
        row=((length, LANES), F32), col=((LANES, length), F32),
        gconv=((8, CONV), F32), gdi=((8, DI), F32),
    )
    names = list(shapes)
    specs = [pltpu.VMEM(*v) for v in shapes.values()]
    for tall, w in chunks:
        for dims, kind in (
            ((2, line, 4, tall, w), BF16), ((line, 4, tall, w), BF16),
            ((line // 2, tall, w), BF16), ((line // 2, tall, w), BF16),
            ((line, tall, w), BF16), ((line, tall, w), BF16),
            ((line, tall, w), BF16), ((line - 1, tall, w), BF16),
            ((tall, w), F32), ((tall // 2, w), F32),
        ):
            specs.append(pltpu.VMEM(dims, kind))
    sems = [
        (2, 2, line), (2, line), (2, 3, line), (2, 3, line), (2, 4 * line), (2, 4 * line),
        (2,), (2,), (len(chunks), 5 + line), (len(chunks), 5 + line),
    ]
    return names, specs + [pltpu.SemaphoreType.DMA(s) for s in sems]


def fused_kernel(n, names, chunks, x_ref, ct_ref, inw_ref, outw_ref, small_ref,
                 out_ref, gx_ref, gi_ref, go_ref, gs_ref, *scratch):
    at = Spot(n)
    core = at.core
    v = dict(zip(names, scratch))
    rest = scratch[len(names):]
    items_refs = [rest[10 * i : 10 * i + 10] for i in range(len(chunks))]
    sems = rest[10 * len(chunks):]
    s_own, r_own, s_red, r_red = sems[6:]
    length, width = x_ref.shape
    share, proj_width = inw_ref.shape
    rows = outw_ref.shape[0]
    chip = at.rank * at.plane + at.spot
    tail = DI + CONV
    stage, win, wout = v["stage"], v["win"], v["wout"]

    stage[0, :, :DI] = inw_ref[:, :DI].astype(F32)
    stage[0, :, DI:] = inw_ref[:, 2 * DI : tail].astype(F32)
    stage[1, :, :DI] = inw_ref[:, DI : 2 * DI].astype(F32)
    stage[1, :, DI : DI + LANES] = jnp.zeros((share, LANES), F32)
    stage[1, :, DI : DI + proj_width - tail] = inw_ref[:, tail:].astype(F32)
    stage[1, :, DI + LANES :] = small_ref[:share, :]
    v["own"][0] = outw_ref[:, : width // 2]
    v["own"][1] = outw_ref[:, width // 2 :]
    at.greet()

    near_in = remote(stage.at[1 - core], v["staged"], s_own.at[0], r_own.at[0], at.partner)
    my_rows = pl.ds(pl.multiple_of((2 * chip + core) * rows, rows), rows)
    near_out = remote(
        v["own"].at[1 - core], wout.at[1 - core, my_rows], s_own.at[1], r_own.at[1], at.partner
    )
    near_in.start()
    near_out.start()
    wout[core, my_rows, :] = v["own"][core]
    near_in.wait_recv()
    mine, other = stage[core], v["staged"][...]
    first = core == 0
    pair = jnp.concatenate(
        [jnp.where(first, mine, other), jnp.where(first, other, mine)], axis=0
    )
    win[core, lower(chip, 2 * share), :] = pair.astype(BF16)
    gather_in = Gather(at, win, 2 * share, 0, *sems[:6])
    gather_out = Gather(at, wout, 2 * rows, 1, *sems[:6])
    in_events = gather_in.events()
    in_events[0]()

    segr = jnp.concatenate([small_ref[share + 4 + k : share + 5 + k, :] for k in range(length // LANES)], axis=1)
    segc = jnp.broadcast_to(segr, (LANES, length)).T
    slots = lax.broadcasted_iota(jnp.int32, (length, LANES), 0)
    for j in range(1, KCONV):
        same = (slots >= j) & (pltpu.roll(segc, j, 0) == segc)
        v["shift"][j - 1] = jnp.where(same, 1.0, 0.0)
    below = lax.broadcasted_iota(jnp.int32, (length, length), 0) >= lax.broadcasted_iota(
        jnp.int32, (length, length), 1
    )
    seg_wide = jnp.concatenate([segc] * (length // LANES), axis=1)
    linked = below & (seg_wide == segr)
    v["mask"][...] = jnp.where(linked, 1.0, 0.0)
    v["neg"][...] = jnp.where(linked, 0.0, -1e30)
    x = x_ref[...].astype(F32)
    inv = lax.rsqrt(jnp.mean(x * x, axis=-1, keepdims=True) + EPSILON)
    v["inv"][...] = jnp.broadcast_to(inv, (length, LANES))
    v["unit"][...] = x * inv
    live = slots[:, :1].astype(F32) < small_ref[share + 3 : share + 4, :1]
    v["masked"][...] = jnp.where(live, ct_ref[...].astype(F32), 0.0).astype(BF16)
    v["enorm"][...] = lane_pick(width // n, width).astype(BF16)
    v["econv"][...] = lane_pick(CONV // n, CONV).astype(BF16)
    v["egate"][...] = lane_pick(DI // n, DI).astype(BF16)
    head = lax.broadcasted_iota(jnp.int32, (LANES, DI), 0) * HDIM
    channel = lax.broadcasted_iota(jnp.int32, (LANES, DI), 1)
    v["eskip"][...] = jnp.where((channel >= head) & (channel < head + HDIM), 1.0, 0.0)
    place_col = lax.broadcasted_iota(jnp.int32, (n, n * share), 1)
    place_row = lax.broadcasted_iota(jnp.int32, (n, n * share), 0) * share
    for k in range(SECTIONS):
        v["psel"][k * n : (k + 1) * n, :] = jnp.where(place_col == place_row + k, 1.0, 0.0).astype(BF16)
    v["skip"][...] = jnp.dot(
        jnp.broadcast_to(small_ref[share + 2 : share + 3, :], (8, LANES)), v["eskip"][...],
        precision=HIGHEST, preferred_element_type=F32,
    )
    bias_row = small_ref[share : share + 1, :]
    rate_row = jnp.exp(small_ref[share + 1 : share + 2, :])

    for event in in_events[1:]:
        event()
    near_out.wait_recv()
    out_events = gather_out.events()
    out_events[0]()
    gather_in.finish()

    vectors = dot(v["psel"][: 8 * n, :], win[1, :, DI + LANES :])

    def spread_vector(k, pick, count):
        wide = dot(vectors[k * n : (k + 1) * n, :], pick)
        return jnp.sum(jnp.where(owner_mask(n, count), wide, 0.0), axis=0, keepdims=True)

    gain = spread_vector(0, v["enorm"][...], width)
    v["gain"][0:1, :] = gain
    exact = v["unit"][...] * gain
    v["normed"][...] = exact.astype(BF16)
    normed = v["normed"]
    v["proj"][:, :CONV] = dot(normed[...], win[0])
    v["proj"][:, CONV : 2 * CONV - LANES] = dot(normed[...], win[1, :, : DI + LANES])
    for k in range(KCONV + 1):
        v["cw"][k : k + 1, :] = spread_vector(1 + k, v["econv"][...], CONV)
    v["gate"][0:1, :] = spread_vector(KCONV + 2, v["egate"][...], DI)
    proj, pre, scan, low = v["proj"], v["pre"], v["scan"], v["low"]
    cw, gate, skip = v["cw"], v["gate"], v["skip"]
    pending = out_events[1:]

    def pump(count=1):
        for _ in range(count):
            if pending:
                pending.pop(0)()

    pump()
    shifted = proj[:, 2 * CONV - 2 * LANES : 2 * CONV - LANES] + bias_row
    step = softplus(shifted)
    decay = -step * rate_row
    running = jnp.dot(v["mask"][...], decay, precision=HIGHEST, preferred_element_type=F32)
    v["run"][...] = running
    v["runt"][...] = running.T
    v["stept"][...] = step.T
    inter, stept, run, runt, neg = v["inter"], v["stept"], v["run"], v["runt"], v["neg"]

    def conv_tile(i):
        return chunk_ds(i + CONV // LANES) if not isinstance(i, int) else slice(i * LANES, (i + 1) * LANES)

    def conv(ds, wide):
        xs = proj[:, wide]
        total = cw[KCONV : KCONV + 1, ds] + cw[KCONV - 1 : KCONV, ds] * xs
        for j in range(1, KCONV):
            moved = pltpu.roll(xs, j, 0) * v["shift"][j - 1]
            total = total + cw[KCONV - 1 - j : KCONV - j, ds] * moved
        pre[:, ds] = total
        return total

    pre_k = conv(slice(DI, DI + LANES), slice(DI, DI + LANES))
    pre_q = conv(slice(DI + LANES, CONV), slice(DI + LANES, CONV))
    keys = (pre_k * sigmoid(pre_k)).astype(BF16)
    queries = (pre_q * sigmoid(pre_q)).astype(BF16)
    inter[...] = dot(queries, keys, NT)
    lane = lax.broadcasted_iota(jnp.int32, (length, LANES), 1)

    def factor_of(h):
        spread = column(run[...], h) - runt[pl.ds(h, 1), :]
        return jnp.exp(spread + neg[...])

    def forward_pair(i, sumsq):
        ds = chunk_ds(i)
        total = conv(ds, conv_tile(i))
        values = total * sigmoid(total)
        low_values = values.astype(BF16)
        outs = []
        for side in range(2):
            h = 2 * i + side
            weights = factor_of(h) * inter[...] * stept[pl.ds(h, 1), :]
            outs.append(dot(weights, low_values))
        scanned = jnp.where(lane < HDIM, outs[0], outs[1]) + skip[0:1, ds] * values
        scan[:, ds] = scanned
        z = proj[:, ds]
        gated = scanned * (z * sigmoid(z))
        v["gated"][:, ds] = gated
        return sumsq + gated * gated

    pairs = DI // LANES
    cuts = 4
    sumsq = jnp.zeros((length, LANES), F32)
    for k in range(cuts):
        pump(3)
        sumsq = lax.fori_loop(k * pairs // cuts, (k + 1) * pairs // cuts, forward_pair, sumsq)
    pump(99)
    scale = lax.rsqrt(jnp.sum(sumsq, axis=1, keepdims=True) / DI + EPSILON)

    def finish(i, _):
        ds = chunk_ds(i)
        low[:, ds] = (v["gated"][:, ds] * scale * gate[0:1, ds]).astype(BF16)
        return 0

    lax.fori_loop(0, pairs, finish, 0)
    items = [Reduce(at, k, refs, s_red, r_red) for k, refs in enumerate(items_refs)]
    weights_item, columns = items[0], items[1:]
    for half in range(2):
        part = dot(low[...], v["masked"][:, half * (width // 2) : (half + 1) * (width // 2)], TN)
        weights_item.part[half] = part.astype(BF16).reshape(weights_item.part.shape[1:])
    weights_item.near().start()
    gather_out.finish()
    for half in range(2):
        term = dot(v["masked"][:, half * (width // 2) : (half + 1) * (width // 2)], wout[half], NT)
        v["gm"][...] = term if half == 0 else v["gm"][...] + term
    v["normt"][...] = (v["unit"][...] * v["gain"][0:1, :]).T.astype(BF16)

    dinter, row_s, col_s, gconv, gdi = v["dinter"], v["row"], v["col"], v["gconv"], v["gdi"]
    glow, gm = v["glow"], v["gm"]
    for ref in (dinter, row_s, col_s, gconv, gdi):
        ref[...] = jnp.zeros_like(ref)

    def sums(i, inner):
        ds = chunk_ds(i)
        return inner + v["gated"][:, ds] * gm[:, ds] * gate[0:1, ds]

    inner = lax.fori_loop(0, pairs, sums, jnp.zeros((length, LANES), F32))
    coef = scale * scale * scale * (jnp.sum(inner, axis=1, keepdims=True) / DI)

    def conv_back(ds, wide, grad_act):
        pre_c = pre[:, ds]
        sg = sigmoid(pre_c)
        gpre = grad_act * (sg * (1.0 + pre_c * (1.0 - sg)))
        xs = proj[:, wide]
        total = cw[KCONV - 1 : KCONV, ds] * gpre
        gconv[KCONV : KCONV + 1, ds] = jnp.sum(gpre, axis=0, keepdims=True)
        gconv[KCONV - 1 : KCONV, ds] = jnp.sum(gpre * xs, axis=0, keepdims=True)
        for j in range(1, KCONV):
            back = pltpu.roll(gpre * v["shift"][j - 1], length - j, 0)
            total = total + cw[KCONV - 1 - j : KCONV - j, ds] * back
            gconv[KCONV - 1 - j : KCONV - j, ds] = jnp.sum(back * xs, axis=0, keepdims=True)
        glow[:, wide] = total.astype(BF16)

    def backward_pair(i):
        ds = chunk_ds(i)
        z = proj[:, ds]
        sz = sigmoid(z)
        silu_z = z * sz
        scanned = scan[:, ds]
        gated = v["gated"][:, ds]
        grad_out = gm[:, ds]
        gdi[0:1, ds] = jnp.sum(grad_out * gated * scale, axis=0, keepdims=True)
        dgated = scale * (grad_out * gate[0:1, ds]) - gated * coef
        dscan = dgated * silu_z
        glow[:, ds] = (dgated * scanned * (sz * (1.0 + z * (1.0 - sz)))).astype(BF16)
        pre_c = pre[:, ds]
        values = pre_c * sigmoid(pre_c)
        gdi[1:2, ds] = jnp.sum(dscan * values, axis=0, keepdims=True)
        low_values = values.astype(BF16)
        dlow = dscan.astype(BF16)
        outs = []
        for side in range(2):
            h = 2 * i + side
            here = (lane < HDIM) if side == 0 else (lane >= HDIM)
            factor = factor_of(h)
            step_row = stept[pl.ds(h, 1), :]
            scaled = factor * step_row
            outs.append(dot(scaled * inter[...], dlow, TN))
            dweights = dot(jnp.where(here, dscan, 0.0), low_values, NT)
            dinter[...] += dweights * scaled
            products = dweights * factor * inter[...]
            col_s[pl.ds(h, 1), :] = jnp.sum(products, axis=0, keepdims=True)
            row = jnp.sum(products * step_row, axis=1, keepdims=True)
            row_s[...] += jnp.where(lane == h, row, 0.0)
        grad_values = jnp.where(lane < HDIM, outs[0], outs[1]) + skip[0:1, ds] * dscan
        conv_back(ds, conv_tile(i), grad_values)

    def launch(k):
        item = columns[k]
        w = item.part.shape[-1]
        for half in range(2):
            cols = slice(half * CONV + k * w, half * CONV + (k + 1) * w)
            part = dot(v["normt"][...], glow[:, cols])
            item.part[half] = part.astype(BF16).reshape(item.part.shape[1:])
        item.near().start()

    schedule = {
        1: [weights_item.pairs],
        2: [lambda: launch(0)],
        3: [columns[0].pairs],
        4: [weights_item.planes],
        5: [columns[0].planes, lambda: launch(1)],
        6: [columns[1].pairs],
        8: [columns[1].planes, lambda: launch(2)],
        9: [columns[2].pairs, weights_item.lines],
        10: [columns[0].lines],
        11: [columns[2].planes, lambda: launch(3)],
    }

    def backward_step(i):
        backward_pair(i)
        for when, todo in schedule.items():
            @pl.when(i == when)
            def _(todo=todo):
                for event in todo:
                    event()

    loop(pairs, backward_step)
    low_dinter = dinter[...].astype(BF16)
    conv_back(slice(DI, DI + LANES), slice(DI, DI + LANES), dot(low_dinter, queries, TN))
    conv_back(slice(DI + LANES, CONV), slice(DI + LANES, CONV), dot(low_dinter, keys))
    columns[3].pairs()
    columns[1].lines()
    dstep = col_s[...].T
    drun = row_s[...] - dstep * step
    ddecay = lax.dot_general(v["mask"][...], drun, TN, precision=HIGHEST, preferred_element_type=F32)
    dstep = dstep - ddecay * rate_row
    graw = dstep * sigmoid(shifted)
    glow[:, 2 * CONV - 2 * LANES : 2 * CONV - LANES] = graw.astype(BF16)
    grad_normed = dot(glow[:, :CONV], win[0], NT)
    grad_normed = grad_normed + dot(glow[:, CONV : 2 * CONV - LANES], win[1, :, : DI + LANES], NT)
    unit = v["unit"][...]
    grad_gain = jnp.sum(grad_normed * unit, axis=0, keepdims=True)
    columns[3].planes()

    def owners(vector, pick):
        wide = jnp.where(owner_mask(n, vector.shape[1]), vector, 0.0)
        return dot(wide, pick, NT)

    skip_part = lax.dot_general(
        gdi[...], v["eskip"][...], NT, precision=HIGHEST, preferred_element_type=F32
    )
    per_head = [
        jnp.sum(graw, axis=0, keepdims=True), jnp.sum(ddecay * decay, axis=0, keepdims=True),
        skip_part[1:2, :],
    ]
    stacked = [owners(grad_gain, v["enorm"][...])]
    stacked += [owners(gconv[k : k + 1, :], v["econv"][...]) for k in range(KCONV + 1)]
    stacked += [owners(gdi[0:1, :], v["egate"][...])]
    stacked += [jnp.broadcast_to(row, (n, LANES)) for row in per_head]
    stacked += [jnp.zeros((n, LANES), F32)] * (SECTIONS - len(stacked))
    spread_rows = dot(v["psel"][...], jnp.concatenate(stacked, axis=0), TN)
    final = columns[4]
    shape = final.part.shape[1:]
    final.part[0] = dot(v["normt"][...], glow[:, DI:CONV]).astype(BF16).reshape(shape)
    raw_part = dot(v["normt"][...], glow[:, 2 * CONV - 2 * LANES : 2 * CONV - LANES])
    final.part[1] = jnp.concatenate([raw_part, spread_rows], axis=1).astype(BF16).reshape(shape)
    final.near().start()
    weights_item.ends()
    columns[2].lines()
    final.pairs()
    grad_unit = grad_normed * v["gain"][0:1, :]
    mean = jnp.mean(grad_unit * unit, axis=-1, keepdims=True)
    gx_ref[...] = ct_ref[...].astype(F32) + v["inv"][:, :1] * (grad_unit - unit * mean)
    columns[0].ends()
    final.planes()
    columns[3].lines()
    columns[1].ends()
    for half in range(2):
        cols = slice(half * (width // 2), (half + 1) * (width // 2))
        branch = dot(low[...], wout[half])
        out_ref[:, cols] = (
            x_ref[:, cols].astype(F32) + jnp.where(live, branch, 0.0)
        ).astype(BF16)
    final.lines()
    columns[2].ends()
    columns[3].ends()
    final.ends()
    go_ref[:, : width // 2], go_ref[:, width // 2 :] = weights_item.halves()
    for k in range(4):
        w = columns[k].part.shape[-1]
        gi_ref[:, k * w : (k + 1) * w], gi_ref[:, DI + k * w : DI + (k + 1) * w] = columns[k].halves()
    gi_ref[:, 2 * DI : tail], ends = final.halves()
    gi_ref[:, tail:] = ends[:, : proj_width - tail]
    gs_ref[...] = ends[:, LANES:]
    gather_in.drain()
    gather_out.drain()
    near_in.wait_send()
    near_out.wait_send()
    for item in items:
        item.drain()


def fused_device(
    block_in, segment_ids, live_count, norm_gain, in_weight, conv_weight, conv_bias, step_bias,
    decay_log, skip_gain, gated_gain, out_weight, out_cotangent,
):
    n = lax.axis_size("fsdp")
    length, width = block_in.shape
    share, proj_width = in_weight.shape
    rows = out_weight.shape[0]
    vectors = [norm_gain] + [conv_weight[:, j] for j in range(KCONV)] + [conv_bias, gated_gain]
    live_row = jnp.broadcast_to(live_count.astype(F32)[:, None], (1, LANES))
    segments = segment_ids.astype(F32).reshape(length // LANES, LANES)
    small = jnp.concatenate(
        [row_of(vec) for vec in vectors]
        + [jnp.zeros((share - len(vectors), LANES), F32)]
        + [row_of(step_bias), row_of(decay_log), row_of(skip_gain), live_row, segments],
        axis=0,
    )
    small = jnp.pad(small, ((0, -small.shape[0] % 8), (0, 0)))
    chunks = [(2 * rows, width // 2)] + [(2 * share, DI // 4)] * 4 + [(2 * share, 2 * LANES)]
    names, scratch = fused_scratch(n, length, width, share, rows, chunks)
    vmem = pl.BlockSpec(memory_space=pltpu.VMEM)
    output, grad_input, in_share, out_share, mine = pl.pallas_call(
        functools.partial(fused_kernel, n, names, chunks),
        out_shape=(
            jax.ShapeDtypeStruct((length, width), BF16),
            jax.ShapeDtypeStruct((length, width), F32),
            jax.ShapeDtypeStruct((share, proj_width), F32),
            jax.ShapeDtypeStruct((rows, width), F32),
            jax.ShapeDtypeStruct((share, LANES), F32),
        ),
        in_specs=[vmem] * 5,
        out_specs=[vmem] * 5,
        scratch_shapes=scratch,
        compiler_params=pltpu.CompilerParams(
            collective_id=2, has_side_effects=True, vmem_limit_bytes=60 * 2**20
        ),
        name="layer",
    )(block_in, out_cotangent, in_weight, out_weight, small)
    taps = conv_weight.shape[0]
    return (
        output,
        grad_input,
        mine[0, : norm_gain.shape[0]],
        in_share,
        mine[1 : 1 + KCONV, :taps].T,
        mine[1 + KCONV, :taps],
        mine[KCONV + 3, :HEADS],
        mine[KCONV + 4, :HEADS],
        mine[KCONV + 5, :HEADS],
        mine[KCONV + 2, : gated_gain.shape[0]],
        out_share,
    )


def fits(block_in, in_weight, out_weight, n):
    plane, line = split(n)
    share, rows = in_weight.shape[0], out_weight.shape[0]
    return (
        plane == 4 and line % 2 == 0 and share % 8 == 0 and rows % 16 == 0
        and block_in.shape[0] % LANES == 0 and share >= SECTIONS
    )


def either(*args):
    n = lax.axis_size("fsdp")
    chosen = fused_device if fits(args[0], args[4], args[11], n) else per_device
    return chosen(*args)


def solution(mesh):
    rows, vec, whole = P("fsdp", None), P("fsdp"), P()
    in_specs = (rows, vec, vec, vec, rows, rows, vec, whole, whole, whole, vec, rows, rows)
    out_specs = (rows, rows, vec, rows, rows, vec, whole, whole, whole, vec, rows)
    return jax.shard_map(
        either, mesh=mesh, in_specs=in_specs, out_specs=out_specs, check_vma=False
    )
```

```python
import functools

import jax
import jax.numpy as jnp
from jax import lax
from jax.experimental import pallas as pl
from jax.experimental.pallas import tpu as pltpu
from jax.sharding import PartitionSpec as P

DI = 1536
STATE = 128
HDIM = 64
KCONV = 4
HEADS = 24
CONV = 1792
LANES = 128
EPSILON = 1e-05
HIGHEST = lax.Precision.HIGHEST
F32 = jnp.float32
BF16 = jnp.bfloat16
NT = (((1,), (1,)), ((), ()))
TN = (((0,), (0,)), ((), ()))
MESH = pl.DeviceIdType.MESH


def rms_scale(values, gain_vec):
    return (
        values * lax.rsqrt(jnp.mean(values * values, axis=-1, keepdims=True) + EPSILON) * gain_vec
    )


def dot(a, b, dims=(((1,), (0,)), ((), ()))):
    return lax.dot_general(a.astype(BF16), b.astype(BF16), dims, preferred_element_type=F32)


def sigmoid(v):
    return 1.0 / (1.0 + jnp.exp(-v))


def softplus(v):
    return jnp.maximum(v, 0.0) + jnp.log1p(jnp.exp(-jnp.abs(v)))


def chunk_ds(i):
    return pl.ds(pl.multiple_of(i * LANES, LANES), LANES)


def head_prelude(raw_ref, segc, segr, bias_ref, rate_ref):
    length = raw_ref.shape[0]
    rows = lax.broadcasted_iota(jnp.int32, (length, length), 0)
    cols = lax.broadcasted_iota(jnp.int32, (length, length), 1)
    mask = ((rows >= cols) & (segc == segr)).astype(F32)
    shifted = raw_ref[...] + bias_ref[...]
    step = softplus(shifted)
    decay = -step * rate_ref[...]
    running = jnp.dot(mask, decay, precision=HIGHEST, preferred_element_type=F32)
    return mask, shifted, step, decay, running


def column(values, h):
    lane = lax.broadcasted_iota(jnp.int32, values.shape, 1)
    return jnp.sum(jnp.where(lane == h, values, 0.0), axis=1, keepdims=True)


def decay_of(mask_ref, run_ref, run_t_ref, h):
    spread = column(run_ref[...], h) - run_t_ref[pl.ds(h, 1), :]
    mask = mask_ref[...]
    return jnp.where(mask > 0, jnp.exp(jnp.where(mask > 0, spread, 0.0)), 0.0)


def forward_kernel(
    proj_ref, raw_ref, segc_ref, segr_ref, shift_ref, cw_ref, bias_ref, rate_ref, skip_ref, gain_ref,
    pre_ref, scan_ref, low_ref,
    mask_s, run_s, runt_s, stept_s, inter_s, gated_s,
):
    length = proj_ref.shape[0]
    mask, _, step, _, running = head_prelude(
        raw_ref, segc_ref[...], segr_ref[...], bias_ref, rate_ref
    )
    mask_s[...] = mask
    run_s[...] = running
    runt_s[...] = running.T
    stept_s[...] = step.T

    def conv(i, _):
        ds = chunk_ds(i)
        x = proj_ref[:, chunk_ds(i + DI // LANES)]
        total = cw_ref[KCONV : KCONV + 1, ds] + cw_ref[KCONV - 1 : KCONV, ds] * x
        for j in range(1, KCONV):
            moved = pltpu.roll(x, j, 0) * shift_ref[:, j - 1 : j]
            total = total + cw_ref[KCONV - 1 - j : KCONV - j, ds] * moved
        pre_ref[:, ds] = total
        return 0

    lax.fori_loop(0, CONV // LANES, conv, 0)
    pre_k = pre_ref[:, DI : DI + STATE]
    pre_q = pre_ref[:, DI + STATE :]
    inter_s[...] = dot(pre_q * sigmoid(pre_q), pre_k * sigmoid(pre_k), NT)

    def pair(i, sumsq):
        ds = chunk_ds(i)
        pre = pre_ref[:, ds]
        values = pre * sigmoid(pre)
        low = values.astype(BF16)
        outs = []
        for side in range(2):
            h = 2 * i + side
            weights = decay_of(mask_s, run_s, runt_s, h) * inter_s[...] * stept_s[pl.ds(h, 1), :]
            outs.append(dot(weights, low))
        lane = lax.broadcasted_iota(jnp.int32, (length, LANES), 1)
        scanned = jnp.where(lane < HDIM, outs[0], outs[1]) + skip_ref[:, ds] * values
        scan_ref[:, ds] = scanned
        z = proj_ref[:, ds]
        gated = scanned * (z * sigmoid(z))
        gated_s[:, ds] = gated
        return sumsq + gated * gated

    sumsq = lax.fori_loop(0, DI // LANES, pair, jnp.zeros((length, LANES), F32))
    scale = lax.rsqrt(jnp.sum(sumsq, axis=1, keepdims=True) / DI + EPSILON)

    def finish(i, _):
        ds = chunk_ds(i)
        low_ref[:, ds] = (gated_s[:, ds] * scale * gain_ref[:, ds]).astype(BF16)
        return 0

    lax.fori_loop(0, DI // LANES, finish, 0)


def backward_kernel(
    proj_ref, raw_ref, segc_ref, segr_ref, shift_ref, cw_ref, bias_ref, rate_ref, skip_ref, gain_ref,
    pre_ref, scan_ref, gm_ref,
    glow_ref, graw_ref, gconv_ref, gdi_ref, ghead_ref,
    mask_s, run_s, runt_s, stept_s, inter_s, dinter_s, row_s, col_s,
):
    length = proj_ref.shape[0]
    mask, shifted, step, decay, running = head_prelude(
        raw_ref, segc_ref[...], segr_ref[...], bias_ref, rate_ref
    )
    mask_s[...] = mask
    run_s[...] = running
    runt_s[...] = running.T
    stept_s[...] = step.T
    pre_k = pre_ref[:, DI : DI + STATE]
    pre_q = pre_ref[:, DI + STATE :]
    keys = (pre_k * sigmoid(pre_k)).astype(BF16)
    queries = (pre_q * sigmoid(pre_q)).astype(BF16)
    inter_s[...] = dot(queries, keys, NT)
    dinter_s[...] = jnp.zeros_like(dinter_s)
    row_s[...] = jnp.zeros_like(row_s)
    col_s[...] = jnp.zeros_like(col_s)
    gconv_ref[...] = jnp.zeros_like(gconv_ref)
    gdi_ref[...] = jnp.zeros_like(gdi_ref)
    ghead_ref[...] = jnp.zeros_like(ghead_ref)

    def sums(i, carry):
        sumsq, inner = carry
        ds = chunk_ds(i)
        z = proj_ref[:, ds]
        gated = scan_ref[:, ds] * (z * sigmoid(z))
        return sumsq + gated * gated, inner + gated * gm_ref[:, ds] * gain_ref[:, ds]

    zero = jnp.zeros((length, LANES), F32)
    sumsq, inner = lax.fori_loop(0, DI // LANES, sums, (zero, zero))
    scale = lax.rsqrt(jnp.sum(sumsq, axis=1, keepdims=True) / DI + EPSILON)
    coef = scale * scale * scale * (jnp.sum(inner, axis=1, keepdims=True) / DI)

    def conv_back(i, grad_act):
        ds = chunk_ds(i)
        wide = chunk_ds(i + DI // LANES)
        pre = pre_ref[:, ds]
        sg = sigmoid(pre)
        gpre = grad_act * (sg * (1.0 + pre * (1.0 - sg)))
        x = proj_ref[:, wide]
        total = cw_ref[KCONV - 1 : KCONV, ds] * gpre
        gconv_ref[KCONV : KCONV + 1, ds] = jnp.sum(gpre, axis=0, keepdims=True)
        gconv_ref[KCONV - 1 : KCONV, ds] = jnp.sum(gpre * x, axis=0, keepdims=True)
        for j in range(1, KCONV):
            live = gpre * shift_ref[:, j - 1 : j]
            back = pltpu.roll(live, length - j, 0)
            total = total + cw_ref[KCONV - 1 - j : KCONV - j, ds] * back
            gconv_ref[KCONV - 1 - j : KCONV - j, ds] = jnp.sum(back * x, axis=0, keepdims=True)
        glow_ref[:, wide] = total.astype(BF16)

    def pair(i, _):
        ds = chunk_ds(i)
        z = proj_ref[:, ds]
        sz = sigmoid(z)
        silu_z = z * sz
        scanned = scan_ref[:, ds]
        gated = scanned * silu_z
        grad_out = gm_ref[:, ds]
        gdi_ref[0:1, ds] = jnp.sum(grad_out * gated * scale, axis=0, keepdims=True)
        dgated = scale * (grad_out * gain_ref[:, ds]) - gated * coef
        dscan = dgated * silu_z
        glow_ref[:, ds] = (dgated * scanned * (sz * (1.0 + z * (1.0 - sz)))).astype(BF16)
        pre = pre_ref[:, ds]
        values = pre * sigmoid(pre)
        gdi_ref[1:2, ds] = jnp.sum(dscan * values, axis=0, keepdims=True)
        low = values.astype(BF16)
        dlow = dscan.astype(BF16)
        lane = lax.broadcasted_iota(jnp.int32, (length, LANES), 1)
        head_lane = lax.broadcasted_iota(jnp.int32, (length, LANES), 1)
        outs = []
        for side in range(2):
            h = 2 * i + side
            here = (lane < HDIM) if side == 0 else (lane >= HDIM)
            factor = decay_of(mask_s, run_s, runt_s, h)
            stept = stept_s[pl.ds(h, 1), :]
            inter = inter_s[...]
            scaled = factor * stept
            outs.append(dot(scaled * inter, dlow, TN))
            dweights = dot(jnp.where(here, dscan, 0.0), low, NT)
            dinter_s[...] += dweights * scaled
            pairs = dweights * factor * inter
            col_s[pl.ds(h, 1), :] = jnp.sum(pairs, axis=0, keepdims=True)
            row = jnp.sum(pairs * stept, axis=1, keepdims=True)
            row_s[...] += jnp.where(head_lane == h, row, 0.0)
        grad_values = jnp.where(lane < HDIM, outs[0], outs[1]) + skip_ref[:, ds] * dscan
        conv_back(i, grad_values)
        return 0

    lax.fori_loop(0, DI // LANES, pair, 0)
    dinter = dinter_s[...].astype(BF16)
    conv_back(DI // LANES, dot(dinter, queries, TN))
    conv_back(DI // LANES + 1, dot(dinter, keys))
    dstep = col_s[...].T
    drun = row_s[...] - dstep * step
    ddecay = lax.dot_general(
        mask_s[...], drun, TN, precision=HIGHEST, preferred_element_type=F32
    )
    dstep = dstep - ddecay * rate_ref[...]
    graw = dstep * sigmoid(shifted)
    graw_ref[...] = graw.astype(BF16)
    ghead_ref[0:1, :] = jnp.sum(graw, axis=0, keepdims=True)
    ghead_ref[1:2, :] = jnp.sum(ddecay * decay, axis=0, keepdims=True)


def forward_mixer(proj, raw, small):
    length = proj.shape[0]
    vec = pltpu.VMEM
    return pl.pallas_call(
        forward_kernel,
        out_shape=(
            jax.ShapeDtypeStruct((length, CONV), F32),
            jax.ShapeDtypeStruct((length, DI), F32),
            jax.ShapeDtypeStruct((length, DI), BF16),
        ),
        in_specs=[pl.BlockSpec(memory_space=vec)] * 10,
        out_specs=[pl.BlockSpec(memory_space=vec)] * 3,
        scratch_shapes=[
            pltpu.VMEM((length, length), F32),
            pltpu.VMEM((length, LANES), F32),
            pltpu.VMEM((LANES, length), F32),
            pltpu.VMEM((LANES, length), F32),
            pltpu.VMEM((length, length), F32),
            pltpu.VMEM((length, DI), F32),
        ],
        compiler_params=pltpu.CompilerParams(vmem_limit_bytes=40 * 2**20),
        cost_estimate=pl.CostEstimate(
            flops=HEADS * length * length * 280, bytes_accessed=length * 30000, transcendentals=0
        ),
        name="mixer_forward",
    )(proj, raw, *small)


def backward_mixer(proj, raw, small, pre, scanned, grad_mixer):
    length, width = proj.shape[0], DI + CONV
    vec = pltpu.VMEM
    return pl.pallas_call(
        backward_kernel,
        out_shape=(
            jax.ShapeDtypeStruct((length, width), BF16),
            jax.ShapeDtypeStruct((length, LANES), BF16),
            jax.ShapeDtypeStruct((8, CONV), F32),
            jax.ShapeDtypeStruct((8, DI), F32),
            jax.ShapeDtypeStruct((8, LANES), F32),
        ),
        in_specs=[pl.BlockSpec(memory_space=vec)] * 13,
        out_specs=[pl.BlockSpec(memory_space=vec)] * 5,
        scratch_shapes=[
            pltpu.VMEM((length, length), F32),
            pltpu.VMEM((length, LANES), F32),
            pltpu.VMEM((LANES, length), F32),
            pltpu.VMEM((LANES, length), F32),
            pltpu.VMEM((length, length), F32),
            pltpu.VMEM((length, length), F32),
            pltpu.VMEM((length, LANES), F32),
            pltpu.VMEM((LANES, length), F32),
        ],
        compiler_params=pltpu.CompilerParams(vmem_limit_bytes=40 * 2**20),
        cost_estimate=pl.CostEstimate(
            flops=HEADS * length * length * 800, bytes_accessed=length * 60000, transcendentals=0
        ),
        name="mixer_backward",
    )(proj, raw, *small, pre, scanned, grad_mixer)


def place(n):
    me = lax.axis_index("fsdp")
    core, chip = lax.rem(me, 2), lax.div(me, 2)
    plane, line = split(n)
    return me, core, lax.rem(chip, plane), lax.div(chip, plane)


def split(n):
    half = n // 2
    plane = 4 if half % 4 == 0 else 1
    return plane, half // plane


def loop(count, step):
    def body(k, _):
        step(k)
        return 0

    lax.fori_loop(0, count, body, 0)


def greet(n, me, core, spot, rank):
    plane, line = split(n)
    barrier = pltpu.get_barrier_semaphore()

    def signal(device):
        pl.semaphore_signal(barrier, inc=1, device_id=(device,), device_id_type=MESH)

    signal(me + 1 - 2 * core)
    for j in range(plane - 1):
        signal(2 * (rank * plane + lax.rem(spot + 1 + j, plane)) + core)
    loop(line - 1, lambda r: signal(2 * (lax.rem(rank + 1 + r, line) * plane + spot) + core))
    pl.semaphore_wait(barrier, plane + line - 1)


def gather_kernel(
    n, x0, x1, x2, o0, o1, o2, own_sem, s_line, r_line, s_plane, r_plane, s_near, r_near
):
    plane, line = split(n)
    me, core, spot, rank = place(n)
    partner = me + 1 - 2 * core
    greet(n, me, core, spot, rank)
    groups = ((x0, o0), (x1, o1), (x2, o2))

    def send(g, src, slot, sems, index, device):
        return pltpu.make_async_remote_copy(
            src_ref=src,
            dst_ref=groups[g][1].at[slot],
            send_sem=sems[0].at[g, index],
            recv_sem=sems[1].at[g, index],
            device_id=(device,),
            device_id_type=MESH,
        )

    def origin(r, j):
        from_rank = lax.rem(rank + 2 * line - 1 - r, line)
        return 2 * (from_rank * plane + lax.rem(spot + 2 * plane - 1 - j, plane))

    def along(g, r, slot):
        device = 2 * (lax.rem(rank + 1 + r, line) * plane + spot) + core
        return send(g, groups[g][0], slot, (s_line, r_line), r, device)

    def across(g, r, j, src, slot):
        device = 2 * (rank * plane + lax.rem(spot + 1 + j, plane)) + core
        return send(g, src, slot, (s_plane, r_plane), plane * r + j, device)

    def near(g, r, j, src, slot):
        return send(g, src, slot, (s_near, r_near), plane * r + j, partner)

    def start_along(r):
        for g in range(3):
            along(g, r, me).start()

    loop(line - 1, start_along)
    for g in range(3):
        x = groups[g][0]
        for j in range(plane - 1):
            across(g, line - 1, j, x, me).start()
        near(g, line - 1, plane - 1, x, me).start()
        pltpu.make_async_copy(x, groups[g][1].at[me], own_sem.at[g]).start()

    def forward(r):
        for j in range(plane - 1):
            slot = origin(r, j) + core
            for g in range(3):
                block = groups[g][1].at[slot]
                across(g, r, j, block, slot).wait_recv()
                near(g, r, j, block, slot).start()

    def spread(r):
        slot = origin(r, plane - 1) + core
        for g in range(3):
            block = groups[g][1].at[slot]
            along(g, r, slot).wait_recv()
            for j in range(plane - 1):
                across(g, r, j, block, slot).start()
            near(g, r, plane - 1, block, slot).start()
        forward(lax.rem(r + line - 1, line))

    loop(line - 1, spread)
    forward((line - 2) % line)

    def drain(r):
        for j in range(plane):
            slot, other = origin(r, j) + core, origin(r, j) + 1 - core
            for g in range(3):
                block = groups[g][1].at[slot]
                near(g, r, j, block, other).wait_recv()
                near(g, r, j, block, slot).wait_send()
                if j < plane - 1:
                    across(g, r, j, block, slot).wait_send()

    loop(line, drain)

    def drain_along(r):
        for g in range(3):
            along(g, r, me).wait_send()

    loop(line - 1, drain_along)
    for g in range(3):
        pltpu.make_async_copy(groups[g][0], groups[g][1].at[me], own_sem.at[g]).wait()


def reduce_kernel(
    n, a0, a1, a2, o0, o1, o2, p0, p1, p2, t0, t1, t2, q0, q1, q2,
    u0, u1, u2, v0, v1, v2, w0, w1, w2,
    s_near, r_near, s_plane, r_plane, s_line, r_line,
):
    plane, line = split(n)
    me, core, spot, rank = place(n)
    partner = me + 1 - 2 * core
    greet(n, me, core, spot, rank)
    groups = (
        (a0, o0, p0, t0, q0, u0, v0, w0),
        (a1, o1, p1, t1, q1, u1, v1, w1),
        (a2, o2, p2, t2, q2, u2, v2, w2),
    )

    def send(src, dst, sems, g, index, device):
        return pltpu.make_async_remote_copy(
            src_ref=src.at[index] if not isinstance(src, tuple) else src[0].at[src[1]],
            dst_ref=dst.at[index],
            send_sem=sems[0].at[g, index],
            recv_sem=sems[1].at[g, index],
            device_id=(device,),
            device_id_type=MESH,
        )

    def owner(r, j):
        return 2 * (lax.rem(rank + 1 + r, line) * plane + lax.rem(spot + 1 + j, plane))

    def near(g, r, j):
        src = (groups[g][0], owner(r, j) + 1 - core)
        return send(src, groups[g][2], (s_near, r_near), g, plane * r + j, partner)

    def across(g, r, j):
        device = 2 * (rank * plane + lax.rem(spot + 1 + j, plane)) + core
        return send(groups[g][3], groups[g][4], (s_plane, r_plane), g, plane * r + j, device)

    def along(g, r):
        device = 2 * (lax.rem(rank + 1 + r, line) * plane + spot) + core
        return send(groups[g][6], groups[g][7], (s_line, r_line), g, r, device)

    def both(g, r, j):
        near(g, r, j).wait_recv()
        return groups[g][0][owner(r, j) + core].astype(F32) + groups[g][2][plane * r + j].astype(F32)

    def start_near(r):
        for j in range(plane):
            for g in range(3):
                near(g, r, j).start()

    loop(line, start_near)

    def pairs(r):
        for j in range(plane):
            for g in range(3):
                if j < plane - 1:
                    sums = groups[g][3]
                    sums[plane * r + j] = both(g, r, j).astype(sums.dtype)
                else:
                    groups[g][5][r] = both(g, r, j)
            if j > 0:
                for g in range(3):
                    across(g, r, j - 1).start()

    def total(g, r):
        result = groups[g][5][r]
        for j in range(plane - 1):
            across(g, r, j).wait_recv()
            result = result + groups[g][4][plane * r + j].astype(F32)
        return result

    def planes(r):
        for g in range(3):
            sums = groups[g][6]
            sums[r] = total(g, r).astype(sums.dtype)
        for g in range(3):
            along(g, r).start()

    def step(r):
        pairs(r)

        @pl.when(r > 0)
        def _():
            planes(r - 1)

    loop(line, step)
    for g in range(3):
        groups[g][1][...] = total(g, line - 1)

    def collect(r):
        for g in range(3):
            along(g, r).wait_recv()
            groups[g][1][...] += groups[g][7][r].astype(F32)

    loop(line - 1, collect)

    def drain(r):
        for g in range(3):
            for j in range(plane):
                near(g, r, j).wait_send()
                if j < plane - 1:
                    across(g, r, j).wait_send()

    loop(line, drain)

    def drain_along(r):
        for g in range(3):
            along(g, r).wait_send()

    loop(line - 1, drain_along)


def gather_all(n, shards):
    vmem = pl.BlockSpec(memory_space=pltpu.VMEM)
    half, (_, line) = n // 2, split(n)
    return pl.pallas_call(
        functools.partial(gather_kernel, n),
        out_shape=tuple(jax.ShapeDtypeStruct((n,) + x.shape, x.dtype) for x in shards),
        in_specs=[vmem] * 3,
        out_specs=[vmem] * 3,
        scratch_shapes=[
            pltpu.SemaphoreType.DMA((3,)),
            pltpu.SemaphoreType.DMA((3, line)),
            pltpu.SemaphoreType.DMA((3, line)),
            pltpu.SemaphoreType.DMA((3, half)),
            pltpu.SemaphoreType.DMA((3, half)),
            pltpu.SemaphoreType.DMA((3, half)),
            pltpu.SemaphoreType.DMA((3, half)),
        ],
        compiler_params=pltpu.CompilerParams(
            collective_id=0, has_side_effects=True, vmem_limit_bytes=60 * 2**20
        ),
        name="gather_all",
    )(*shards)


def reduce_all(n, terms):
    vmem = pl.BlockSpec(memory_space=pltpu.VMEM)
    half, (_, line) = n // 2, split(n)
    slots = [pltpu.VMEM((half,) + x.shape[1:], x.dtype) for x in terms]
    partial_sums = [pltpu.VMEM((line,) + x.shape[1:], F32) for x in terms]
    lines = [pltpu.VMEM((line,) + x.shape[1:], x.dtype) for x in terms]
    return pl.pallas_call(
        functools.partial(reduce_kernel, n),
        out_shape=tuple(jax.ShapeDtypeStruct(x.shape[1:], F32) for x in terms),
        in_specs=[vmem] * 3,
        out_specs=[vmem] * 3,
        scratch_shapes=slots * 3
        + partial_sums
        + lines * 2
        + [pltpu.SemaphoreType.DMA((3, half))] * 4
        + [pltpu.SemaphoreType.DMA((3, line))] * 2,
        compiler_params=pltpu.CompilerParams(
            collective_id=1, has_side_effects=True, vmem_limit_bytes=60 * 2**20
        ),
        name="reduce_all",
    )(*terms)


def per_device(
    block_in,
    segment_ids,
    live_count,
    norm_gain,
    in_weight,
    conv_weight,
    conv_bias,
    step_bias,
    decay_log,
    skip_gain,
    gated_gain,
    out_weight,
    out_cotangent,
):
    devices = lax.axis_size("fsdp")
    length = block_in.shape[0]
    share, proj_width = in_weight.shape
    width = block_in.shape[1]
    smalls = jnp.concatenate(
        [norm_gain, conv_weight.T.reshape(-1), conv_bias, gated_gain]
    )
    small_rows = -(-smalls.shape[0] // (8 * LANES)) * 8
    smalls = jnp.pad(smalls, (0, small_rows * LANES - smalls.shape[0])).reshape(small_rows, LANES)
    in_blocks, out_blocks, rest = gather_all(devices, (in_weight, out_weight, smalls))
    in_full = in_blocks.reshape(devices * share, proj_width)
    out_full = out_blocks.reshape(devices * out_weight.shape[0], width)
    rest = rest.reshape(devices, -1).astype(F32)
    a = norm_gain.shape[0]
    b = a + conv_weight.size
    c = b + conv_bias.shape[0]
    d = c + gated_gain.shape[0]
    gain_norm = rest[:, :a].reshape(-1)
    kernel_rows = jnp.moveaxis(rest[:, a:b].reshape(devices, KCONV, -1), 1, 0).reshape(KCONV, CONV)
    kernel_bias = rest[:, b:c].reshape(1, CONV)
    gated = rest[:, c:d].reshape(1, DI)
    conv_rows = jnp.concatenate([kernel_rows, kernel_bias, jnp.zeros((3, CONV), F32)], axis=0)

    def lanes(v):
        return jnp.pad(v, (0, LANES - v.shape[0])).reshape(1, LANES)

    slots = jnp.arange(length)
    shift = jnp.stack(
        [
            ((slots >= j) & (jnp.roll(segment_ids, j) == segment_ids)).astype(F32)
            for j in range(1, KCONV)
        ],
        axis=1,
    )
    shift = jnp.pad(shift, ((0, 0), (0, 8 - shift.shape[1])))
    small = (
        segment_ids.reshape(length, 1),
        segment_ids.reshape(1, length),
        shift,
        conv_rows,
        lanes(step_bias),
        lanes(jnp.exp(decay_log)),
        jnp.repeat(skip_gain, HDIM).reshape(1, DI),
        gated,
    )
    source = block_in.astype(F32)
    live_rows = (lax.iota(jnp.int32, length) < live_count[0]).astype(F32)
    masked = jnp.where(live_rows[:, None] > 0, out_cotangent, jnp.zeros_like(out_cotangent))
    normed = rms_scale(source, gain_norm).astype(BF16)
    main = DI + CONV
    projected = jnp.dot(normed, in_full[:, :main], preferred_element_type=F32)
    tail = jnp.pad(in_full[:, main:], ((0, 0), (0, LANES - HEADS)))
    raw = jnp.dot(normed, tail, preferred_element_type=F32)
    grad_mixer = lax.dot_general(masked, out_full, NT, preferred_element_type=F32)
    pre, scanned, mixer_low = forward_mixer(projected, raw, small)
    grad_out_w = lax.dot_general(mixer_low, masked, TN, preferred_element_type=F32)
    branch = jnp.dot(mixer_low, out_full, preferred_element_type=F32)
    output = (source + live_rows[:, None] * branch).astype(BF16)
    glow, graw, gconv, gdi, ghead = backward_mixer(projected, raw, small, pre, scanned, grad_mixer)
    grad_low = jnp.concatenate([glow, graw], axis=1)
    grad_in_w = lax.dot_general(normed, grad_low, TN, preferred_element_type=F32)
    grad_normed = lax.dot_general(glow, in_full[:, :main], NT, preferred_element_type=F32)
    grad_normed = grad_normed + lax.dot_general(graw, tail, NT, preferred_element_type=F32)
    _, norm_vjp = jax.vjp(rms_scale, source, gain_norm)
    grad_source, grad_gain = norm_vjp(grad_normed)
    grad_input = out_cotangent.astype(F32) + grad_source
    skip_part = gdi[1].reshape(HEADS, HDIM).sum(axis=1)
    heads = jnp.concatenate([ghead[0, :HEADS], ghead[1, :HEADS], skip_part])
    rows = jnp.concatenate(
        [
            grad_gain.reshape(devices, -1),
            jnp.moveaxis(gconv[:KCONV].reshape(KCONV, devices, -1), 0, 1).reshape(devices, -1),
            gconv[KCONV].reshape(devices, -1),
            gdi[0].reshape(devices, -1),
            jnp.broadcast_to(heads, (devices, heads.shape[0])),
        ],
        axis=1,
    )
    sum_rows = -(-rows.shape[1] // (8 * LANES)) * 8
    rows = jnp.pad(rows, ((0, 0), (0, sum_rows * LANES - rows.shape[1])))
    in_share, out_share, mine = reduce_all(
        devices,
        (
            grad_in_w.astype(BF16).reshape(devices, share, -1),
            grad_out_w.astype(BF16).reshape(devices, -1, width),
            rows.reshape(devices, sum_rows, LANES),
        ),
    )
    in_share = in_share[:, :proj_width]
    mine = mine.reshape(-1)
    head_sums = mine[d : d + 3 * HEADS].reshape(3, HEADS)
    return (
        output,
        grad_input,
        mine[:a],
        in_share,
        mine[a:b].reshape(KCONV, -1).T,
        mine[b:c],
        head_sums[0],
        head_sums[1],
        head_sums[2],
        mine[c:d],
        out_share,
    )


SECTIONS = 16


def lower(index, length):
    return pl.ds(pl.multiple_of(index * length, length), length)


class Spot:
    def __init__(self, n):
        self.plane, self.line = split(n)
        self.me, self.core, self.spot, self.rank = place(n)
        self.partner = self.me + 1 - 2 * self.core
        bit0, bit1 = lax.rem(self.spot, 2), lax.div(self.spot, 2)
        self.x = self.spot + 1 - 2 * bit0
        self.y = self.spot + 2 - 4 * bit1
        self.d = 3 - self.spot

    def device(self, rank, spot):
        return 2 * (rank * self.plane + spot) + self.core

    def greet(self):
        barrier = pltpu.get_barrier_semaphore()

        def signal(device):
            pl.semaphore_signal(barrier, inc=1, device_id=(device,), device_id_type=MESH)

        signal(self.partner)
        signal(self.device(self.rank, self.x))
        signal(self.device(self.rank, self.y))
        for k in range(1, self.line):
            signal(self.device(lax.rem(self.rank + k, self.line), self.spot))
        pl.semaphore_wait(barrier, self.line + 2)


def remote(src, dst, send_sem, recv_sem, device):
    return pltpu.make_async_remote_copy(
        src_ref=src, dst_ref=dst, send_sem=send_sem, recv_sem=recv_sem,
        device_id=(device,), device_id_type=MESH,
    )


class Gather:
    def __init__(self, at, buf, rows, g, s_line, r_line, s_plane, r_plane, s_near, r_near):
        self.at, self.buf, self.rows, self.g = at, buf, rows, g
        self.sems = (s_line, r_line, s_plane, r_plane, s_near, r_near)

    def block(self, half, rank, spot):
        return self.buf.at[half, lower(rank * self.at.plane + spot, self.rows)]

    def move(self, half, rank, spot, send, recv, device):
        ref = self.block(half, rank, spot)
        return remote(ref, ref, send, recv, device)

    def step(self, rank, way):
        at, g = self.at, self.g
        s_line, r_line = self.sems[:2]
        device = at.device(at.rank + way, at.spot)
        side = 0 if way > 0 else 1
        return self.move(at.core, rank, at.spot, s_line.at[g, side, rank], r_line.at[g, rank], device)

    def across(self, rank, kind):
        at, g = self.at, self.g
        s_plane, r_plane = self.sems[2:4]
        spot, to = (
            (at.spot, at.x), (at.spot, at.y), (at.x, at.y), (at.y, at.x)
        )[kind]
        slot = min(kind, 2)
        return self.move(
            at.core, rank, spot, s_plane.at[g, slot, rank], r_plane.at[g, slot, rank],
            at.device(at.rank, to),
        )

    def arrived(self, rank, kind):
        at, g = self.at, self.g
        s_plane, r_plane = self.sems[2:4]
        spot = (at.x, at.y, at.d)[kind]
        self.move(
            at.core, rank, spot, s_plane.at[g, kind, rank], r_plane.at[g, kind, rank],
            at.device(at.rank, at.x),
        ).wait_recv()

    def near(self, half, rank, spot):
        at, g = self.at, self.g
        s_near, r_near = self.sems[4:]
        chip = rank * at.plane + spot
        return self.move(half, rank, spot, s_near.at[g, chip], r_near.at[g, chip], at.partner)

    def spread(self, rank):
        self.across(rank, 0).start()
        self.across(rank, 1).start()
        self.near(self.at.core, rank, self.at.spot).start()

    def own(self):
        at = self.at

        @pl.when(at.rank < at.line - 1)
        def _():
            self.step(at.rank, 1).start()

        @pl.when(at.rank > 0)
        def _():
            self.step(at.rank, -1).start()

        self.spread(at.rank)

    def line_event(self, rank, below):
        at = self.at
        self.step(rank, 1).wait_recv()
        if below:
            @pl.when(at.rank < at.line - 1)
            def _():
                self.step(rank, 1).start()
        else:
            @pl.when(at.rank > 0)
            def _():
                self.step(rank, -1).start()
        self.spread(rank)

    def plane_event(self, rank, below=None):
        at = self.at
        self.arrived(rank, 0)

        @pl.when(rank < at.line // 2)
        def _():
            self.across(rank, 2).start()

        self.near(at.core, rank, at.x).start()
        self.arrived(rank, 1)

        @pl.when(rank >= at.line // 2)
        def _():
            self.across(rank, 3).start()

        self.near(at.core, rank, at.y).start()

    def diagonal_event(self, rank, below=None):
        self.arrived(rank, 2)
        self.near(self.at.core, rank, self.at.d).start()

    def away(self, k, event):
        at = self.at

        @pl.when(at.rank >= k)
        def _():
            event(at.rank - k, True)

        @pl.when(at.rank + k < at.line)
        def _():
            event(at.rank + k, False)

    def events(self):
        at, out = self.at, []
        for k in range(at.line + 2):
            if k == 0:
                out.append(self.own)
            elif k < at.line:
                out.append(functools.partial(self.away, k, self.line_event))
            if k == 1:
                out.append(functools.partial(self.plane_event, at.rank))
            elif 1 < k <= at.line:
                out.append(functools.partial(self.away, k - 1, self.plane_event))
            if k == 2:
                out.append(functools.partial(self.diagonal_event, at.rank))
            elif k > 2:
                out.append(functools.partial(self.away, k - 2, self.diagonal_event))
        return out

    def finish(self):
        at = self.at

        def chip(i):
            rank, spot = lax.div(i, at.plane), lax.rem(i, at.plane)
            self.near(1 - at.core, rank, spot).wait_recv()

        loop(at.line * at.plane, chip)

    def drain(self):
        at = self.at

        def chip(i):
            rank, spot = lax.div(i, at.plane), lax.rem(i, at.plane)
            self.near(at.core, rank, spot).wait_send()

        loop(at.line * at.plane, chip)

        def ranks(rank):
            for kind in range(3):
                self.across(rank, kind).wait_send()

            @pl.when((at.rank < at.line - 1) & (rank <= at.rank))
            def _():
                self.step(rank, 1).wait_send()

            @pl.when((at.rank > 0) & (rank >= at.rank))
            def _():
                self.step(rank, -1).wait_send()

        loop(at.line, ranks)


class Reduce:
    def __init__(self, at, index, refs, send, recv):
        self.at, self.index = at, index
        self.part, self.near_in, self.x1, self.y1, self.x2, self.y2 = refs[:6]
        self.out, self.line_in, self.total, self.last_in = refs[6:]
        self.send, self.recv = send, recv

    def copy(self, k, src, dst, device):
        return remote(src, dst, self.send.at[self.index, k], self.recv.at[self.index, k], device)

    def near(self, k):
        at = self.at
        spot = (at.d, at.y, at.x, at.spot)[k]
        return self.copy(k, self.part.at[1 - at.core, :, spot], self.near_in.at[:, spot], at.partner)

    def start(self):
        for k in range(4):
            self.near(k).start()

    def first(self, side):
        at, half = self.at, self.at.line // 2
        src = self.part.at[at.core, pl.ds(side * half, half), at.d]
        to = at.device(at.rank, (at.x, at.y)[side])
        return self.copy(4 + side, src, (self.x1, self.y1)[side], to)

    def second(self, side):
        at = self.at
        spot = (at.x, at.y)[side]
        src = self.part.at[at.core, :, spot]
        return self.copy(6 + side, src, (self.x2, self.y2)[side], at.device(at.rank, spot))

    def along(self, k):
        at = self.at
        rank = lax.rem(at.rank + 1 + k, at.line)
        return self.copy(9 + k, self.out.at[rank], self.line_in.at[k], at.device(rank, at.spot))

    def last(self):
        at = self.at
        rows = self.last_in.shape[0]
        return self.copy(8, self.total.at[lower(1 - at.core, rows)], self.last_in, at.partner)

    def pair(self, k, ranks=slice(None)):
        at = self.at
        spot = (at.d, at.y, at.x, at.spot)[k]
        return self.part[at.core, ranks, spot].astype(F32) + self.near_in[ranks, spot].astype(F32)

    def pairs(self):
        at = self.at
        self.near(0).wait_recv()
        self.part[at.core, :, at.d] = self.pair(0).astype(BF16)
        self.first(0).start()
        self.first(1).start()

    def planes(self):
        at, half = self.at, self.at.line // 2
        for side, spot in ((0, at.y), (1, at.x)):
            self.near(1 + side).wait_recv()
            self.first(side).wait_recv()
            for part in range(2):
                ranks = slice(part * half, (part + 1) * half)
                mine = self.pair(1 + side, ranks)
                if part == side:
                    mine = mine + (self.x1, self.y1)[side][...].astype(F32)
                self.part[at.core, ranks, spot] = mine.astype(BF16)
            self.second(1 - side).start()

    def lines(self):
        at = self.at
        self.near(3).wait_recv()
        self.second(0).wait_recv()
        self.second(1).wait_recv()
        mine = self.pair(3) + self.x2[...].astype(F32) + self.y2[...].astype(F32)
        self.out[...] = mine.astype(BF16)
        for k in range(at.line - 1):
            self.along(k).start()
        mine = self.part[at.core, at.rank, at.spot].astype(F32)
        mine = mine + self.near_in[at.rank, at.spot].astype(F32)
        self.total[...] = mine + self.x2[at.rank].astype(F32) + self.y2[at.rank].astype(F32)

    def ends(self):
        at = self.at
        for k in range(at.line - 1):
            self.along(k).wait_recv()
        total = self.total[...]
        for k in range(at.line - 1):
            total = total + self.line_in[k].astype(F32)
        self.total[...] = total
        self.last().start()

    def halves(self):
        at = self.at
        self.last().wait_recv()
        rows = self.last_in.shape[0]
        mine, other = self.total[lower(at.core, rows), :], self.last_in[...]
        first = at.core == 0
        return jnp.where(first, mine, other), jnp.where(first, other, mine)

    def drain(self):
        for k in range(4):
            self.near(k).wait_send()
        for side in range(2):
            self.first(side).wait_send()
            self.second(side).wait_send()
        for k in range(self.at.line - 1):
            self.along(k).wait_send()
        self.last().wait_send()


def owner_mask(n, count):
    share = count // n
    rows = lax.broadcasted_iota(jnp.int32, (n, count), 0) * share
    cols = lax.broadcasted_iota(jnp.int32, (n, count), 1)
    return (cols >= rows) & (cols < rows + share)


def lane_pick(share, count):
    lane = lax.broadcasted_iota(jnp.int32, (LANES, count), 0).astype(F32)
    col = lax.broadcasted_iota(jnp.int32, (LANES, count), 1).astype(F32)
    owner = jnp.floor((col + 0.5) * (1.0 / share))
    return jnp.where(col - owner * share == lane, 1.0, 0.0)


def fused_scratch(n, length, width, share, rows, chunks):
    _, line = split(n)
    wide, half_out, half_z = CONV, width // 2, DI // 2
    conv_w = half_z + 2 * LANES
    shapes = dict(
        stage_c=((2, share, conv_w), F32), staged_c=((share, conv_w), F32),
        stage_z=((2, share, half_z), F32), staged_z=((share, half_z), F32),
        own=((2, rows, half_out), BF16), win_c=((2, n * share, conv_w), BF16),
        win_z=((2, n * share, half_z), BF16), wout=((2, n * rows, half_out), BF16),
        mask=((length, length), F32), neg=((length, length), F32),
        shift=((KCONV - 1, length, LANES), F32), unit=((length, width), F32),
        inv=((length, LANES), F32), masked=((length, width), BF16),
        normed=((length, width), BF16), normt=((width, length), BF16),
        enorm=((LANES, width), BF16), econv=((LANES, CONV), BF16), egate=((LANES, DI), BF16),
        eskip=((LANES, DI), F32), psel=((SECTIONS * n, n * share), BF16),
        cw=((8, CONV), F32), gate=((8, DI), F32), skip=((8, DI), F32), gain=((8, width), F32),
        proj=((length, 2 * wide), F32), pre=((length, CONV), F32), scan=((length, DI), F32),
        gated=((length, DI), F32), low=((length, DI), BF16), gm=((length, DI), F32),
        glow=((length, 2 * wide), BF16),
        run=((length, LANES), F32), runt=((LANES, length), F32), stept=((LANES, length), F32),
        inter=((length, length), F32), dinter=((length, length), F32),
        row=((length, LANES), F32), col=((LANES, length), F32),
        gconv=((8, CONV), F32), gdi=((8, DI), F32), misc=((8, LANES), F32),
    )
    names = list(shapes)
    specs = [pltpu.VMEM(*v) for v in shapes.values()]
    for tall, w in chunks:
        for dims, kind in (
            ((2, line, 4, tall, w), BF16), ((line, 4, tall, w), BF16),
            ((line // 2, tall, w), BF16), ((line // 2, tall, w), BF16),
            ((line, tall, w), BF16), ((line, tall, w), BF16),
            ((line, tall, w), BF16), ((line - 1, tall, w), BF16),
            ((tall, w), F32), ((tall // 2, w), F32),
        ):
            specs.append(pltpu.VMEM(dims, kind))
    sems = [
        (3, 2, line), (3, line), (3, 3, line), (3, 3, line), (3, 4 * line), (3, 4 * line),
        (3,), (3,), (len(chunks), 8 + line), (len(chunks), 8 + line),
    ]
    return names, specs + [pltpu.SemaphoreType.DMA(s) for s in sems]


def fused_kernel(n, names, chunks, x_ref, ct_ref, inw_ref, outw_ref,
                 norm_ref, taps_ref, cbias_ref, gated_ref, bias_ref, rate_ref, skip_ref, seg_ref, live_ref,
                 out_ref, gx_ref, gi_ref, go_ref, gs_ref, *scratch):
    at = Spot(n)
    core = at.core
    v = dict(zip(names, scratch))
    rest = scratch[len(names):]
    items_refs = [rest[10 * i : 10 * i + 10] for i in range(len(chunks))]
    sems = rest[10 * len(chunks):]
    s_own, r_own, s_red, r_red = sems[6:]
    length, width = x_ref.shape
    share, proj_width = inw_ref.shape
    rows = outw_ref.shape[0]
    chip = at.rank * at.plane + at.spot
    tail = DI + CONV
    wout, win_c, win_z, stage_c, stage_z = (
        v[k] for k in ("wout", "win_c", "win_z", "stage_c", "stage_z")
    )
    hz = DI // 2
    spare = hz + LANES

    def put(ref, row, lane, values):
        ref[..., row : row + values.shape[0], lane : lane + values.shape[1]] = values.astype(F32)

    for half in range(2):
        stage_c[half, :, :hz] = inw_ref[:, DI + half * hz : DI + (half + 1) * hz].astype(F32)
    stage_c[0, :, hz:] = inw_ref[:, 2 * DI : tail].astype(F32)
    stage_c[1, :, hz:] = jnp.zeros((share, 2 * LANES), F32)
    tile = stage_c.at[1]
    put(tile, 0, hz, inw_ref[:, tail:])
    put(tile, 0, spare, norm_ref[...][None])
    put(tile, 1, spare, taps_ref[...])
    put(tile, 1 + KCONV, spare, cbias_ref[...][None])
    put(tile, 2 + KCONV, spare, gated_ref[...][None])
    at.greet()

    def exchange(g, src, dst):
        return remote(src, dst, s_own.at[g], r_own.at[g], at.partner)

    my_rows = pl.ds(pl.multiple_of((2 * chip + core) * rows, rows), rows)
    near_c = exchange(0, stage_c.at[1 - core], v["staged_c"])
    near_z = exchange(1, stage_z.at[1 - core], v["staged_z"])
    near_out = exchange(2, v["own"].at[1 - core], wout.at[1 - core, my_rows])
    near_c.start()
    for half in range(2):
        stage_z[half] = inw_ref[:, half * hz : (half + 1) * hz].astype(F32)
        v["own"][half] = outw_ref[:, half * (width // 2) : (half + 1) * (width // 2)]
    near_z.start()
    near_out.start()
    wout[core, my_rows, :] = v["own"][core]
    first = core == 0

    def settle(near, stage, staged, win):
        near.wait_recv()
        mine, other = stage[core], staged[...]
        pair = jnp.concatenate(
            [jnp.where(first, mine, other), jnp.where(first, other, mine)], axis=0
        )
        win[core, lower(chip, 2 * share), :] = pair.astype(BF16)

    settle(near_c, stage_c, v["staged_c"], win_c)
    gathers = [
        Gather(at, buf, tall, g, *sems[:6])
        for g, (buf, tall) in enumerate(((win_c, 2 * share), (win_z, 2 * share), (wout, 2 * rows)))
    ]
    events = [g.events() for g in gathers]

    def run_events(order):
        for g, k in order:
            events[g][k]()

    run_events([(0, 0)])
    settle(near_z, stage_z, v["staged_z"], win_z)
    misc = v["misc"]
    misc[...] = jnp.zeros_like(misc)
    put(misc, 0, 0, bias_ref[...][None])
    put(misc, 1, 0, rate_ref[...][None])
    put(misc, 2, 0, skip_ref[...][None])

    segr = seg_ref[...][None].astype(F32)
    segc = jnp.broadcast_to(segr, (LANES, length)).T
    slots = lax.broadcasted_iota(jnp.int32, (length, LANES), 0)
    for j in range(1, KCONV):
        same = (slots >= j) & (pltpu.roll(segc, j, 0) == segc)
        v["shift"][j - 1] = jnp.where(same, 1.0, 0.0)
    below = lax.broadcasted_iota(jnp.int32, (length, length), 0) >= lax.broadcasted_iota(
        jnp.int32, (length, length), 1
    )
    seg_wide = jnp.concatenate([segc] * (length // LANES), axis=1)
    linked = below & (seg_wide == segr)
    v["mask"][...] = jnp.where(linked, 1.0, 0.0)
    v["neg"][...] = jnp.where(linked, 0.0, -1e30)
    x = x_ref[...].astype(F32)
    inv = lax.rsqrt(jnp.mean(x * x, axis=-1, keepdims=True) + EPSILON)
    v["inv"][...] = jnp.broadcast_to(inv, (length, LANES))
    v["unit"][...] = x * inv
    live = slots[:, :1] < live_ref[...][None]
    v["masked"][...] = jnp.where(live, ct_ref[...].astype(F32), 0.0).astype(BF16)
    v["enorm"][...] = lane_pick(width // n, width).astype(BF16)
    v["econv"][...] = lane_pick(CONV // n, CONV).astype(BF16)
    v["egate"][...] = lane_pick(DI // n, DI).astype(BF16)
    head = lax.broadcasted_iota(jnp.int32, (LANES, DI), 0) * HDIM
    channel = lax.broadcasted_iota(jnp.int32, (LANES, DI), 1)
    v["eskip"][...] = jnp.where((channel >= head) & (channel < head + HDIM), 1.0, 0.0)
    place_col = lax.broadcasted_iota(jnp.int32, (n, n * share), 1)
    place_row = lax.broadcasted_iota(jnp.int32, (n, n * share), 0) * share
    for k in range(SECTIONS):
        v["psel"][k * n : (k + 1) * n, :] = jnp.where(place_col == place_row + k, 1.0, 0.0).astype(BF16)
    v["skip"][...] = jnp.dot(
        jnp.broadcast_to(misc[2:3, :], (8, LANES)), v["eskip"][...],
        precision=HIGHEST, preferred_element_type=F32,
    )
    bias_row = misc[0:1, :]
    rate_row = jnp.exp(misc[1:2, :])

    run_events(
        [(0, 1), (0, 2), (1, 0), (0, 3), (0, 4), (0, 5), (1, 1), (1, 2), (0, 6), (0, 7), (0, 8)]
        + [(1, 3), (1, 4), (0, 9), (0, 10), (1, 5)]
    )
    near_out.wait_recv()
    run_events([(2, 0), (0, 11), (1, 6)])
    gathers[0].finish()
    left = [(1, 7), (1, 8), (2, 1), (1, 9), (2, 2), (1, 10), (2, 3), (1, 11), (2, 4)]
    left += [(2, k) for k in range(5, 12)]

    def pump(count):
        run_events(left[:count])
        del left[:count]

    vectors = dot(v["psel"][: 8 * n, :], win_c[1, :, spare:])

    def spread_vector(k, pick, count):
        wide = dot(vectors[k * n : (k + 1) * n, :], pick)
        return jnp.sum(jnp.where(owner_mask(n, count), wide, 0.0), axis=0, keepdims=True)

    gain = spread_vector(0, v["enorm"][...], width)
    v["gain"][0:1, :] = gain
    exact = v["unit"][...] * gain
    v["normed"][...] = exact.astype(BF16)
    normed = v["normed"]
    part = dot(normed[...], win_c[0])
    v["proj"][:, CONV : CONV + hz] = part[:, :hz]
    v["proj"][:, DI:CONV] = part[:, hz:]
    v["proj"][:, CONV + hz : CONV + DI + LANES] = dot(normed[...], win_c[1, :, :spare])
    pump(2)
    for k in range(KCONV + 1):
        v["cw"][k : k + 1, :] = spread_vector(1 + k, v["econv"][...], CONV)
    v["gate"][0:1, :] = spread_vector(KCONV + 2, v["egate"][...], DI)
    proj, pre, scan, low = v["proj"], v["pre"], v["scan"], v["low"]
    cw, gate, skip = v["cw"], v["gate"], v["skip"]
    shifted = proj[:, 2 * CONV - 2 * LANES : 2 * CONV - LANES] + bias_row
    step = softplus(shifted)
    decay = -step * rate_row
    running = jnp.dot(v["mask"][...], decay, precision=HIGHEST, preferred_element_type=F32)
    v["run"][...] = running
    v["runt"][...] = running.T
    v["stept"][...] = step.T
    inter, stept, run, runt, neg = v["inter"], v["stept"], v["run"], v["runt"], v["neg"]

    def conv_tile(i):
        return chunk_ds(i + CONV // LANES) if not isinstance(i, int) else slice(i * LANES, (i + 1) * LANES)

    def conv(ds, wide):
        xs = proj[:, wide]
        total = cw[KCONV : KCONV + 1, ds] + cw[KCONV - 1 : KCONV, ds] * xs
        for j in range(1, KCONV):
            moved = pltpu.roll(xs, j, 0) * v["shift"][j - 1]
            total = total + cw[KCONV - 1 - j : KCONV - j, ds] * moved
        pre[:, ds] = total
        return total

    pre_k = conv(slice(DI, DI + LANES), slice(DI, DI + LANES))
    pre_q = conv(slice(DI + LANES, CONV), slice(DI + LANES, CONV))
    keys = (pre_k * sigmoid(pre_k)).astype(BF16)
    queries = (pre_q * sigmoid(pre_q)).astype(BF16)
    inter[...] = dot(queries, keys, NT)
    lane = lax.broadcasted_iota(jnp.int32, (length, LANES), 1)

    def factor_of(h):
        spread = column(run[...], h) - runt[pl.ds(h, 1), :]
        return jnp.exp(spread + neg[...])

    def forward_pair(i):
        ds = chunk_ds(i)
        total = conv(ds, conv_tile(i))
        values = total * sigmoid(total)
        low_values = values.astype(BF16)
        outs = []
        for side in range(2):
            h = 2 * i + side
            weights = factor_of(h) * inter[...] * stept[pl.ds(h, 1), :]
            outs.append(dot(weights, low_values))
        scan[:, ds] = jnp.where(lane < HDIM, outs[0], outs[1]) + skip[0:1, ds] * values

    pairs = DI // LANES
    cuts = 4
    for k in range(cuts):
        pump(2)
        loop(pairs // cuts, lambda i, k=k: forward_pair(i + k * (pairs // cuts)))
    while len(left) > 3:
        pump(1)
    gathers[1].finish()
    for half in range(2):
        proj[:, half * hz : (half + 1) * hz] = dot(normed[...], win_z[half])
    pump(1)

    def gate_tile(i, sumsq):
        ds = chunk_ds(i)
        z = proj[:, ds]
        gated = scan[:, ds] * (z * sigmoid(z))
        v["gated"][:, ds] = gated
        return sumsq + gated * gated

    sumsq = lax.fori_loop(0, pairs, gate_tile, jnp.zeros((length, LANES), F32))
    pump(1)
    scale = lax.rsqrt(jnp.sum(sumsq, axis=1, keepdims=True) / DI + EPSILON)

    def finish(i, _):
        ds = chunk_ds(i)
        low[:, ds] = (v["gated"][:, ds] * scale * gate[0:1, ds]).astype(BF16)
        return 0

    lax.fori_loop(0, pairs, finish, 0)
    items = [Reduce(at, k, refs, s_red, r_red) for k, refs in enumerate(items_refs)]
    weights_item, columns = items[0], items[1:]
    for half in range(2):
        part = dot(low[...], v["masked"][:, half * (width // 2) : (half + 1) * (width // 2)], TN)
        weights_item.part[half] = part.astype(BF16).reshape(weights_item.part.shape[1:])
    weights_item.start()
    pump(99)
    gathers[2].finish()
    for half in range(2):
        term = dot(v["masked"][:, half * (width // 2) : (half + 1) * (width // 2)], wout[half], NT)
        v["gm"][...] = term if half == 0 else v["gm"][...] + term
    v["normt"][...] = (v["unit"][...] * v["gain"][0:1, :]).T.astype(BF16)

    dinter, row_s, col_s, gconv, gdi = v["dinter"], v["row"], v["col"], v["gconv"], v["gdi"]
    glow, gm = v["glow"], v["gm"]
    for ref in (dinter, row_s, col_s, gconv, gdi):
        ref[...] = jnp.zeros_like(ref)

    def sums(i, inner):
        ds = chunk_ds(i)
        return inner + v["gated"][:, ds] * gm[:, ds] * gate[0:1, ds]

    inner = lax.fori_loop(0, pairs, sums, jnp.zeros((length, LANES), F32))
    weights_item.pairs()
    coef = scale * scale * scale * (jnp.sum(inner, axis=1, keepdims=True) / DI)

    def conv_back(ds, wide, grad_act):
        pre_c = pre[:, ds]
        sg = sigmoid(pre_c)
        gpre = grad_act * (sg * (1.0 + pre_c * (1.0 - sg)))
        xs = proj[:, wide]
        total = cw[KCONV - 1 : KCONV, ds] * gpre
        gconv[KCONV : KCONV + 1, ds] = jnp.sum(gpre, axis=0, keepdims=True)
        gconv[KCONV - 1 : KCONV, ds] = jnp.sum(gpre * xs, axis=0, keepdims=True)
        for j in range(1, KCONV):
            back = pltpu.roll(gpre * v["shift"][j - 1], length - j, 0)
            total = total + cw[KCONV - 1 - j : KCONV - j, ds] * back
            gconv[KCONV - 1 - j : KCONV - j, ds] = jnp.sum(back * xs, axis=0, keepdims=True)
        glow[:, wide] = total.astype(BF16)

    def backward_pair(i):
        ds = chunk_ds(i)
        z = proj[:, ds]
        sz = sigmoid(z)
        silu_z = z * sz
        scanned = scan[:, ds]
        gated = v["gated"][:, ds]
        grad_out = gm[:, ds]
        gdi[0:1, ds] = jnp.sum(grad_out * gated * scale, axis=0, keepdims=True)
        dgated = scale * (grad_out * gate[0:1, ds]) - gated * coef
        dscan = dgated * silu_z
        glow[:, ds] = (dgated * scanned * (sz * (1.0 + z * (1.0 - sz)))).astype(BF16)
        pre_c = pre[:, ds]
        values = pre_c * sigmoid(pre_c)
        gdi[1:2, ds] = jnp.sum(dscan * values, axis=0, keepdims=True)
        low_values = values.astype(BF16)
        dlow = dscan.astype(BF16)
        outs = []
        for side in range(2):
            h = 2 * i + side
            here = (lane < HDIM) if side == 0 else (lane >= HDIM)
            factor = factor_of(h)
            step_row = stept[pl.ds(h, 1), :]
            scaled = factor * step_row
            outs.append(dot(scaled * inter[...], dlow, TN))
            dweights = dot(jnp.where(here, dscan, 0.0), low_values, NT)
            dinter[...] += dweights * scaled
            products = dweights * factor * inter[...]
            col_s[pl.ds(h, 1), :] = jnp.sum(products, axis=0, keepdims=True)
            row = jnp.sum(products * step_row, axis=1, keepdims=True)
            row_s[...] += jnp.where(lane == h, row, 0.0)
        grad_values = jnp.where(lane < HDIM, outs[0], outs[1]) + skip[0:1, ds] * dscan
        conv_back(ds, conv_tile(i), grad_values)

    def launch(k):
        item = columns[k]
        w = item.part.shape[-1]
        for half in range(2):
            cols = slice(half * CONV + k * w, half * CONV + (k + 1) * w)
            part = dot(v["normt"][...], glow[:, cols])
            item.part[half] = part.astype(BF16).reshape(item.part.shape[1:])
        item.start()

    schedule = {
        2: [lambda: launch(0)],
        4: [columns[0].pairs],
        5: [weights_item.planes, lambda: launch(1)],
        7: [columns[1].pairs, columns[0].planes],
        8: [lambda: launch(2)],
        10: [columns[2].pairs],
        11: [lambda: launch(3)],
    }

    def backward_step(i):
        backward_pair(i)
        for when, todo in schedule.items():
            @pl.when(i == when)
            def _(todo=todo):
                for event in todo:
                    event()

    loop(pairs, backward_step)
    low_dinter = dinter[...].astype(BF16)
    conv_back(slice(DI, DI + LANES), slice(DI, DI + LANES), dot(low_dinter, queries, TN))
    conv_back(slice(DI + LANES, CONV), slice(DI + LANES, CONV), dot(low_dinter, keys))
    dstep = col_s[...].T
    drun = row_s[...] - dstep * step
    ddecay = lax.dot_general(v["mask"][...], drun, TN, precision=HIGHEST, preferred_element_type=F32)
    dstep = dstep - ddecay * rate_row
    graw = dstep * sigmoid(shifted)
    glow[:, 2 * CONV - 2 * LANES : 2 * CONV - LANES] = graw.astype(BF16)
    columns[3].pairs()
    columns[1].planes()
    grad_normed = dot(glow[:, :hz], win_z[0], NT) + dot(glow[:, hz:DI], win_z[1], NT)
    grad_normed = grad_normed + dot(glow[:, CONV : CONV + hz], win_c[0, :, :hz], NT)
    grad_normed = grad_normed + dot(glow[:, DI:CONV], win_c[0, :, hz:], NT)
    grad_normed = grad_normed + dot(
        glow[:, CONV + hz : 2 * CONV - LANES], win_c[1, :, :spare], NT
    )
    unit = v["unit"][...]
    grad_gain = jnp.sum(grad_normed * unit, axis=0, keepdims=True)
    weights_item.lines()

    def owners(vector, pick):
        wide = jnp.where(owner_mask(n, vector.shape[1]), vector, 0.0)
        return dot(wide, pick, NT)

    skip_part = lax.dot_general(
        gdi[...], v["eskip"][...], NT, precision=HIGHEST, preferred_element_type=F32
    )
    per_head = [
        jnp.sum(graw, axis=0, keepdims=True), jnp.sum(ddecay * decay, axis=0, keepdims=True),
        skip_part[1:2, :],
    ]
    stacked = [owners(grad_gain, v["enorm"][...])]
    stacked += [owners(gconv[k : k + 1, :], v["econv"][...]) for k in range(KCONV + 1)]
    stacked += [owners(gdi[0:1, :], v["egate"][...])]
    stacked += [jnp.broadcast_to(row, (n, LANES)) for row in per_head]
    stacked += [jnp.zeros((n, LANES), F32)] * (SECTIONS - len(stacked))
    spread_rows = dot(v["psel"][...], jnp.concatenate(stacked, axis=0), TN)
    final = columns[4]
    shape = final.part.shape[1:]
    final.part[0] = dot(v["normt"][...], glow[:, DI:CONV]).astype(BF16).reshape(shape)
    raw_part = dot(v["normt"][...], glow[:, 2 * CONV - 2 * LANES : 2 * CONV - LANES])
    final.part[1] = jnp.concatenate([raw_part, spread_rows], axis=1).astype(BF16).reshape(shape)
    final.start()
    columns[0].lines()
    columns[2].planes()
    final.pairs()
    columns[1].lines()
    columns[3].planes()
    weights_item.ends()
    grad_unit = grad_normed * v["gain"][0:1, :]
    mean = jnp.mean(grad_unit * unit, axis=-1, keepdims=True)
    gx_ref[...] = ct_ref[...].astype(F32) + v["inv"][:, :1] * (grad_unit - unit * mean)
    columns[2].lines()
    final.planes()
    columns[0].ends()
    columns[3].lines()
    for half in range(2):
        cols = slice(half * (width // 2), (half + 1) * (width // 2))
        branch = dot(low[...], wout[half])
        out_ref[:, cols] = (
            x_ref[:, cols].astype(F32) + jnp.where(live, branch, 0.0)
        ).astype(BF16)
    columns[1].ends()
    columns[2].ends()
    final.lines()
    columns[3].ends()
    final.ends()
    go_ref[:, : width // 2], go_ref[:, width // 2 :] = weights_item.halves()
    for k in range(4):
        w = columns[k].part.shape[-1]
        gi_ref[:, k * w : (k + 1) * w], gi_ref[:, DI + k * w : DI + (k + 1) * w] = columns[k].halves()
    gi_ref[:, 2 * DI : tail], ends = final.halves()
    gi_ref[:, tail:] = ends[:, : proj_width - tail]
    gs_ref[...] = ends[:, LANES:]
    for near in (near_c, near_z, near_out):
        near.wait_send()
    for gather in gathers:
        gather.drain()
    for item in items:
        item.drain()


def finish_kernel(
    out_ref, gx_ref, gi_ref, go_ref, gs_ref,
    output, grad_input, norm, in_share, taps, bias, step, decay, skip, gated, out_share,
):
    output[...] = out_ref[...]
    grad_input[...] = gx_ref[...]
    in_share[...] = gi_ref[...]
    out_share[...] = go_ref[...]
    norm[...] = gs_ref[0, : norm.shape[0]]
    taps[...] = gs_ref[1 : 1 + KCONV, : taps.shape[1]]
    bias[...] = gs_ref[1 + KCONV, : bias.shape[0]]
    gated[...] = gs_ref[2 + KCONV, : gated.shape[0]]
    step[...] = gs_ref[3 + KCONV, :HEADS]
    decay[...] = gs_ref[4 + KCONV, :HEADS]
    skip[...] = gs_ref[5 + KCONV, :HEADS]


def fused_device(
    block_in, segment_ids, live_count, norm_gain, in_weight, conv_weight, conv_bias, step_bias,
    decay_log, skip_gain, gated_gain, out_weight, out_cotangent,
):
    n = lax.axis_size("fsdp")
    length, width = block_in.shape
    share, proj_width = in_weight.shape
    rows = out_weight.shape[0]
    chunks = [(2 * rows, width // 2)] + [(2 * share, DI // 4)] * 4 + [(2 * share, 2 * LANES)]
    names, scratch = fused_scratch(n, length, width, share, rows, chunks)
    vmem = pl.BlockSpec(memory_space=pltpu.VMEM)
    output, grad_input, in_share, out_share, mine = pl.pallas_call(
        functools.partial(fused_kernel, n, names, chunks),
        out_shape=(
            jax.ShapeDtypeStruct((length, width), BF16),
            jax.ShapeDtypeStruct((length, width), F32),
            jax.ShapeDtypeStruct((share, proj_width), F32),
            jax.ShapeDtypeStruct((rows, width), F32),
            jax.ShapeDtypeStruct((share, LANES), F32),
        ),
        in_specs=[vmem] * 13,
        out_specs=[vmem] * 5,
        scratch_shapes=scratch,
        compiler_params=pltpu.CompilerParams(
            collective_id=2, has_side_effects=True, vmem_limit_bytes=60 * 2**20
        ),
        name="layer",
    )(
        block_in, out_cotangent, in_weight, out_weight, norm_gain, conv_weight.T, conv_bias,
        gated_gain, step_bias, decay_log, skip_gain, segment_ids, live_count,
    )
    taps, gated_share = conv_weight.shape[0], gated_gain.shape[0]
    vector = lambda size: jax.ShapeDtypeStruct((size,), F32)
    results = pl.pallas_call(
        finish_kernel,
        out_shape=(
            jax.ShapeDtypeStruct((length, width), BF16),
            jax.ShapeDtypeStruct((length, width), F32),
            vector(norm_gain.shape[0]),
            jax.ShapeDtypeStruct((share, proj_width), F32),
            jax.ShapeDtypeStruct((KCONV, taps), F32),
            vector(taps), vector(HEADS), vector(HEADS), vector(HEADS), vector(gated_share),
            jax.ShapeDtypeStruct((rows, width), F32),
        ),
        in_specs=[vmem] * 5,
        out_specs=[vmem] * 11,
        name="finish",
    )(output, grad_input, in_share, out_share, mine)
    return results[:4] + (results[4].T,) + results[5:]


def fits(block_in, in_weight, out_weight, n):
    plane, line = split(n)
    share, rows = in_weight.shape[0], out_weight.shape[0]
    return (
        plane == 4 and line % 2 == 0 and share % 8 == 0 and rows % 16 == 0
        and block_in.shape[0] % LANES == 0 and share >= SECTIONS
    )


def either(*args):
    n = lax.axis_size("fsdp")
    chosen = fused_device if fits(args[0], args[4], args[11], n) else per_device
    return chosen(*args)


def solution(mesh):
    rows, vec, whole = P("fsdp", None), P("fsdp"), P()
    in_specs = (rows, vec, vec, vec, rows, rows, vec, whole, whole, whole, vec, rows, rows)
    out_specs = (rows, rows, vec, rows, rows, vec, whole, whole, whole, vec, rows)
    return jax.shard_map(
        either, mesh=mesh, in_specs=in_specs, out_specs=out_specs, check_vma=False
    )
```

```python
import functools

import jax
import jax.numpy as jnp
from jax import lax
from jax.experimental import pallas as pl
from jax.experimental.pallas import tpu as pltpu
from jax.sharding import PartitionSpec as P

DI = 1536
STATE = 128
HDIM = 64
KCONV = 4
HEADS = 24
CONV = 1792
LANES = 128
EPSILON = 1e-05
HIGHEST = lax.Precision.HIGHEST
F32 = jnp.float32
BF16 = jnp.bfloat16
NT = (((1,), (1,)), ((), ()))
TN = (((0,), (0,)), ((), ()))
MESH = pl.DeviceIdType.MESH


def rms_scale(values, gain_vec):
    return (
        values * lax.rsqrt(jnp.mean(values * values, axis=-1, keepdims=True) + EPSILON) * gain_vec
    )


def dot(a, b, dims=(((1,), (0,)), ((), ()))):
    return lax.dot_general(a.astype(BF16), b.astype(BF16), dims, preferred_element_type=F32)


def sigmoid(v):
    return 1.0 / (1.0 + jnp.exp(-v))


def softplus(v):
    return jnp.maximum(v, 0.0) + jnp.log1p(jnp.exp(-jnp.abs(v)))


def chunk_ds(i):
    return pl.ds(pl.multiple_of(i * LANES, LANES), LANES)


def head_prelude(raw_ref, segc, segr, bias_ref, rate_ref):
    length = raw_ref.shape[0]
    rows = lax.broadcasted_iota(jnp.int32, (length, length), 0)
    cols = lax.broadcasted_iota(jnp.int32, (length, length), 1)
    mask = ((rows >= cols) & (segc == segr)).astype(F32)
    shifted = raw_ref[...] + bias_ref[...]
    step = softplus(shifted)
    decay = -step * rate_ref[...]
    running = jnp.dot(mask, decay, precision=HIGHEST, preferred_element_type=F32)
    return mask, shifted, step, decay, running


def column(values, h):
    lane = lax.broadcasted_iota(jnp.int32, values.shape, 1)
    return jnp.sum(jnp.where(lane == h, values, 0.0), axis=1, keepdims=True)


def decay_of(mask_ref, run_ref, run_t_ref, h):
    spread = column(run_ref[...], h) - run_t_ref[pl.ds(h, 1), :]
    mask = mask_ref[...]
    return jnp.where(mask > 0, jnp.exp(jnp.where(mask > 0, spread, 0.0)), 0.0)


def forward_kernel(
    proj_ref, raw_ref, segc_ref, segr_ref, shift_ref, cw_ref, bias_ref, rate_ref, skip_ref, gain_ref,
    pre_ref, scan_ref, low_ref,
    mask_s, run_s, runt_s, stept_s, inter_s, gated_s,
):
    length = proj_ref.shape[0]
    mask, _, step, _, running = head_prelude(
        raw_ref, segc_ref[...], segr_ref[...], bias_ref, rate_ref
    )
    mask_s[...] = mask
    run_s[...] = running
    runt_s[...] = running.T
    stept_s[...] = step.T

    def conv(i, _):
        ds = chunk_ds(i)
        x = proj_ref[:, chunk_ds(i + DI // LANES)]
        total = cw_ref[KCONV : KCONV + 1, ds] + cw_ref[KCONV - 1 : KCONV, ds] * x
        for j in range(1, KCONV):
            moved = pltpu.roll(x, j, 0) * shift_ref[:, j - 1 : j]
            total = total + cw_ref[KCONV - 1 - j : KCONV - j, ds] * moved
        pre_ref[:, ds] = total
        return 0

    lax.fori_loop(0, CONV // LANES, conv, 0)
    pre_k = pre_ref[:, DI : DI + STATE]
    pre_q = pre_ref[:, DI + STATE :]
    inter_s[...] = dot(pre_q * sigmoid(pre_q), pre_k * sigmoid(pre_k), NT)

    def pair(i, sumsq):
        ds = chunk_ds(i)
        pre = pre_ref[:, ds]
        values = pre * sigmoid(pre)
        low = values.astype(BF16)
        outs = []
        for side in range(2):
            h = 2 * i + side
            weights = decay_of(mask_s, run_s, runt_s, h) * inter_s[...] * stept_s[pl.ds(h, 1), :]
            outs.append(dot(weights, low))
        lane = lax.broadcasted_iota(jnp.int32, (length, LANES), 1)
        scanned = jnp.where(lane < HDIM, outs[0], outs[1]) + skip_ref[:, ds] * values
        scan_ref[:, ds] = scanned
        z = proj_ref[:, ds]
        gated = scanned * (z * sigmoid(z))
        gated_s[:, ds] = gated
        return sumsq + gated * gated

    sumsq = lax.fori_loop(0, DI // LANES, pair, jnp.zeros((length, LANES), F32))
    scale = lax.rsqrt(jnp.sum(sumsq, axis=1, keepdims=True) / DI + EPSILON)

    def finish(i, _):
        ds = chunk_ds(i)
        low_ref[:, ds] = (gated_s[:, ds] * scale * gain_ref[:, ds]).astype(BF16)
        return 0

    lax.fori_loop(0, DI // LANES, finish, 0)


def backward_kernel(
    proj_ref, raw_ref, segc_ref, segr_ref, shift_ref, cw_ref, bias_ref, rate_ref, skip_ref, gain_ref,
    pre_ref, scan_ref, gm_ref,
    glow_ref, graw_ref, gconv_ref, gdi_ref, ghead_ref,
    mask_s, run_s, runt_s, stept_s, inter_s, dinter_s, row_s, col_s,
):
    length = proj_ref.shape[0]
    mask, shifted, step, decay, running = head_prelude(
        raw_ref, segc_ref[...], segr_ref[...], bias_ref, rate_ref
    )
    mask_s[...] = mask
    run_s[...] = running
    runt_s[...] = running.T
    stept_s[...] = step.T
    pre_k = pre_ref[:, DI : DI + STATE]
    pre_q = pre_ref[:, DI + STATE :]
    keys = (pre_k * sigmoid(pre_k)).astype(BF16)
    queries = (pre_q * sigmoid(pre_q)).astype(BF16)
    inter_s[...] = dot(queries, keys, NT)
    dinter_s[...] = jnp.zeros_like(dinter_s)
    row_s[...] = jnp.zeros_like(row_s)
    col_s[...] = jnp.zeros_like(col_s)
    gconv_ref[...] = jnp.zeros_like(gconv_ref)
    gdi_ref[...] = jnp.zeros_like(gdi_ref)
    ghead_ref[...] = jnp.zeros_like(ghead_ref)

    def sums(i, carry):
        sumsq, inner = carry
        ds = chunk_ds(i)
        z = proj_ref[:, ds]
        gated = scan_ref[:, ds] * (z * sigmoid(z))
        return sumsq + gated * gated, inner + gated * gm_ref[:, ds] * gain_ref[:, ds]

    zero = jnp.zeros((length, LANES), F32)
    sumsq, inner = lax.fori_loop(0, DI // LANES, sums, (zero, zero))
    scale = lax.rsqrt(jnp.sum(sumsq, axis=1, keepdims=True) / DI + EPSILON)
    coef = scale * scale * scale * (jnp.sum(inner, axis=1, keepdims=True) / DI)

    def conv_back(i, grad_act):
        ds = chunk_ds(i)
        wide = chunk_ds(i + DI // LANES)
        pre = pre_ref[:, ds]
        sg = sigmoid(pre)
        gpre = grad_act * (sg * (1.0 + pre * (1.0 - sg)))
        x = proj_ref[:, wide]
        total = cw_ref[KCONV - 1 : KCONV, ds] * gpre
        gconv_ref[KCONV : KCONV + 1, ds] = jnp.sum(gpre, axis=0, keepdims=True)
        gconv_ref[KCONV - 1 : KCONV, ds] = jnp.sum(gpre * x, axis=0, keepdims=True)
        for j in range(1, KCONV):
            live = gpre * shift_ref[:, j - 1 : j]
            back = pltpu.roll(live, length - j, 0)
            total = total + cw_ref[KCONV - 1 - j : KCONV - j, ds] * back
            gconv_ref[KCONV - 1 - j : KCONV - j, ds] = jnp.sum(back * x, axis=0, keepdims=True)
        glow_ref[:, wide] = total.astype(BF16)

    def pair(i, _):
        ds = chunk_ds(i)
        z = proj_ref[:, ds]
        sz = sigmoid(z)
        silu_z = z * sz
        scanned = scan_ref[:, ds]
        gated = scanned * silu_z
        grad_out = gm_ref[:, ds]
        gdi_ref[0:1, ds] = jnp.sum(grad_out * gated * scale, axis=0, keepdims=True)
        dgated = scale * (grad_out * gain_ref[:, ds]) - gated * coef
        dscan = dgated * silu_z
        glow_ref[:, ds] = (dgated * scanned * (sz * (1.0 + z * (1.0 - sz)))).astype(BF16)
        pre = pre_ref[:, ds]
        values = pre * sigmoid(pre)
        gdi_ref[1:2, ds] = jnp.sum(dscan * values, axis=0, keepdims=True)
        low = values.astype(BF16)
        dlow = dscan.astype(BF16)
        lane = lax.broadcasted_iota(jnp.int32, (length, LANES), 1)
        head_lane = lax.broadcasted_iota(jnp.int32, (length, LANES), 1)
        outs = []
        for side in range(2):
            h = 2 * i + side
            here = (lane < HDIM) if side == 0 else (lane >= HDIM)
            factor = decay_of(mask_s, run_s, runt_s, h)
            stept = stept_s[pl.ds(h, 1), :]
            inter = inter_s[...]
            scaled = factor * stept
            outs.append(dot(scaled * inter, dlow, TN))
            dweights = dot(jnp.where(here, dscan, 0.0), low, NT)
            dinter_s[...] += dweights * scaled
            pairs = dweights * factor * inter
            col_s[pl.ds(h, 1), :] = jnp.sum(pairs, axis=0, keepdims=True)
            row = jnp.sum(pairs * stept, axis=1, keepdims=True)
            row_s[...] += jnp.where(head_lane == h, row, 0.0)
        grad_values = jnp.where(lane < HDIM, outs[0], outs[1]) + skip_ref[:, ds] * dscan
        conv_back(i, grad_values)
        return 0

    lax.fori_loop(0, DI // LANES, pair, 0)
    dinter = dinter_s[...].astype(BF16)
    conv_back(DI // LANES, dot(dinter, queries, TN))
    conv_back(DI // LANES + 1, dot(dinter, keys))
    dstep = col_s[...].T
    drun = row_s[...] - dstep * step
    ddecay = lax.dot_general(
        mask_s[...], drun, TN, precision=HIGHEST, preferred_element_type=F32
    )
    dstep = dstep - ddecay * rate_ref[...]
    graw = dstep * sigmoid(shifted)
    graw_ref[...] = graw.astype(BF16)
    ghead_ref[0:1, :] = jnp.sum(graw, axis=0, keepdims=True)
    ghead_ref[1:2, :] = jnp.sum(ddecay * decay, axis=0, keepdims=True)


def forward_mixer(proj, raw, small):
    length = proj.shape[0]
    vec = pltpu.VMEM
    return pl.pallas_call(
        forward_kernel,
        out_shape=(
            jax.ShapeDtypeStruct((length, CONV), F32),
            jax.ShapeDtypeStruct((length, DI), F32),
            jax.ShapeDtypeStruct((length, DI), BF16),
        ),
        in_specs=[pl.BlockSpec(memory_space=vec)] * 10,
        out_specs=[pl.BlockSpec(memory_space=vec)] * 3,
        scratch_shapes=[
            pltpu.VMEM((length, length), F32),
            pltpu.VMEM((length, LANES), F32),
            pltpu.VMEM((LANES, length), F32),
            pltpu.VMEM((LANES, length), F32),
            pltpu.VMEM((length, length), F32),
            pltpu.VMEM((length, DI), F32),
        ],
        compiler_params=pltpu.CompilerParams(vmem_limit_bytes=40 * 2**20),
        cost_estimate=pl.CostEstimate(
            flops=HEADS * length * length * 280, bytes_accessed=length * 30000, transcendentals=0
        ),
        name="mixer_forward",
    )(proj, raw, *small)


def backward_mixer(proj, raw, small, pre, scanned, grad_mixer):
    length, width = proj.shape[0], DI + CONV
    vec = pltpu.VMEM
    return pl.pallas_call(
        backward_kernel,
        out_shape=(
            jax.ShapeDtypeStruct((length, width), BF16),
            jax.ShapeDtypeStruct((length, LANES), BF16),
            jax.ShapeDtypeStruct((8, CONV), F32),
            jax.ShapeDtypeStruct((8, DI), F32),
            jax.ShapeDtypeStruct((8, LANES), F32),
        ),
        in_specs=[pl.BlockSpec(memory_space=vec)] * 13,
        out_specs=[pl.BlockSpec(memory_space=vec)] * 5,
        scratch_shapes=[
            pltpu.VMEM((length, length), F32),
            pltpu.VMEM((length, LANES), F32),
            pltpu.VMEM((LANES, length), F32),
            pltpu.VMEM((LANES, length), F32),
            pltpu.VMEM((length, length), F32),
            pltpu.VMEM((length, length), F32),
            pltpu.VMEM((length, LANES), F32),
            pltpu.VMEM((LANES, length), F32),
        ],
        compiler_params=pltpu.CompilerParams(vmem_limit_bytes=40 * 2**20),
        cost_estimate=pl.CostEstimate(
            flops=HEADS * length * length * 800, bytes_accessed=length * 60000, transcendentals=0
        ),
        name="mixer_backward",
    )(proj, raw, *small, pre, scanned, grad_mixer)


def place(n):
    me = lax.axis_index("fsdp")
    core, chip = lax.rem(me, 2), lax.div(me, 2)
    plane, line = split(n)
    return me, core, lax.rem(chip, plane), lax.div(chip, plane)


def split(n):
    half = n // 2
    plane = 4 if half % 4 == 0 else 1
    return plane, half // plane


def loop(count, step):
    def body(k, _):
        step(k)
        return 0

    lax.fori_loop(0, count, body, 0)


def greet(n, me, core, spot, rank):
    plane, line = split(n)
    barrier = pltpu.get_barrier_semaphore()

    def signal(device):
        pl.semaphore_signal(barrier, inc=1, device_id=(device,), device_id_type=MESH)

    signal(me + 1 - 2 * core)
    for j in range(plane - 1):
        signal(2 * (rank * plane + lax.rem(spot + 1 + j, plane)) + core)
    loop(line - 1, lambda r: signal(2 * (lax.rem(rank + 1 + r, line) * plane + spot) + core))
    pl.semaphore_wait(barrier, plane + line - 1)


def gather_kernel(
    n, x0, x1, x2, o0, o1, o2, own_sem, s_line, r_line, s_plane, r_plane, s_near, r_near
):
    plane, line = split(n)
    me, core, spot, rank = place(n)
    partner = me + 1 - 2 * core
    greet(n, me, core, spot, rank)
    groups = ((x0, o0), (x1, o1), (x2, o2))

    def send(g, src, slot, sems, index, device):
        return pltpu.make_async_remote_copy(
            src_ref=src,
            dst_ref=groups[g][1].at[slot],
            send_sem=sems[0].at[g, index],
            recv_sem=sems[1].at[g, index],
            device_id=(device,),
            device_id_type=MESH,
        )

    def origin(r, j):
        from_rank = lax.rem(rank + 2 * line - 1 - r, line)
        return 2 * (from_rank * plane + lax.rem(spot + 2 * plane - 1 - j, plane))

    def along(g, r, slot):
        device = 2 * (lax.rem(rank + 1 + r, line) * plane + spot) + core
        return send(g, groups[g][0], slot, (s_line, r_line), r, device)

    def across(g, r, j, src, slot):
        device = 2 * (rank * plane + lax.rem(spot + 1 + j, plane)) + core
        return send(g, src, slot, (s_plane, r_plane), plane * r + j, device)

    def near(g, r, j, src, slot):
        return send(g, src, slot, (s_near, r_near), plane * r + j, partner)

    def start_along(r):
        for g in range(3):
            along(g, r, me).start()

    loop(line - 1, start_along)
    for g in range(3):
        x = groups[g][0]
        for j in range(plane - 1):
            across(g, line - 1, j, x, me).start()
        near(g, line - 1, plane - 1, x, me).start()
        pltpu.make_async_copy(x, groups[g][1].at[me], own_sem.at[g]).start()

    def forward(r):
        for j in range(plane - 1):
            slot = origin(r, j) + core
            for g in range(3):
                block = groups[g][1].at[slot]
                across(g, r, j, block, slot).wait_recv()
                near(g, r, j, block, slot).start()

    def spread(r):
        slot = origin(r, plane - 1) + core
        for g in range(3):
            block = groups[g][1].at[slot]
            along(g, r, slot).wait_recv()
            for j in range(plane - 1):
                across(g, r, j, block, slot).start()
            near(g, r, plane - 1, block, slot).start()
        forward(lax.rem(r + line - 1, line))

    loop(line - 1, spread)
    forward((line - 2) % line)

    def drain(r):
        for j in range(plane):
            slot, other = origin(r, j) + core, origin(r, j) + 1 - core
            for g in range(3):
                block = groups[g][1].at[slot]
                near(g, r, j, block, other).wait_recv()
                near(g, r, j, block, slot).wait_send()
                if j < plane - 1:
                    across(g, r, j, block, slot).wait_send()

    loop(line, drain)

    def drain_along(r):
        for g in range(3):
            along(g, r, me).wait_send()

    loop(line - 1, drain_along)
    for g in range(3):
        pltpu.make_async_copy(groups[g][0], groups[g][1].at[me], own_sem.at[g]).wait()


def reduce_kernel(
    n, a0, a1, a2, o0, o1, o2, p0, p1, p2, t0, t1, t2, q0, q1, q2,
    u0, u1, u2, v0, v1, v2, w0, w1, w2,
    s_near, r_near, s_plane, r_plane, s_line, r_line,
):
    plane, line = split(n)
    me, core, spot, rank = place(n)
    partner = me + 1 - 2 * core
    greet(n, me, core, spot, rank)
    groups = (
        (a0, o0, p0, t0, q0, u0, v0, w0),
        (a1, o1, p1, t1, q1, u1, v1, w1),
        (a2, o2, p2, t2, q2, u2, v2, w2),
    )

    def send(src, dst, sems, g, index, device):
        return pltpu.make_async_remote_copy(
            src_ref=src.at[index] if not isinstance(src, tuple) else src[0].at[src[1]],
            dst_ref=dst.at[index],
            send_sem=sems[0].at[g, index],
            recv_sem=sems[1].at[g, index],
            device_id=(device,),
            device_id_type=MESH,
        )

    def owner(r, j):
        return 2 * (lax.rem(rank + 1 + r, line) * plane + lax.rem(spot + 1 + j, plane))

    def near(g, r, j):
        src = (groups[g][0], owner(r, j) + 1 - core)
        return send(src, groups[g][2], (s_near, r_near), g, plane * r + j, partner)

    def across(g, r, j):
        device = 2 * (rank * plane + lax.rem(spot + 1 + j, plane)) + core
        return send(groups[g][3], groups[g][4], (s_plane, r_plane), g, plane * r + j, device)

    def along(g, r):
        device = 2 * (lax.rem(rank + 1 + r, line) * plane + spot) + core
        return send(groups[g][6], groups[g][7], (s_line, r_line), g, r, device)

    def both(g, r, j):
        near(g, r, j).wait_recv()
        return groups[g][0][owner(r, j) + core].astype(F32) + groups[g][2][plane * r + j].astype(F32)

    def start_near(r):
        for j in range(plane):
            for g in range(3):
                near(g, r, j).start()

    loop(line, start_near)

    def pairs(r):
        for j in range(plane):
            for g in range(3):
                if j < plane - 1:
                    sums = groups[g][3]
                    sums[plane * r + j] = both(g, r, j).astype(sums.dtype)
                else:
                    groups[g][5][r] = both(g, r, j)
            if j > 0:
                for g in range(3):
                    across(g, r, j - 1).start()

    def total(g, r):
        result = groups[g][5][r]
        for j in range(plane - 1):
            across(g, r, j).wait_recv()
            result = result + groups[g][4][plane * r + j].astype(F32)
        return result

    def planes(r):
        for g in range(3):
            sums = groups[g][6]
            sums[r] = total(g, r).astype(sums.dtype)
        for g in range(3):
            along(g, r).start()

    def step(r):
        pairs(r)

        @pl.when(r > 0)
        def _():
            planes(r - 1)

    loop(line, step)
    for g in range(3):
        groups[g][1][...] = total(g, line - 1)

    def collect(r):
        for g in range(3):
            along(g, r).wait_recv()
            groups[g][1][...] += groups[g][7][r].astype(F32)

    loop(line - 1, collect)

    def drain(r):
        for g in range(3):
            for j in range(plane):
                near(g, r, j).wait_send()
                if j < plane - 1:
                    across(g, r, j).wait_send()

    loop(line, drain)

    def drain_along(r):
        for g in range(3):
            along(g, r).wait_send()

    loop(line - 1, drain_along)


def gather_all(n, shards):
    vmem = pl.BlockSpec(memory_space=pltpu.VMEM)
    half, (_, line) = n // 2, split(n)
    return pl.pallas_call(
        functools.partial(gather_kernel, n),
        out_shape=tuple(jax.ShapeDtypeStruct((n,) + x.shape, x.dtype) for x in shards),
        in_specs=[vmem] * 3,
        out_specs=[vmem] * 3,
        scratch_shapes=[
            pltpu.SemaphoreType.DMA((3,)),
            pltpu.SemaphoreType.DMA((3, line)),
            pltpu.SemaphoreType.DMA((3, line)),
            pltpu.SemaphoreType.DMA((3, half)),
            pltpu.SemaphoreType.DMA((3, half)),
            pltpu.SemaphoreType.DMA((3, half)),
            pltpu.SemaphoreType.DMA((3, half)),
        ],
        compiler_params=pltpu.CompilerParams(
            collective_id=0, has_side_effects=True, vmem_limit_bytes=60 * 2**20
        ),
        name="gather_all",
    )(*shards)


def reduce_all(n, terms):
    vmem = pl.BlockSpec(memory_space=pltpu.VMEM)
    half, (_, line) = n // 2, split(n)
    slots = [pltpu.VMEM((half,) + x.shape[1:], x.dtype) for x in terms]
    partial_sums = [pltpu.VMEM((line,) + x.shape[1:], F32) for x in terms]
    lines = [pltpu.VMEM((line,) + x.shape[1:], x.dtype) for x in terms]
    return pl.pallas_call(
        functools.partial(reduce_kernel, n),
        out_shape=tuple(jax.ShapeDtypeStruct(x.shape[1:], F32) for x in terms),
        in_specs=[vmem] * 3,
        out_specs=[vmem] * 3,
        scratch_shapes=slots * 3
        + partial_sums
        + lines * 2
        + [pltpu.SemaphoreType.DMA((3, half))] * 4
        + [pltpu.SemaphoreType.DMA((3, line))] * 2,
        compiler_params=pltpu.CompilerParams(
            collective_id=1, has_side_effects=True, vmem_limit_bytes=60 * 2**20
        ),
        name="reduce_all",
    )(*terms)


def per_device(
    block_in,
    segment_ids,
    live_count,
    norm_gain,
    in_weight,
    conv_weight,
    conv_bias,
    step_bias,
    decay_log,
    skip_gain,
    gated_gain,
    out_weight,
    out_cotangent,
):
    devices = lax.axis_size("fsdp")
    length = block_in.shape[0]
    share, proj_width = in_weight.shape
    width = block_in.shape[1]
    smalls = jnp.concatenate(
        [norm_gain, conv_weight.T.reshape(-1), conv_bias, gated_gain]
    )
    small_rows = -(-smalls.shape[0] // (8 * LANES)) * 8
    smalls = jnp.pad(smalls, (0, small_rows * LANES - smalls.shape[0])).reshape(small_rows, LANES)
    in_blocks, out_blocks, rest = gather_all(devices, (in_weight, out_weight, smalls))
    in_full = in_blocks.reshape(devices * share, proj_width)
    out_full = out_blocks.reshape(devices * out_weight.shape[0], width)
    rest = rest.reshape(devices, -1).astype(F32)
    a = norm_gain.shape[0]
    b = a + conv_weight.size
    c = b + conv_bias.shape[0]
    d = c + gated_gain.shape[0]
    gain_norm = rest[:, :a].reshape(-1)
    kernel_rows = jnp.moveaxis(rest[:, a:b].reshape(devices, KCONV, -1), 1, 0).reshape(KCONV, CONV)
    kernel_bias = rest[:, b:c].reshape(1, CONV)
    gated = rest[:, c:d].reshape(1, DI)
    conv_rows = jnp.concatenate([kernel_rows, kernel_bias, jnp.zeros((3, CONV), F32)], axis=0)

    def lanes(v):
        return jnp.pad(v, (0, LANES - v.shape[0])).reshape(1, LANES)

    slots = jnp.arange(length)
    shift = jnp.stack(
        [
            ((slots >= j) & (jnp.roll(segment_ids, j) == segment_ids)).astype(F32)
            for j in range(1, KCONV)
        ],
        axis=1,
    )
    shift = jnp.pad(shift, ((0, 0), (0, 8 - shift.shape[1])))
    small = (
        segment_ids.reshape(length, 1),
        segment_ids.reshape(1, length),
        shift,
        conv_rows,
        lanes(step_bias),
        lanes(jnp.exp(decay_log)),
        jnp.repeat(skip_gain, HDIM).reshape(1, DI),
        gated,
    )
    source = block_in.astype(F32)
    live_rows = (lax.iota(jnp.int32, length) < live_count[0]).astype(F32)
    masked = jnp.where(live_rows[:, None] > 0, out_cotangent, jnp.zeros_like(out_cotangent))
    normed = rms_scale(source, gain_norm).astype(BF16)
    main = DI + CONV
    projected = jnp.dot(normed, in_full[:, :main], preferred_element_type=F32)
    tail = jnp.pad(in_full[:, main:], ((0, 0), (0, LANES - HEADS)))
    raw = jnp.dot(normed, tail, preferred_element_type=F32)
    grad_mixer = lax.dot_general(masked, out_full, NT, preferred_element_type=F32)
    pre, scanned, mixer_low = forward_mixer(projected, raw, small)
    grad_out_w = lax.dot_general(mixer_low, masked, TN, preferred_element_type=F32)
    branch = jnp.dot(mixer_low, out_full, preferred_element_type=F32)
    output = (source + live_rows[:, None] * branch).astype(BF16)
    glow, graw, gconv, gdi, ghead = backward_mixer(projected, raw, small, pre, scanned, grad_mixer)
    grad_low = jnp.concatenate([glow, graw], axis=1)
    grad_in_w = lax.dot_general(normed, grad_low, TN, preferred_element_type=F32)
    grad_normed = lax.dot_general(glow, in_full[:, :main], NT, preferred_element_type=F32)
    grad_normed = grad_normed + lax.dot_general(graw, tail, NT, preferred_element_type=F32)
    _, norm_vjp = jax.vjp(rms_scale, source, gain_norm)
    grad_source, grad_gain = norm_vjp(grad_normed)
    grad_input = out_cotangent.astype(F32) + grad_source
    skip_part = gdi[1].reshape(HEADS, HDIM).sum(axis=1)
    heads = jnp.concatenate([ghead[0, :HEADS], ghead[1, :HEADS], skip_part])
    rows = jnp.concatenate(
        [
            grad_gain.reshape(devices, -1),
            jnp.moveaxis(gconv[:KCONV].reshape(KCONV, devices, -1), 0, 1).reshape(devices, -1),
            gconv[KCONV].reshape(devices, -1),
            gdi[0].reshape(devices, -1),
            jnp.broadcast_to(heads, (devices, heads.shape[0])),
        ],
        axis=1,
    )
    sum_rows = -(-rows.shape[1] // (8 * LANES)) * 8
    rows = jnp.pad(rows, ((0, 0), (0, sum_rows * LANES - rows.shape[1])))
    in_share, out_share, mine = reduce_all(
        devices,
        (
            grad_in_w.astype(BF16).reshape(devices, share, -1),
            grad_out_w.astype(BF16).reshape(devices, -1, width),
            rows.reshape(devices, sum_rows, LANES),
        ),
    )
    in_share = in_share[:, :proj_width]
    mine = mine.reshape(-1)
    head_sums = mine[d : d + 3 * HEADS].reshape(3, HEADS)
    return (
        output,
        grad_input,
        mine[:a],
        in_share,
        mine[a:b].reshape(KCONV, -1).T,
        mine[b:c],
        head_sums[0],
        head_sums[1],
        head_sums[2],
        mine[c:d],
        out_share,
    )


SECTIONS = 16


def lower(index, length):
    return pl.ds(pl.multiple_of(index * length, length), length)


class Spot:
    def __init__(self, n):
        self.plane, self.line = split(n)
        self.me, self.core, self.spot, self.rank = place(n)
        self.partner = self.me + 1 - 2 * self.core
        bit0, bit1 = lax.rem(self.spot, 2), lax.div(self.spot, 2)
        self.x = self.spot + 1 - 2 * bit0
        self.y = self.spot + 2 - 4 * bit1
        self.d = 3 - self.spot

    def device(self, rank, spot):
        return 2 * (rank * self.plane + spot) + self.core

    def greet(self):
        barrier = pltpu.get_barrier_semaphore()

        def signal(device):
            pl.semaphore_signal(barrier, inc=1, device_id=(device,), device_id_type=MESH)

        signal(self.partner)
        signal(self.device(self.rank, self.x))
        signal(self.device(self.rank, self.y))
        for k in range(1, self.line):
            signal(self.device(lax.rem(self.rank + k, self.line), self.spot))
        pl.semaphore_wait(barrier, self.line + 2)


def remote(src, dst, send_sem, recv_sem, device):
    return pltpu.make_async_remote_copy(
        src_ref=src, dst_ref=dst, send_sem=send_sem, recv_sem=recv_sem,
        device_id=(device,), device_id_type=MESH,
    )


class Gather:
    def __init__(self, at, buf, rows, g, s_line, r_line, s_plane, r_plane, s_near, r_near):
        self.at, self.buf, self.rows, self.g = at, buf, rows, g
        self.sems = (s_line, r_line, s_plane, r_plane, s_near, r_near)

    def block(self, half, rank, spot):
        return self.buf.at[half, lower(rank * self.at.plane + spot, self.rows)]

    def move(self, half, rank, spot, send, recv, device):
        ref = self.block(half, rank, spot)
        return remote(ref, ref, send, recv, device)

    def step(self, rank, way):
        at, g = self.at, self.g
        s_line, r_line = self.sems[:2]
        device = at.device(at.rank + way, at.spot)
        side = 0 if way > 0 else 1
        return self.move(at.core, rank, at.spot, s_line.at[g, side, rank], r_line.at[g, rank], device)

    def across(self, rank, kind):
        at, g = self.at, self.g
        s_plane, r_plane = self.sems[2:4]
        spot, to = (
            (at.spot, at.x), (at.spot, at.y), (at.x, at.y), (at.y, at.x)
        )[kind]
        slot = min(kind, 2)
        return self.move(
            at.core, rank, spot, s_plane.at[g, slot, rank], r_plane.at[g, slot, rank],
            at.device(at.rank, to),
        )

    def arrived(self, rank, kind):
        at, g = self.at, self.g
        s_plane, r_plane = self.sems[2:4]
        spot = (at.x, at.y, at.d)[kind]
        self.move(
            at.core, rank, spot, s_plane.at[g, kind, rank], r_plane.at[g, kind, rank],
            at.device(at.rank, at.x),
        ).wait_recv()

    def near(self, half, rank):
        at, g = self.at, self.g
        s_near, r_near = self.sems[4:]
        ref = self.buf.at[half, lower(rank, at.plane * self.rows)]
        return remote(ref, ref, s_near.at[g, rank], r_near.at[g, rank], at.partner)

    def spread(self, rank):
        self.across(rank, 0).start()
        self.across(rank, 1).start()

    def own(self):
        at = self.at

        @pl.when(at.rank < at.line - 1)
        def _():
            self.step(at.rank, 1).start()

        @pl.when(at.rank > 0)
        def _():
            self.step(at.rank, -1).start()

        self.spread(at.rank)

    def line_event(self, rank, below):
        at = self.at
        self.step(rank, 1).wait_recv()
        if below:
            @pl.when(at.rank < at.line - 1)
            def _():
                self.step(rank, 1).start()
        else:
            @pl.when(at.rank > 0)
            def _():
                self.step(rank, -1).start()
        self.spread(rank)

    def plane_event(self, rank, below=None):
        at = self.at
        self.arrived(rank, 0)

        @pl.when(lax.rem(rank, 2) == 0)
        def _():
            self.across(rank, 2).start()

        self.arrived(rank, 1)

        @pl.when(lax.rem(rank, 2) == 1)
        def _():
            self.across(rank, 3).start()


    def diagonal_event(self, rank, below=None):
        self.arrived(rank, 2)
        self.near(self.at.core, rank).start()

    def away(self, k, event):
        at = self.at

        @pl.when(at.rank >= k)
        def _():
            event(at.rank - k, True)

        @pl.when(at.rank + k < at.line)
        def _():
            event(at.rank + k, False)

    def events(self):
        at, out = self.at, []
        for k in range(at.line + 2):
            if k == 0:
                out.append(self.own)
            elif k < at.line:
                out.append(functools.partial(self.away, k, self.line_event))
            if k == 1:
                out.append(functools.partial(self.plane_event, at.rank))
            elif 1 < k <= at.line:
                out.append(functools.partial(self.away, k - 1, self.plane_event))
            if k == 2:
                out.append(functools.partial(self.diagonal_event, at.rank))
            elif k > 2:
                out.append(functools.partial(self.away, k - 2, self.diagonal_event))
        return out

    def finish(self):
        at = self.at
        loop(at.line, lambda rank: self.near(1 - at.core, rank).wait_recv())

    def drain(self):
        at = self.at
        loop(at.line, lambda rank: self.near(at.core, rank).wait_send())

        def ranks(rank):
            for kind in range(3):
                self.across(rank, kind).wait_send()

            @pl.when((at.rank < at.line - 1) & (rank <= at.rank))
            def _():
                self.step(rank, 1).wait_send()

            @pl.when((at.rank > 0) & (rank >= at.rank))
            def _():
                self.step(rank, -1).wait_send()

        loop(at.line, ranks)


class Reduce:
    def __init__(self, at, index, refs, send, recv):
        self.at, self.index = at, index
        self.part, self.near_in, self.x1, self.y1, self.x2, self.y2 = refs[:6]
        self.out, self.line_in, self.total, self.last_in = refs[6:]
        self.send, self.recv = send, recv

    def copy(self, k, src, dst, device):
        return remote(src, dst, self.send.at[self.index, k], self.recv.at[self.index, k], device)

    def near(self, k):
        at = self.at
        spot = (at.d, at.y, at.x, at.spot)[k]
        return self.copy(k, self.part.at[1 - at.core, :, spot], self.near_in.at[:, spot], at.partner)

    def start(self):
        for k in range(4):
            self.near(k).start()

    def first(self, side):
        at, half = self.at, self.at.line // 2
        src = self.part.at[at.core, pl.ds(side * half, half), at.d]
        to = at.device(at.rank, (at.x, at.y)[side])
        return self.copy(4 + side, src, (self.x1, self.y1)[side], to)

    def second(self, side):
        at = self.at
        spot = (at.x, at.y)[side]
        src = self.part.at[at.core, :, spot]
        return self.copy(6 + side, src, (self.x2, self.y2)[side], at.device(at.rank, spot))

    def along(self, k):
        at = self.at
        rank = lax.rem(at.rank + 1 + k, at.line)
        return self.copy(9 + k, self.out.at[rank], self.line_in.at[k], at.device(rank, at.spot))

    def last(self):
        at = self.at
        rows = self.last_in.shape[0]
        return self.copy(8, self.total.at[lower(1 - at.core, rows)], self.last_in, at.partner)

    def pair(self, k, ranks=slice(None)):
        at = self.at
        spot = (at.d, at.y, at.x, at.spot)[k]
        return self.part[at.core, ranks, spot].astype(F32) + self.near_in[ranks, spot].astype(F32)

    def pairs(self):
        at = self.at
        self.near(0).wait_recv()
        self.part[at.core, :, at.d] = self.pair(0).astype(BF16)
        self.first(0).start()
        self.first(1).start()

    def planes(self):
        at, half = self.at, self.at.line // 2
        for side, spot in ((0, at.y), (1, at.x)):
            self.near(1 + side).wait_recv()
            self.first(side).wait_recv()
            for part in range(2):
                ranks = slice(part * half, (part + 1) * half)
                mine = self.pair(1 + side, ranks)
                if part == side:
                    mine = mine + (self.x1, self.y1)[side][...].astype(F32)
                self.part[at.core, ranks, spot] = mine.astype(BF16)
            self.second(1 - side).start()

    def lines(self):
        at = self.at
        self.near(3).wait_recv()
        self.second(0).wait_recv()
        self.second(1).wait_recv()
        mine = self.pair(3) + self.x2[...].astype(F32) + self.y2[...].astype(F32)
        self.out[...] = mine.astype(BF16)
        for k in range(at.line - 1):
            self.along(k).start()
        mine = self.part[at.core, at.rank, at.spot].astype(F32)
        mine = mine + self.near_in[at.rank, at.spot].astype(F32)
        self.total[...] = mine + self.x2[at.rank].astype(F32) + self.y2[at.rank].astype(F32)

    def ends(self):
        at = self.at
        for k in range(at.line - 1):
            self.along(k).wait_recv()
        total = self.total[...]
        for k in range(at.line - 1):
            total = total + self.line_in[k].astype(F32)
        self.total[...] = total
        self.last().start()

    def halves(self):
        at = self.at
        self.last().wait_recv()
        rows = self.last_in.shape[0]
        mine, other = self.total[lower(at.core, rows), :], self.last_in[...]
        first = at.core == 0
        return jnp.where(first, mine, other), jnp.where(first, other, mine)

    def drain(self):
        for k in range(4):
            self.near(k).wait_send()
        for side in range(2):
            self.first(side).wait_send()
            self.second(side).wait_send()
        for k in range(self.at.line - 1):
            self.along(k).wait_send()
        self.last().wait_send()


def owner_mask(n, count):
    share = count // n
    rows = lax.broadcasted_iota(jnp.int32, (n, count), 0) * share
    cols = lax.broadcasted_iota(jnp.int32, (n, count), 1)
    return (cols >= rows) & (cols < rows + share)


def lane_pick(share, count):
    lane = lax.broadcasted_iota(jnp.int32, (LANES, count), 0).astype(F32)
    col = lax.broadcasted_iota(jnp.int32, (LANES, count), 1).astype(F32)
    owner = jnp.floor((col + 0.5) * (1.0 / share))
    return jnp.where(col - owner * share == lane, 1.0, 0.0)


def fused_scratch(n, length, width, share, rows, chunks):
    _, line = split(n)
    wide, half_out, half_z = CONV, width // 2, DI // 2
    conv_w = half_z + 2 * LANES
    shapes = dict(
        stage_c=((2, share, conv_w), F32), staged_c=((share, conv_w), F32),
        stage_z=((2, share, half_z), F32), staged_z=((share, half_z), F32),
        own=((2, rows, half_out), BF16), win_c=((2, n * share, conv_w), BF16),
        win_z=((2, n * share, half_z), BF16), wout=((2, n * rows, half_out), BF16),
        mask=((length, length), F32), neg=((length, length), F32),
        shift=((KCONV - 1, length, LANES), F32), unit=((length, width), F32),
        inv=((length, LANES), F32), masked=((length, width), BF16),
        normed=((length, width), BF16), normt=((width, length), BF16),
        enorm=((LANES, width), BF16), econv=((LANES, CONV), BF16), egate=((LANES, DI), BF16),
        eskip=((LANES, DI), F32), psel=((SECTIONS * n, n * share), BF16),
        cw=((8, CONV), F32), gate=((8, DI), F32), skip=((8, DI), F32), gain=((8, width), F32),
        proj=((length, 2 * wide), F32), pre=((length, CONV), F32), scan=((length, DI), F32),
        gated=((length, DI), F32), low=((length, DI), BF16), gm=((length, DI), F32),
        glow=((length, 2 * wide), BF16),
        run=((length, LANES), F32), runt=((LANES, length), F32), stept=((LANES, length), F32),
        inter=((length, length), F32), dinter=((length, length), F32),
        row=((length, LANES), F32), col=((LANES, length), F32),
        gconv=((8, CONV), F32), gdi=((8, DI), F32), misc=((8, LANES), F32),
    )
    names = list(shapes)
    specs = [pltpu.VMEM(*v) for v in shapes.values()]
    for tall, w in chunks:
        for dims, kind in (
            ((2, line, 4, tall, w), BF16), ((line, 4, tall, w), BF16),
            ((line // 2, tall, w), BF16), ((line // 2, tall, w), BF16),
            ((line, tall, w), BF16), ((line, tall, w), BF16),
            ((line, tall, w), BF16), ((line - 1, tall, w), BF16),
            ((tall, w), F32), ((tall // 2, w), F32),
        ):
            specs.append(pltpu.VMEM(dims, kind))
    sems = [
        (3, 2, line), (3, line), (3, 3, line), (3, 3, line), (3, line), (3, line),
        (3,), (3,), (len(chunks), 8 + line), (len(chunks), 8 + line),
    ]
    return names, specs + [pltpu.SemaphoreType.DMA(s) for s in sems]


def fused_kernel(n, names, chunks, x_ref, ct_ref, inw_ref, outw_ref,
                 norm_ref, taps_ref, cbias_ref, gated_ref, bias_ref, rate_ref, skip_ref, seg_ref, live_ref,
                 out_ref, gx_ref, gi_ref, go_ref, gs_ref, *scratch):
    at = Spot(n)
    core = at.core
    v = dict(zip(names, scratch))
    rest = scratch[len(names):]
    items_refs = [rest[10 * i : 10 * i + 10] for i in range(len(chunks))]
    sems = rest[10 * len(chunks):]
    s_own, r_own, s_red, r_red = sems[6:]
    length, width = x_ref.shape
    share, proj_width = inw_ref.shape
    rows = outw_ref.shape[0]
    chip = at.rank * at.plane + at.spot
    tail = DI + CONV
    wout, win_c, win_z, stage_c, stage_z = (
        v[k] for k in ("wout", "win_c", "win_z", "stage_c", "stage_z")
    )
    hz = DI // 2
    spare = hz + LANES

    def put(ref, row, lane, values):
        ref[..., row : row + values.shape[0], lane : lane + values.shape[1]] = values.astype(F32)

    for half in range(2):
        stage_c[half, :, :hz] = inw_ref[:, DI + half * hz : DI + (half + 1) * hz].astype(F32)
    stage_c[0, :, hz:] = inw_ref[:, 2 * DI : tail].astype(F32)
    stage_c[1, :, hz:] = jnp.zeros((share, 2 * LANES), F32)
    tile = stage_c.at[1]
    put(tile, 0, hz, inw_ref[:, tail:])
    put(tile, 0, spare, norm_ref[...][None])
    put(tile, 1, spare, taps_ref[...])
    put(tile, 1 + KCONV, spare, cbias_ref[...][None])
    put(tile, 2 + KCONV, spare, gated_ref[...][None])
    at.greet()

    def exchange(g, src, dst):
        return remote(src, dst, s_own.at[g], r_own.at[g], at.partner)

    my_rows = pl.ds(pl.multiple_of((2 * chip + core) * rows, rows), rows)
    near_c = exchange(0, stage_c.at[1 - core], v["staged_c"])
    near_z = exchange(1, stage_z.at[1 - core], v["staged_z"])
    near_out = exchange(2, v["own"].at[1 - core], wout.at[1 - core, my_rows])
    near_c.start()
    for half in range(2):
        stage_z[half] = inw_ref[:, half * hz : (half + 1) * hz].astype(F32)
        v["own"][half] = outw_ref[:, half * (width // 2) : (half + 1) * (width // 2)]
    near_z.start()
    near_out.start()
    wout[core, my_rows, :] = v["own"][core]
    first = core == 0

    def settle(near, stage, staged, win):
        near.wait_recv()
        mine, other = stage[core], staged[...]
        pair = jnp.concatenate(
            [jnp.where(first, mine, other), jnp.where(first, other, mine)], axis=0
        )
        win[core, lower(chip, 2 * share), :] = pair.astype(BF16)

    settle(near_c, stage_c, v["staged_c"], win_c)
    gathers = [
        Gather(at, buf, tall, g, *sems[:6])
        for g, (buf, tall) in enumerate(((win_c, 2 * share), (win_z, 2 * share), (wout, 2 * rows)))
    ]
    events = [g.events() for g in gathers]

    def run_events(order):
        for g, k in order:
            events[g][k]()

    run_events([(0, 0)])
    settle(near_z, stage_z, v["staged_z"], win_z)
    misc = v["misc"]
    misc[...] = jnp.zeros_like(misc)
    put(misc, 0, 0, bias_ref[...][None])
    put(misc, 1, 0, rate_ref[...][None])
    put(misc, 2, 0, skip_ref[...][None])

    segr = seg_ref[...][None].astype(F32)
    segc = jnp.broadcast_to(segr, (LANES, length)).T
    slots = lax.broadcasted_iota(jnp.int32, (length, LANES), 0)
    for j in range(1, KCONV):
        same = (slots >= j) & (pltpu.roll(segc, j, 0) == segc)
        v["shift"][j - 1] = jnp.where(same, 1.0, 0.0)
    below = lax.broadcasted_iota(jnp.int32, (length, length), 0) >= lax.broadcasted_iota(
        jnp.int32, (length, length), 1
    )
    seg_wide = jnp.concatenate([segc] * (length // LANES), axis=1)
    linked = below & (seg_wide == segr)
    v["mask"][...] = jnp.where(linked, 1.0, 0.0)
    v["neg"][...] = jnp.where(linked, 0.0, -1e30)
    x = x_ref[...].astype(F32)
    inv = lax.rsqrt(jnp.mean(x * x, axis=-1, keepdims=True) + EPSILON)
    v["inv"][...] = jnp.broadcast_to(inv, (length, LANES))
    v["unit"][...] = x * inv
    live = slots[:, :1] < live_ref[...][None]
    v["masked"][...] = jnp.where(live, ct_ref[...].astype(F32), 0.0).astype(BF16)
    v["enorm"][...] = lane_pick(width // n, width).astype(BF16)
    v["econv"][...] = lane_pick(CONV // n, CONV).astype(BF16)
    v["egate"][...] = lane_pick(DI // n, DI).astype(BF16)
    head = lax.broadcasted_iota(jnp.int32, (LANES, DI), 0) * HDIM
    channel = lax.broadcasted_iota(jnp.int32, (LANES, DI), 1)
    v["eskip"][...] = jnp.where((channel >= head) & (channel < head + HDIM), 1.0, 0.0)
    place_col = lax.broadcasted_iota(jnp.int32, (n, n * share), 1)
    place_row = lax.broadcasted_iota(jnp.int32, (n, n * share), 0) * share
    for k in range(SECTIONS):
        v["psel"][k * n : (k + 1) * n, :] = jnp.where(place_col == place_row + k, 1.0, 0.0).astype(BF16)
    v["skip"][...] = jnp.dot(
        jnp.broadcast_to(misc[2:3, :], (8, LANES)), v["eskip"][...],
        precision=HIGHEST, preferred_element_type=F32,
    )
    bias_row = misc[0:1, :]
    rate_row = jnp.exp(misc[1:2, :])

    run_events(
        [(0, 1), (0, 2), (1, 0), (0, 3), (0, 4), (0, 5), (1, 1), (1, 2), (0, 6), (0, 7), (0, 8)]
        + [(1, 3), (1, 4), (0, 9), (0, 10), (1, 5)]
    )
    near_out.wait_recv()
    run_events([(2, 0), (0, 11), (1, 6)])
    gathers[0].finish()
    left = [(1, 7), (1, 8), (2, 1), (1, 9), (2, 2), (1, 10), (2, 3), (1, 11), (2, 4)]
    left += [(2, k) for k in range(5, 12)]

    def pump(count):
        run_events(left[:count])
        del left[:count]

    vectors = dot(v["psel"][: 8 * n, :], win_c[1, :, spare:])

    def spread_vector(k, pick, count):
        wide = dot(vectors[k * n : (k + 1) * n, :], pick)
        return jnp.sum(jnp.where(owner_mask(n, count), wide, 0.0), axis=0, keepdims=True)

    gain = spread_vector(0, v["enorm"][...], width)
    v["gain"][0:1, :] = gain
    exact = v["unit"][...] * gain
    v["normed"][...] = exact.astype(BF16)
    normed = v["normed"]
    part = dot(normed[...], win_c[0])
    v["proj"][:, CONV : CONV + hz] = part[:, :hz]
    v["proj"][:, DI:CONV] = part[:, hz:]
    v["proj"][:, CONV + hz : CONV + DI + LANES] = dot(normed[...], win_c[1, :, :spare])
    pump(2)
    for k in range(KCONV + 1):
        v["cw"][k : k + 1, :] = spread_vector(1 + k, v["econv"][...], CONV)
    v["gate"][0:1, :] = spread_vector(KCONV + 2, v["egate"][...], DI)
    proj, pre, scan, low = v["proj"], v["pre"], v["scan"], v["low"]
    cw, gate, skip = v["cw"], v["gate"], v["skip"]
    shifted = proj[:, 2 * CONV - 2 * LANES : 2 * CONV - LANES] + bias_row
    step = softplus(shifted)
    decay = -step * rate_row
    running = jnp.dot(v["mask"][...], decay, precision=HIGHEST, preferred_element_type=F32)
    v["run"][...] = running
    v["runt"][...] = running.T
    v["stept"][...] = step.T
    inter, stept, run, runt, neg = v["inter"], v["stept"], v["run"], v["runt"], v["neg"]

    def conv_tile(i):
        return chunk_ds(i + CONV // LANES) if not isinstance(i, int) else slice(i * LANES, (i + 1) * LANES)

    def conv(ds, wide):
        xs = proj[:, wide]
        total = cw[KCONV : KCONV + 1, ds] + cw[KCONV - 1 : KCONV, ds] * xs
        for j in range(1, KCONV):
            moved = pltpu.roll(xs, j, 0) * v["shift"][j - 1]
            total = total + cw[KCONV - 1 - j : KCONV - j, ds] * moved
        pre[:, ds] = total
        return total

    pre_k = conv(slice(DI, DI + LANES), slice(DI, DI + LANES))
    pre_q = conv(slice(DI + LANES, CONV), slice(DI + LANES, CONV))
    keys = (pre_k * sigmoid(pre_k)).astype(BF16)
    queries = (pre_q * sigmoid(pre_q)).astype(BF16)
    inter[...] = dot(queries, keys, NT)
    lane = lax.broadcasted_iota(jnp.int32, (length, LANES), 1)

    def factor_of(h):
        spread = column(run[...], h) - runt[pl.ds(h, 1), :]
        return jnp.exp(spread + neg[...])

    def forward_pair(i):
        ds = chunk_ds(i)
        total = conv(ds, conv_tile(i))
        values = total * sigmoid(total)
        low_values = values.astype(BF16)
        outs = []
        for side in range(2):
            h = 2 * i + side
            weights = factor_of(h) * inter[...] * stept[pl.ds(h, 1), :]
            outs.append(dot(weights, low_values))
        scan[:, ds] = jnp.where(lane < HDIM, outs[0], outs[1]) + skip[0:1, ds] * values

    pairs = DI // LANES
    cuts = 4
    for k in range(cuts):
        pump(2)
        loop(pairs // cuts, lambda i, k=k: forward_pair(i + k * (pairs // cuts)))
    while (1, 11) in left:
        pump(1)
    gathers[1].finish()
    for half in range(2):
        proj[:, half * hz : (half + 1) * hz] = dot(normed[...], win_z[half])
    pump(2)

    def gate_tile(i, sumsq):
        ds = chunk_ds(i)
        z = proj[:, ds]
        gated = scan[:, ds] * (z * sigmoid(z))
        v["gated"][:, ds] = gated
        return sumsq + gated * gated

    sumsq = lax.fori_loop(0, pairs, gate_tile, jnp.zeros((length, LANES), F32))
    pump(2)
    scale = lax.rsqrt(jnp.sum(sumsq, axis=1, keepdims=True) / DI + EPSILON)

    def finish(i, _):
        ds = chunk_ds(i)
        low[:, ds] = (v["gated"][:, ds] * scale * gate[0:1, ds]).astype(BF16)
        return 0

    lax.fori_loop(0, pairs, finish, 0)
    items = [Reduce(at, k, refs, s_red, r_red) for k, refs in enumerate(items_refs)]
    weights_item, columns = items[0], items[1:]
    for half in range(2):
        part = dot(low[...], v["masked"][:, half * (width // 2) : (half + 1) * (width // 2)], TN)
        weights_item.part[half] = part.astype(BF16).reshape(weights_item.part.shape[1:])
    weights_item.start()
    pump(99)
    gathers[2].finish()
    weights_item.pairs()
    for half in range(2):
        term = dot(v["masked"][:, half * (width // 2) : (half + 1) * (width // 2)], wout[half], NT)
        v["gm"][...] = term if half == 0 else v["gm"][...] + term
    v["normt"][...] = (v["unit"][...] * v["gain"][0:1, :]).T.astype(BF16)

    dinter, row_s, col_s, gconv, gdi = v["dinter"], v["row"], v["col"], v["gconv"], v["gdi"]
    glow, gm = v["glow"], v["gm"]
    for ref in (dinter, row_s, col_s, gconv, gdi):
        ref[...] = jnp.zeros_like(ref)

    def sums(i, inner):
        ds = chunk_ds(i)
        return inner + v["gated"][:, ds] * gm[:, ds] * gate[0:1, ds]

    inner = lax.fori_loop(0, pairs, sums, jnp.zeros((length, LANES), F32))
    coef = scale * scale * scale * (jnp.sum(inner, axis=1, keepdims=True) / DI)

    def conv_back(ds, wide, grad_act):
        pre_c = pre[:, ds]
        sg = sigmoid(pre_c)
        gpre = grad_act * (sg * (1.0 + pre_c * (1.0 - sg)))
        xs = proj[:, wide]
        total = cw[KCONV - 1 : KCONV, ds] * gpre
        gconv[KCONV : KCONV + 1, ds] = jnp.sum(gpre, axis=0, keepdims=True)
        gconv[KCONV - 1 : KCONV, ds] = jnp.sum(gpre * xs, axis=0, keepdims=True)
        for j in range(1, KCONV):
            back = pltpu.roll(gpre * v["shift"][j - 1], length - j, 0)
            total = total + cw[KCONV - 1 - j : KCONV - j, ds] * back
            gconv[KCONV - 1 - j : KCONV - j, ds] = jnp.sum(back * xs, axis=0, keepdims=True)
        glow[:, wide] = total.astype(BF16)

    def backward_pair(i):
        ds = chunk_ds(i)
        z = proj[:, ds]
        sz = sigmoid(z)
        silu_z = z * sz
        scanned = scan[:, ds]
        gated = v["gated"][:, ds]
        grad_out = gm[:, ds]
        gdi[0:1, ds] = jnp.sum(grad_out * gated * scale, axis=0, keepdims=True)
        dgated = scale * (grad_out * gate[0:1, ds]) - gated * coef
        dscan = dgated * silu_z
        glow[:, ds] = (dgated * scanned * (sz * (1.0 + z * (1.0 - sz)))).astype(BF16)
        pre_c = pre[:, ds]
        values = pre_c * sigmoid(pre_c)
        gdi[1:2, ds] = jnp.sum(dscan * values, axis=0, keepdims=True)
        low_values = values.astype(BF16)
        dlow = dscan.astype(BF16)
        outs = []
        for side in range(2):
            h = 2 * i + side
            here = (lane < HDIM) if side == 0 else (lane >= HDIM)
            mine = jnp.where(here, dscan, 0.0).astype(BF16)
            until = column(run[...], h)
            until_row, step_all = runt[pl.ds(h, 1), :], stept[pl.ds(h, 1), :]
            parts, cols, sums_of_rows = [], [], []
            for begin, end in ((0, length // 2), (length // 2, length)):
                here_rows, seen = slice(begin, end), slice(0, end)
                spread = until[here_rows] - until_row[:, seen]
                factor = jnp.exp(spread + neg[here_rows, seen])
                step_row = step_all[:, seen]
                scaled = factor * step_row
                inter_part = inter[here_rows, seen]
                parts.append(dot(scaled * inter_part, dlow[here_rows], TN))
                dweights = dot(mine[here_rows], low_values[seen], NT)
                dinter[here_rows, seen] += dweights * scaled
                products = dweights * factor * inter_part
                cols.append(jnp.sum(products, axis=0, keepdims=True))
                sums_of_rows.append(jnp.sum(products * step_row, axis=1, keepdims=True))
            half = length // 2
            outs.append(jnp.concatenate([parts[0] + parts[1][:half], parts[1][half:]], axis=0))
            col_s[pl.ds(h, 1), :] = jnp.concatenate(
                [cols[0] + cols[1][:, :half], cols[1][:, half:]], axis=1
            )
            row = jnp.concatenate(sums_of_rows, axis=0)
            row_s[...] += jnp.where(lane == h, row, 0.0)
        grad_values = jnp.where(lane < HDIM, outs[0], outs[1]) + skip[0:1, ds] * dscan
        conv_back(ds, conv_tile(i), grad_values)

    def launch(k):
        item = columns[k]
        w = item.part.shape[-1]
        for half in range(2):
            cols = slice(half * CONV + k * w, half * CONV + (k + 1) * w)
            part = dot(v["normt"][...], glow[:, cols])
            item.part[half] = part.astype(BF16).reshape(item.part.shape[1:])
        item.start()

    schedule = {
        2: [lambda: launch(0)],
        3: [columns[0].pairs],
        4: [weights_item.planes],
        5: [lambda: launch(1)],
        6: [columns[1].pairs],
        7: [columns[0].planes],
        8: [lambda: launch(2)],
        9: [columns[2].pairs],
        11: [lambda: launch(3)],
    }

    def backward_step(i):
        backward_pair(i)
        for when, todo in schedule.items():
            @pl.when(i == when)
            def _(todo=todo):
                for event in todo:
                    event()

    loop(pairs, backward_step)
    columns[1].planes()
    low_dinter = dinter[...].astype(BF16)
    conv_back(slice(DI, DI + LANES), slice(DI, DI + LANES), dot(low_dinter, queries, TN))
    conv_back(slice(DI + LANES, CONV), slice(DI + LANES, CONV), dot(low_dinter, keys))
    columns[3].pairs()
    weights_item.lines()
    dstep = col_s[...].T
    drun = row_s[...] - dstep * step
    ddecay = lax.dot_general(v["mask"][...], drun, TN, precision=HIGHEST, preferred_element_type=F32)
    dstep = dstep - ddecay * rate_row
    graw = dstep * sigmoid(shifted)
    glow[:, 2 * CONV - 2 * LANES : 2 * CONV - LANES] = graw.astype(BF16)
    columns[0].lines()
    columns[2].planes()
    grad_normed = dot(glow[:, :hz], win_z[0], NT) + dot(glow[:, hz:DI], win_z[1], NT)
    grad_normed = grad_normed + dot(glow[:, CONV : CONV + hz], win_c[0, :, :hz], NT)
    grad_normed = grad_normed + dot(glow[:, DI:CONV], win_c[0, :, hz:], NT)
    grad_normed = grad_normed + dot(
        glow[:, CONV + hz : 2 * CONV - LANES], win_c[1, :, :spare], NT
    )
    unit = v["unit"][...]
    grad_gain = jnp.sum(grad_normed * unit, axis=0, keepdims=True)
    columns[1].lines()

    def owners(vector, pick):
        wide = jnp.where(owner_mask(n, vector.shape[1]), vector, 0.0)
        return dot(wide, pick, NT)

    skip_part = lax.dot_general(
        gdi[...], v["eskip"][...], NT, precision=HIGHEST, preferred_element_type=F32
    )
    per_head = [
        jnp.sum(graw, axis=0, keepdims=True), jnp.sum(ddecay * decay, axis=0, keepdims=True),
        skip_part[1:2, :],
    ]
    stacked = [owners(grad_gain, v["enorm"][...])]
    stacked += [owners(gconv[k : k + 1, :], v["econv"][...]) for k in range(KCONV + 1)]
    stacked += [owners(gdi[0:1, :], v["egate"][...])]
    stacked += [jnp.broadcast_to(row, (n, LANES)) for row in per_head]
    stacked += [jnp.zeros((n, LANES), F32)] * (SECTIONS - len(stacked))
    spread_rows = dot(v["psel"][...], jnp.concatenate(stacked, axis=0), TN)
    final = columns[4]
    shape = final.part.shape[1:]
    final.part[0] = dot(v["normt"][...], glow[:, DI:CONV]).astype(BF16).reshape(shape)
    raw_part = dot(v["normt"][...], glow[:, 2 * CONV - 2 * LANES : 2 * CONV - LANES])
    final.part[1] = jnp.concatenate([raw_part, spread_rows], axis=1).astype(BF16).reshape(shape)
    final.start()
    columns[3].planes()
    final.pairs()
    weights_item.ends()
    grad_unit = grad_normed * v["gain"][0:1, :]
    mean = jnp.mean(grad_unit * unit, axis=-1, keepdims=True)
    gx_ref[...] = ct_ref[...].astype(F32) + v["inv"][:, :1] * (grad_unit - unit * mean)
    columns[2].lines()
    final.planes()
    columns[0].ends()
    columns[3].lines()
    for half in range(2):
        cols = slice(half * (width // 2), (half + 1) * (width // 2))
        branch = dot(low[...], wout[half])
        out_ref[:, cols] = (
            x_ref[:, cols].astype(F32) + jnp.where(live, branch, 0.0)
        ).astype(BF16)
    columns[1].ends()
    columns[2].ends()
    final.lines()
    columns[3].ends()
    final.ends()
    go_ref[:, : width // 2], go_ref[:, width // 2 :] = weights_item.halves()
    for k in range(4):
        w = columns[k].part.shape[-1]
        gi_ref[:, k * w : (k + 1) * w], gi_ref[:, DI + k * w : DI + (k + 1) * w] = columns[k].halves()
    gi_ref[:, 2 * DI : tail], ends = final.halves()
    gi_ref[:, tail:] = ends[:, : proj_width - tail]
    gs_ref[...] = ends[:, LANES:]
    for near in (near_c, near_z, near_out):
        near.wait_send()
    for gather in gathers:
        gather.drain()
    for item in items:
        item.drain()


def finish_kernel(
    out_ref, gx_ref, gi_ref, go_ref, gs_ref,
    output, grad_input, norm, in_share, taps, bias, step, decay, skip, gated, out_share,
):
    output[...] = out_ref[...]
    grad_input[...] = gx_ref[...]
    in_share[...] = gi_ref[...]
    out_share[...] = go_ref[...]
    norm[...] = gs_ref[0, : norm.shape[0]]
    taps[...] = gs_ref[1 : 1 + KCONV, : taps.shape[1]]
    bias[...] = gs_ref[1 + KCONV, : bias.shape[0]]
    gated[...] = gs_ref[2 + KCONV, : gated.shape[0]]
    step[...] = gs_ref[3 + KCONV, :HEADS]
    decay[...] = gs_ref[4 + KCONV, :HEADS]
    skip[...] = gs_ref[5 + KCONV, :HEADS]


def fused_device(
    block_in, segment_ids, live_count, norm_gain, in_weight, conv_weight, conv_bias, step_bias,
    decay_log, skip_gain, gated_gain, out_weight, out_cotangent,
):
    n = lax.axis_size("fsdp")
    length, width = block_in.shape
    share, proj_width = in_weight.shape
    rows = out_weight.shape[0]
    chunks = [(2 * rows, width // 2)] + [(2 * share, DI // 4)] * 4 + [(2 * share, 2 * LANES)]
    names, scratch = fused_scratch(n, length, width, share, rows, chunks)
    vmem = pl.BlockSpec(memory_space=pltpu.VMEM)
    output, grad_input, in_share, out_share, mine = pl.pallas_call(
        functools.partial(fused_kernel, n, names, chunks),
        out_shape=(
            jax.ShapeDtypeStruct((length, width), BF16),
            jax.ShapeDtypeStruct((length, width), F32),
            jax.ShapeDtypeStruct((share, proj_width), F32),
            jax.ShapeDtypeStruct((rows, width), F32),
            jax.ShapeDtypeStruct((share, LANES), F32),
        ),
        in_specs=[vmem] * 13,
        out_specs=[vmem] * 5,
        scratch_shapes=scratch,
        compiler_params=pltpu.CompilerParams(
            collective_id=2, has_side_effects=True, vmem_limit_bytes=60 * 2**20
        ),
        name="layer",
    )(
        block_in, out_cotangent, in_weight, out_weight, norm_gain, conv_weight.T, conv_bias,
        gated_gain, step_bias, decay_log, skip_gain, segment_ids, live_count,
    )
    taps, gated_share = conv_weight.shape[0], gated_gain.shape[0]
    vector = lambda size: jax.ShapeDtypeStruct((size,), F32)
    results = pl.pallas_call(
        finish_kernel,
        out_shape=(
            jax.ShapeDtypeStruct((length, width), BF16),
            jax.ShapeDtypeStruct((length, width), F32),
            vector(norm_gain.shape[0]),
            jax.ShapeDtypeStruct((share, proj_width), F32),
            jax.ShapeDtypeStruct((KCONV, taps), F32),
            vector(taps), vector(HEADS), vector(HEADS), vector(HEADS), vector(gated_share),
            jax.ShapeDtypeStruct((rows, width), F32),
        ),
        in_specs=[vmem] * 5,
        out_specs=[vmem] * 11,
        name="finish",
    )(output, grad_input, in_share, out_share, mine)
    return results[:4] + (results[4].T,) + results[5:]


def fits(block_in, in_weight, out_weight, n):
    plane, line = split(n)
    share, rows = in_weight.shape[0], out_weight.shape[0]
    return (
        plane == 4 and line % 2 == 0 and share % 8 == 0 and rows % 16 == 0
        and block_in.shape[0] % (2 * LANES) == 0 and share >= SECTIONS
    )


def either(*args):
    n = lax.axis_size("fsdp")
    chosen = fused_device if fits(args[0], args[4], args[11], n) else per_device
    return chosen(*args)


def solution(mesh):
    rows, vec, whole = P("fsdp", None), P("fsdp"), P()
    in_specs = (rows, vec, vec, vec, rows, rows, vec, whole, whole, whole, vec, rows, rows)
    out_specs = (rows, rows, vec, rows, rows, vec, whole, whole, whole, vec, rows)
    return jax.shard_map(
        either, mesh=mesh, in_specs=in_specs, out_specs=out_specs, check_vma=False
    )
```

```python
import functools

import jax
import jax.numpy as jnp
from jax import lax
from jax.experimental import pallas as pl
from jax.experimental.pallas import tpu as pltpu
from jax.sharding import PartitionSpec as P

DI = 1536
STATE = 128
HDIM = 64
KCONV = 4
HEADS = 24
CONV = 1792
LANES = 128
EPSILON = 1e-05
HIGHEST = lax.Precision.HIGHEST
F32 = jnp.float32
BF16 = jnp.bfloat16
NT = (((1,), (1,)), ((), ()))
TN = (((0,), (0,)), ((), ()))
MESH = pl.DeviceIdType.MESH


def rms_scale(values, gain_vec):
    return (
        values * lax.rsqrt(jnp.mean(values * values, axis=-1, keepdims=True) + EPSILON) * gain_vec
    )


def dot(a, b, dims=(((1,), (0,)), ((), ()))):
    return lax.dot_general(a.astype(BF16), b.astype(BF16), dims, preferred_element_type=F32)


def sigmoid(v):
    return 1.0 / (1.0 + jnp.exp(-v))


def softplus(v):
    return jnp.maximum(v, 0.0) + jnp.log1p(jnp.exp(-jnp.abs(v)))


def chunk_ds(i):
    return pl.ds(pl.multiple_of(i * LANES, LANES), LANES)


def head_prelude(raw_ref, segc, segr, bias_ref, rate_ref):
    length = raw_ref.shape[0]
    rows = lax.broadcasted_iota(jnp.int32, (length, length), 0)
    cols = lax.broadcasted_iota(jnp.int32, (length, length), 1)
    mask = ((rows >= cols) & (segc == segr)).astype(F32)
    shifted = raw_ref[...] + bias_ref[...]
    step = softplus(shifted)
    decay = -step * rate_ref[...]
    running = jnp.dot(mask, decay, precision=HIGHEST, preferred_element_type=F32)
    return mask, shifted, step, decay, running


def column(values, h):
    lane = lax.broadcasted_iota(jnp.int32, values.shape, 1)
    return jnp.sum(jnp.where(lane == h, values, 0.0), axis=1, keepdims=True)


def decay_of(mask_ref, run_ref, run_t_ref, h):
    spread = column(run_ref[...], h) - run_t_ref[pl.ds(h, 1), :]
    mask = mask_ref[...]
    return jnp.where(mask > 0, jnp.exp(jnp.where(mask > 0, spread, 0.0)), 0.0)


def forward_kernel(
    proj_ref, raw_ref, segc_ref, segr_ref, shift_ref, cw_ref, bias_ref, rate_ref, skip_ref, gain_ref,
    pre_ref, scan_ref, low_ref,
    mask_s, run_s, runt_s, stept_s, inter_s, gated_s,
):
    length = proj_ref.shape[0]
    mask, _, step, _, running = head_prelude(
        raw_ref, segc_ref[...], segr_ref[...], bias_ref, rate_ref
    )
    mask_s[...] = mask
    run_s[...] = running
    runt_s[...] = running.T
    stept_s[...] = step.T

    def conv(i, _):
        ds = chunk_ds(i)
        x = proj_ref[:, chunk_ds(i + DI // LANES)]
        total = cw_ref[KCONV : KCONV + 1, ds] + cw_ref[KCONV - 1 : KCONV, ds] * x
        for j in range(1, KCONV):
            moved = pltpu.roll(x, j, 0) * shift_ref[:, j - 1 : j]
            total = total + cw_ref[KCONV - 1 - j : KCONV - j, ds] * moved
        pre_ref[:, ds] = total
        return 0

    lax.fori_loop(0, CONV // LANES, conv, 0)
    pre_k = pre_ref[:, DI : DI + STATE]
    pre_q = pre_ref[:, DI + STATE :]
    inter_s[...] = dot(pre_q * sigmoid(pre_q), pre_k * sigmoid(pre_k), NT)

    def pair(i, sumsq):
        ds = chunk_ds(i)
        pre = pre_ref[:, ds]
        values = pre * sigmoid(pre)
        low = values.astype(BF16)
        outs = []
        for side in range(2):
            h = 2 * i + side
            weights = decay_of(mask_s, run_s, runt_s, h) * inter_s[...] * stept_s[pl.ds(h, 1), :]
            outs.append(dot(weights, low))
        lane = lax.broadcasted_iota(jnp.int32, (length, LANES), 1)
        scanned = jnp.where(lane < HDIM, outs[0], outs[1]) + skip_ref[:, ds] * values
        scan_ref[:, ds] = scanned
        z = proj_ref[:, ds]
        gated = scanned * (z * sigmoid(z))
        gated_s[:, ds] = gated
        return sumsq + gated * gated

    sumsq = lax.fori_loop(0, DI // LANES, pair, jnp.zeros((length, LANES), F32))
    scale = lax.rsqrt(jnp.sum(sumsq, axis=1, keepdims=True) / DI + EPSILON)

    def finish(i, _):
        ds = chunk_ds(i)
        low_ref[:, ds] = (gated_s[:, ds] * scale * gain_ref[:, ds]).astype(BF16)
        return 0

    lax.fori_loop(0, DI // LANES, finish, 0)


def backward_kernel(
    proj_ref, raw_ref, segc_ref, segr_ref, shift_ref, cw_ref, bias_ref, rate_ref, skip_ref, gain_ref,
    pre_ref, scan_ref, gm_ref,
    glow_ref, graw_ref, gconv_ref, gdi_ref, ghead_ref,
    mask_s, run_s, runt_s, stept_s, inter_s, dinter_s, row_s, col_s,
):
    length = proj_ref.shape[0]
    mask, shifted, step, decay, running = head_prelude(
        raw_ref, segc_ref[...], segr_ref[...], bias_ref, rate_ref
    )
    mask_s[...] = mask
    run_s[...] = running
    runt_s[...] = running.T
    stept_s[...] = step.T
    pre_k = pre_ref[:, DI : DI + STATE]
    pre_q = pre_ref[:, DI + STATE :]
    keys = (pre_k * sigmoid(pre_k)).astype(BF16)
    queries = (pre_q * sigmoid(pre_q)).astype(BF16)
    inter_s[...] = dot(queries, keys, NT)
    dinter_s[...] = jnp.zeros_like(dinter_s)
    row_s[...] = jnp.zeros_like(row_s)
    col_s[...] = jnp.zeros_like(col_s)
    gconv_ref[...] = jnp.zeros_like(gconv_ref)
    gdi_ref[...] = jnp.zeros_like(gdi_ref)
    ghead_ref[...] = jnp.zeros_like(ghead_ref)

    def sums(i, carry):
        sumsq, inner = carry
        ds = chunk_ds(i)
        z = proj_ref[:, ds]
        gated = scan_ref[:, ds] * (z * sigmoid(z))
        return sumsq + gated * gated, inner + gated * gm_ref[:, ds] * gain_ref[:, ds]

    zero = jnp.zeros((length, LANES), F32)
    sumsq, inner = lax.fori_loop(0, DI // LANES, sums, (zero, zero))
    scale = lax.rsqrt(jnp.sum(sumsq, axis=1, keepdims=True) / DI + EPSILON)
    coef = scale * scale * scale * (jnp.sum(inner, axis=1, keepdims=True) / DI)

    def conv_back(i, grad_act):
        ds = chunk_ds(i)
        wide = chunk_ds(i + DI // LANES)
        pre = pre_ref[:, ds]
        sg = sigmoid(pre)
        gpre = grad_act * (sg * (1.0 + pre * (1.0 - sg)))
        x = proj_ref[:, wide]
        total = cw_ref[KCONV - 1 : KCONV, ds] * gpre
        gconv_ref[KCONV : KCONV + 1, ds] = jnp.sum(gpre, axis=0, keepdims=True)
        gconv_ref[KCONV - 1 : KCONV, ds] = jnp.sum(gpre * x, axis=0, keepdims=True)
        for j in range(1, KCONV):
            live = gpre * shift_ref[:, j - 1 : j]
            back = pltpu.roll(live, length - j, 0)
            total = total + cw_ref[KCONV - 1 - j : KCONV - j, ds] * back
            gconv_ref[KCONV - 1 - j : KCONV - j, ds] = jnp.sum(back * x, axis=0, keepdims=True)
        glow_ref[:, wide] = total.astype(BF16)

    def pair(i, _):
        ds = chunk_ds(i)
        z = proj_ref[:, ds]
        sz = sigmoid(z)
        silu_z = z * sz
        scanned = scan_ref[:, ds]
        gated = scanned * silu_z
        grad_out = gm_ref[:, ds]
        gdi_ref[0:1, ds] = jnp.sum(grad_out * gated * scale, axis=0, keepdims=True)
        dgated = scale * (grad_out * gain_ref[:, ds]) - gated * coef
        dscan = dgated * silu_z
        glow_ref[:, ds] = (dgated * scanned * (sz * (1.0 + z * (1.0 - sz)))).astype(BF16)
        pre = pre_ref[:, ds]
        values = pre * sigmoid(pre)
        gdi_ref[1:2, ds] = jnp.sum(dscan * values, axis=0, keepdims=True)
        low = values.astype(BF16)
        dlow = dscan.astype(BF16)
        lane = lax.broadcasted_iota(jnp.int32, (length, LANES), 1)
        head_lane = lax.broadcasted_iota(jnp.int32, (length, LANES), 1)
        outs = []
        for side in range(2):
            h = 2 * i + side
            here = (lane < HDIM) if side == 0 else (lane >= HDIM)
            factor = decay_of(mask_s, run_s, runt_s, h)
            stept = stept_s[pl.ds(h, 1), :]
            inter = inter_s[...]
            scaled = factor * stept
            outs.append(dot(scaled * inter, dlow, TN))
            dweights = dot(jnp.where(here, dscan, 0.0), low, NT)
            dinter_s[...] += dweights * scaled
            pairs = dweights * factor * inter
            col_s[pl.ds(h, 1), :] = jnp.sum(pairs, axis=0, keepdims=True)
            row = jnp.sum(pairs * stept, axis=1, keepdims=True)
            row_s[...] += jnp.where(head_lane == h, row, 0.0)
        grad_values = jnp.where(lane < HDIM, outs[0], outs[1]) + skip_ref[:, ds] * dscan
        conv_back(i, grad_values)
        return 0

    lax.fori_loop(0, DI // LANES, pair, 0)
    dinter = dinter_s[...].astype(BF16)
    conv_back(DI // LANES, dot(dinter, queries, TN))
    conv_back(DI // LANES + 1, dot(dinter, keys))
    dstep = col_s[...].T
    drun = row_s[...] - dstep * step
    ddecay = lax.dot_general(
        mask_s[...], drun, TN, precision=HIGHEST, preferred_element_type=F32
    )
    dstep = dstep - ddecay * rate_ref[...]
    graw = dstep * sigmoid(shifted)
    graw_ref[...] = graw.astype(BF16)
    ghead_ref[0:1, :] = jnp.sum(graw, axis=0, keepdims=True)
    ghead_ref[1:2, :] = jnp.sum(ddecay * decay, axis=0, keepdims=True)


def forward_mixer(proj, raw, small):
    length = proj.shape[0]
    vec = pltpu.VMEM
    return pl.pallas_call(
        forward_kernel,
        out_shape=(
            jax.ShapeDtypeStruct((length, CONV), F32),
            jax.ShapeDtypeStruct((length, DI), F32),
            jax.ShapeDtypeStruct((length, DI), BF16),
        ),
        in_specs=[pl.BlockSpec(memory_space=vec)] * 10,
        out_specs=[pl.BlockSpec(memory_space=vec)] * 3,
        scratch_shapes=[
            pltpu.VMEM((length, length), F32),
            pltpu.VMEM((length, LANES), F32),
            pltpu.VMEM((LANES, length), F32),
            pltpu.VMEM((LANES, length), F32),
            pltpu.VMEM((length, length), F32),
            pltpu.VMEM((length, DI), F32),
        ],
        compiler_params=pltpu.CompilerParams(vmem_limit_bytes=40 * 2**20),
        cost_estimate=pl.CostEstimate(
            flops=HEADS * length * length * 280, bytes_accessed=length * 30000, transcendentals=0
        ),
        name="mixer_forward",
    )(proj, raw, *small)


def backward_mixer(proj, raw, small, pre, scanned, grad_mixer):
    length, width = proj.shape[0], DI + CONV
    vec = pltpu.VMEM
    return pl.pallas_call(
        backward_kernel,
        out_shape=(
            jax.ShapeDtypeStruct((length, width), BF16),
            jax.ShapeDtypeStruct((length, LANES), BF16),
            jax.ShapeDtypeStruct((8, CONV), F32),
            jax.ShapeDtypeStruct((8, DI), F32),
            jax.ShapeDtypeStruct((8, LANES), F32),
        ),
        in_specs=[pl.BlockSpec(memory_space=vec)] * 13,
        out_specs=[pl.BlockSpec(memory_space=vec)] * 5,
        scratch_shapes=[
            pltpu.VMEM((length, length), F32),
            pltpu.VMEM((length, LANES), F32),
            pltpu.VMEM((LANES, length), F32),
            pltpu.VMEM((LANES, length), F32),
            pltpu.VMEM((length, length), F32),
            pltpu.VMEM((length, length), F32),
            pltpu.VMEM((length, LANES), F32),
            pltpu.VMEM((LANES, length), F32),
        ],
        compiler_params=pltpu.CompilerParams(vmem_limit_bytes=40 * 2**20),
        cost_estimate=pl.CostEstimate(
            flops=HEADS * length * length * 800, bytes_accessed=length * 60000, transcendentals=0
        ),
        name="mixer_backward",
    )(proj, raw, *small, pre, scanned, grad_mixer)


def place(n):
    me = lax.axis_index("fsdp")
    core, chip = lax.rem(me, 2), lax.div(me, 2)
    plane, line = split(n)
    return me, core, lax.rem(chip, plane), lax.div(chip, plane)


def split(n):
    half = n // 2
    plane = 4 if half % 4 == 0 else 1
    return plane, half // plane


def loop(count, step):
    def body(k, _):
        step(k)
        return 0

    lax.fori_loop(0, count, body, 0)


def greet(n, me, core, spot, rank):
    plane, line = split(n)
    barrier = pltpu.get_barrier_semaphore()

    def signal(device):
        pl.semaphore_signal(barrier, inc=1, device_id=(device,), device_id_type=MESH)

    signal(me + 1 - 2 * core)
    for j in range(plane - 1):
        signal(2 * (rank * plane + lax.rem(spot + 1 + j, plane)) + core)
    loop(line - 1, lambda r: signal(2 * (lax.rem(rank + 1 + r, line) * plane + spot) + core))
    pl.semaphore_wait(barrier, plane + line - 1)


def gather_kernel(
    n, x0, x1, x2, o0, o1, o2, own_sem, s_line, r_line, s_plane, r_plane, s_near, r_near
):
    plane, line = split(n)
    me, core, spot, rank = place(n)
    partner = me + 1 - 2 * core
    greet(n, me, core, spot, rank)
    groups = ((x0, o0), (x1, o1), (x2, o2))

    def send(g, src, slot, sems, index, device):
        return pltpu.make_async_remote_copy(
            src_ref=src,
            dst_ref=groups[g][1].at[slot],
            send_sem=sems[0].at[g, index],
            recv_sem=sems[1].at[g, index],
            device_id=(device,),
            device_id_type=MESH,
        )

    def origin(r, j):
        from_rank = lax.rem(rank + 2 * line - 1 - r, line)
        return 2 * (from_rank * plane + lax.rem(spot + 2 * plane - 1 - j, plane))

    def along(g, r, slot):
        device = 2 * (lax.rem(rank + 1 + r, line) * plane + spot) + core
        return send(g, groups[g][0], slot, (s_line, r_line), r, device)

    def across(g, r, j, src, slot):
        device = 2 * (rank * plane + lax.rem(spot + 1 + j, plane)) + core
        return send(g, src, slot, (s_plane, r_plane), plane * r + j, device)

    def near(g, r, j, src, slot):
        return send(g, src, slot, (s_near, r_near), plane * r + j, partner)

    def start_along(r):
        for g in range(3):
            along(g, r, me).start()

    loop(line - 1, start_along)
    for g in range(3):
        x = groups[g][0]
        for j in range(plane - 1):
            across(g, line - 1, j, x, me).start()
        near(g, line - 1, plane - 1, x, me).start()
        pltpu.make_async_copy(x, groups[g][1].at[me], own_sem.at[g]).start()

    def forward(r):
        for j in range(plane - 1):
            slot = origin(r, j) + core
            for g in range(3):
                block = groups[g][1].at[slot]
                across(g, r, j, block, slot).wait_recv()
                near(g, r, j, block, slot).start()

    def spread(r):
        slot = origin(r, plane - 1) + core
        for g in range(3):
            block = groups[g][1].at[slot]
            along(g, r, slot).wait_recv()
            for j in range(plane - 1):
                across(g, r, j, block, slot).start()
            near(g, r, plane - 1, block, slot).start()
        forward(lax.rem(r + line - 1, line))

    loop(line - 1, spread)
    forward((line - 2) % line)

    def drain(r):
        for j in range(plane):
            slot, other = origin(r, j) + core, origin(r, j) + 1 - core
            for g in range(3):
                block = groups[g][1].at[slot]
                near(g, r, j, block, other).wait_recv()
                near(g, r, j, block, slot).wait_send()
                if j < plane - 1:
                    across(g, r, j, block, slot).wait_send()

    loop(line, drain)

    def drain_along(r):
        for g in range(3):
            along(g, r, me).wait_send()

    loop(line - 1, drain_along)
    for g in range(3):
        pltpu.make_async_copy(groups[g][0], groups[g][1].at[me], own_sem.at[g]).wait()


def reduce_kernel(
    n, a0, a1, a2, o0, o1, o2, p0, p1, p2, t0, t1, t2, q0, q1, q2,
    u0, u1, u2, v0, v1, v2, w0, w1, w2,
    s_near, r_near, s_plane, r_plane, s_line, r_line,
):
    plane, line = split(n)
    me, core, spot, rank = place(n)
    partner = me + 1 - 2 * core
    greet(n, me, core, spot, rank)
    groups = (
        (a0, o0, p0, t0, q0, u0, v0, w0),
        (a1, o1, p1, t1, q1, u1, v1, w1),
        (a2, o2, p2, t2, q2, u2, v2, w2),
    )

    def send(src, dst, sems, g, index, device):
        return pltpu.make_async_remote_copy(
            src_ref=src.at[index] if not isinstance(src, tuple) else src[0].at[src[1]],
            dst_ref=dst.at[index],
            send_sem=sems[0].at[g, index],
            recv_sem=sems[1].at[g, index],
            device_id=(device,),
            device_id_type=MESH,
        )

    def owner(r, j):
        return 2 * (lax.rem(rank + 1 + r, line) * plane + lax.rem(spot + 1 + j, plane))

    def near(g, r, j):
        src = (groups[g][0], owner(r, j) + 1 - core)
        return send(src, groups[g][2], (s_near, r_near), g, plane * r + j, partner)

    def across(g, r, j):
        device = 2 * (rank * plane + lax.rem(spot + 1 + j, plane)) + core
        return send(groups[g][3], groups[g][4], (s_plane, r_plane), g, plane * r + j, device)

    def along(g, r):
        device = 2 * (lax.rem(rank + 1 + r, line) * plane + spot) + core
        return send(groups[g][6], groups[g][7], (s_line, r_line), g, r, device)

    def both(g, r, j):
        near(g, r, j).wait_recv()
        return groups[g][0][owner(r, j) + core].astype(F32) + groups[g][2][plane * r + j].astype(F32)

    def start_near(r):
        for j in range(plane):
            for g in range(3):
                near(g, r, j).start()

    loop(line, start_near)

    def pairs(r):
        for j in range(plane):
            for g in range(3):
                if j < plane - 1:
                    sums = groups[g][3]
                    sums[plane * r + j] = both(g, r, j).astype(sums.dtype)
                else:
                    groups[g][5][r] = both(g, r, j)
            if j > 0:
                for g in range(3):
                    across(g, r, j - 1).start()

    def total(g, r):
        result = groups[g][5][r]
        for j in range(plane - 1):
            across(g, r, j).wait_recv()
            result = result + groups[g][4][plane * r + j].astype(F32)
        return result

    def planes(r):
        for g in range(3):
            sums = groups[g][6]
            sums[r] = total(g, r).astype(sums.dtype)
        for g in range(3):
            along(g, r).start()

    def step(r):
        pairs(r)

        @pl.when(r > 0)
        def _():
            planes(r - 1)

    loop(line, step)
    for g in range(3):
        groups[g][1][...] = total(g, line - 1)

    def collect(r):
        for g in range(3):
            along(g, r).wait_recv()
            groups[g][1][...] += groups[g][7][r].astype(F32)

    loop(line - 1, collect)

    def drain(r):
        for g in range(3):
            for j in range(plane):
                near(g, r, j).wait_send()
                if j < plane - 1:
                    across(g, r, j).wait_send()

    loop(line, drain)

    def drain_along(r):
        for g in range(3):
            along(g, r).wait_send()

    loop(line - 1, drain_along)


def gather_all(n, shards):
    vmem = pl.BlockSpec(memory_space=pltpu.VMEM)
    half, (_, line) = n // 2, split(n)
    return pl.pallas_call(
        functools.partial(gather_kernel, n),
        out_shape=tuple(jax.ShapeDtypeStruct((n,) + x.shape, x.dtype) for x in shards),
        in_specs=[vmem] * 3,
        out_specs=[vmem] * 3,
        scratch_shapes=[
            pltpu.SemaphoreType.DMA((3,)),
            pltpu.SemaphoreType.DMA((3, line)),
            pltpu.SemaphoreType.DMA((3, line)),
            pltpu.SemaphoreType.DMA((3, half)),
            pltpu.SemaphoreType.DMA((3, half)),
            pltpu.SemaphoreType.DMA((3, half)),
            pltpu.SemaphoreType.DMA((3, half)),
        ],
        compiler_params=pltpu.CompilerParams(
            collective_id=0, has_side_effects=True, vmem_limit_bytes=60 * 2**20
        ),
        name="gather_all",
    )(*shards)


def reduce_all(n, terms):
    vmem = pl.BlockSpec(memory_space=pltpu.VMEM)
    half, (_, line) = n // 2, split(n)
    slots = [pltpu.VMEM((half,) + x.shape[1:], x.dtype) for x in terms]
    partial_sums = [pltpu.VMEM((line,) + x.shape[1:], F32) for x in terms]
    lines = [pltpu.VMEM((line,) + x.shape[1:], x.dtype) for x in terms]
    return pl.pallas_call(
        functools.partial(reduce_kernel, n),
        out_shape=tuple(jax.ShapeDtypeStruct(x.shape[1:], F32) for x in terms),
        in_specs=[vmem] * 3,
        out_specs=[vmem] * 3,
        scratch_shapes=slots * 3
        + partial_sums
        + lines * 2
        + [pltpu.SemaphoreType.DMA((3, half))] * 4
        + [pltpu.SemaphoreType.DMA((3, line))] * 2,
        compiler_params=pltpu.CompilerParams(
            collective_id=1, has_side_effects=True, vmem_limit_bytes=60 * 2**20
        ),
        name="reduce_all",
    )(*terms)


def per_device(
    block_in,
    segment_ids,
    live_count,
    norm_gain,
    in_weight,
    conv_weight,
    conv_bias,
    step_bias,
    decay_log,
    skip_gain,
    gated_gain,
    out_weight,
    out_cotangent,
):
    devices = lax.axis_size("fsdp")
    length = block_in.shape[0]
    share, proj_width = in_weight.shape
    width = block_in.shape[1]
    smalls = jnp.concatenate(
        [norm_gain, conv_weight.T.reshape(-1), conv_bias, gated_gain]
    )
    small_rows = -(-smalls.shape[0] // (8 * LANES)) * 8
    smalls = jnp.pad(smalls, (0, small_rows * LANES - smalls.shape[0])).reshape(small_rows, LANES)
    in_blocks, out_blocks, rest = gather_all(devices, (in_weight, out_weight, smalls))
    in_full = in_blocks.reshape(devices * share, proj_width)
    out_full = out_blocks.reshape(devices * out_weight.shape[0], width)
    rest = rest.reshape(devices, -1).astype(F32)
    a = norm_gain.shape[0]
    b = a + conv_weight.size
    c = b + conv_bias.shape[0]
    d = c + gated_gain.shape[0]
    gain_norm = rest[:, :a].reshape(-1)
    kernel_rows = jnp.moveaxis(rest[:, a:b].reshape(devices, KCONV, -1), 1, 0).reshape(KCONV, CONV)
    kernel_bias = rest[:, b:c].reshape(1, CONV)
    gated = rest[:, c:d].reshape(1, DI)
    conv_rows = jnp.concatenate([kernel_rows, kernel_bias, jnp.zeros((3, CONV), F32)], axis=0)

    def lanes(v):
        return jnp.pad(v, (0, LANES - v.shape[0])).reshape(1, LANES)

    slots = jnp.arange(length)
    shift = jnp.stack(
        [
            ((slots >= j) & (jnp.roll(segment_ids, j) == segment_ids)).astype(F32)
            for j in range(1, KCONV)
        ],
        axis=1,
    )
    shift = jnp.pad(shift, ((0, 0), (0, 8 - shift.shape[1])))
    small = (
        segment_ids.reshape(length, 1),
        segment_ids.reshape(1, length),
        shift,
        conv_rows,
        lanes(step_bias),
        lanes(jnp.exp(decay_log)),
        jnp.repeat(skip_gain, HDIM).reshape(1, DI),
        gated,
    )
    source = block_in.astype(F32)
    live_rows = (lax.iota(jnp.int32, length) < live_count[0]).astype(F32)
    masked = jnp.where(live_rows[:, None] > 0, out_cotangent, jnp.zeros_like(out_cotangent))
    normed = rms_scale(source, gain_norm).astype(BF16)
    main = DI + CONV
    projected = jnp.dot(normed, in_full[:, :main], preferred_element_type=F32)
    tail = jnp.pad(in_full[:, main:], ((0, 0), (0, LANES - HEADS)))
    raw = jnp.dot(normed, tail, preferred_element_type=F32)
    grad_mixer = lax.dot_general(masked, out_full, NT, preferred_element_type=F32)
    pre, scanned, mixer_low = forward_mixer(projected, raw, small)
    grad_out_w = lax.dot_general(mixer_low, masked, TN, preferred_element_type=F32)
    branch = jnp.dot(mixer_low, out_full, preferred_element_type=F32)
    output = (source + live_rows[:, None] * branch).astype(BF16)
    glow, graw, gconv, gdi, ghead = backward_mixer(projected, raw, small, pre, scanned, grad_mixer)
    grad_low = jnp.concatenate([glow, graw], axis=1)
    grad_in_w = lax.dot_general(normed, grad_low, TN, preferred_element_type=F32)
    grad_normed = lax.dot_general(glow, in_full[:, :main], NT, preferred_element_type=F32)
    grad_normed = grad_normed + lax.dot_general(graw, tail, NT, preferred_element_type=F32)
    _, norm_vjp = jax.vjp(rms_scale, source, gain_norm)
    grad_source, grad_gain = norm_vjp(grad_normed)
    grad_input = out_cotangent.astype(F32) + grad_source
    skip_part = gdi[1].reshape(HEADS, HDIM).sum(axis=1)
    heads = jnp.concatenate([ghead[0, :HEADS], ghead[1, :HEADS], skip_part])
    rows = jnp.concatenate(
        [
            grad_gain.reshape(devices, -1),
            jnp.moveaxis(gconv[:KCONV].reshape(KCONV, devices, -1), 0, 1).reshape(devices, -1),
            gconv[KCONV].reshape(devices, -1),
            gdi[0].reshape(devices, -1),
            jnp.broadcast_to(heads, (devices, heads.shape[0])),
        ],
        axis=1,
    )
    sum_rows = -(-rows.shape[1] // (8 * LANES)) * 8
    rows = jnp.pad(rows, ((0, 0), (0, sum_rows * LANES - rows.shape[1])))
    in_share, out_share, mine = reduce_all(
        devices,
        (
            grad_in_w.astype(BF16).reshape(devices, share, -1),
            grad_out_w.astype(BF16).reshape(devices, -1, width),
            rows.reshape(devices, sum_rows, LANES),
        ),
    )
    in_share = in_share[:, :proj_width]
    mine = mine.reshape(-1)
    head_sums = mine[d : d + 3 * HEADS].reshape(3, HEADS)
    return (
        output,
        grad_input,
        mine[:a],
        in_share,
        mine[a:b].reshape(KCONV, -1).T,
        mine[b:c],
        head_sums[0],
        head_sums[1],
        head_sums[2],
        mine[c:d],
        out_share,
    )


SECTIONS = 16


def lower(index, length):
    return pl.ds(pl.multiple_of(index * length, length), length)


class Spot:
    def __init__(self, n):
        self.plane, self.line = split(n)
        self.me, self.core, self.spot, self.rank = place(n)
        self.partner = self.me + 1 - 2 * self.core
        bit0, bit1 = lax.rem(self.spot, 2), lax.div(self.spot, 2)
        self.x = self.spot + 1 - 2 * bit0
        self.y = self.spot + 2 - 4 * bit1
        self.d = 3 - self.spot

    def device(self, rank, spot):
        return 2 * (rank * self.plane + spot) + self.core

    def greet(self):
        barrier = pltpu.get_barrier_semaphore()

        def signal(device):
            pl.semaphore_signal(barrier, inc=1, device_id=(device,), device_id_type=MESH)

        signal(self.partner)
        signal(self.device(self.rank, self.x))
        signal(self.device(self.rank, self.y))
        for k in range(1, self.line):
            signal(self.device(lax.rem(self.rank + k, self.line), self.spot))
        pl.semaphore_wait(barrier, self.line + 2)


def remote(src, dst, send_sem, recv_sem, device):
    return pltpu.make_async_remote_copy(
        src_ref=src, dst_ref=dst, send_sem=send_sem, recv_sem=recv_sem,
        device_id=(device,), device_id_type=MESH,
    )


class Gather:
    def __init__(self, at, buf, rows, g, s_line, r_line, s_plane, r_plane, s_near, r_near):
        self.at, self.buf, self.rows, self.g = at, buf, rows, g
        self.sems = (s_line, r_line, s_plane, r_plane, s_near, r_near)

    def block(self, half, rank, spot):
        return self.buf.at[half, lower(rank * self.at.plane + spot, self.rows)]

    def move(self, half, rank, spot, send, recv, device):
        ref = self.block(half, rank, spot)
        return remote(ref, ref, send, recv, device)

    def step(self, rank, way):
        at, g = self.at, self.g
        s_line, r_line = self.sems[:2]
        device = at.device(at.rank + way, at.spot)
        side = 0 if way > 0 else 1
        return self.move(at.core, rank, at.spot, s_line.at[g, side, rank], r_line.at[g, rank], device)

    def across(self, rank, kind):
        at, g = self.at, self.g
        s_plane, r_plane = self.sems[2:4]
        spot, to = (
            (at.spot, at.x), (at.spot, at.y), (at.x, at.y), (at.y, at.x)
        )[kind]
        slot = min(kind, 2)
        return self.move(
            at.core, rank, spot, s_plane.at[g, slot, rank], r_plane.at[g, slot, rank],
            at.device(at.rank, to),
        )

    def arrived(self, rank, kind):
        at, g = self.at, self.g
        s_plane, r_plane = self.sems[2:4]
        spot = (at.x, at.y, at.d)[kind]
        self.move(
            at.core, rank, spot, s_plane.at[g, kind, rank], r_plane.at[g, kind, rank],
            at.device(at.rank, at.x),
        ).wait_recv()

    def near(self, half, rank):
        at, g = self.at, self.g
        s_near, r_near = self.sems[4:]
        ref = self.buf.at[half, lower(rank, at.plane * self.rows)]
        return remote(ref, ref, s_near.at[g, rank], r_near.at[g, rank], at.partner)

    def spread(self, rank):
        self.across(rank, 0).start()
        self.across(rank, 1).start()

    def own(self):
        at = self.at

        @pl.when(at.rank < at.line - 1)
        def _():
            self.step(at.rank, 1).start()

        @pl.when(at.rank > 0)
        def _():
            self.step(at.rank, -1).start()

        self.spread(at.rank)

    def line_event(self, rank, below):
        at = self.at
        self.step(rank, 1).wait_recv()
        if below:
            @pl.when(at.rank < at.line - 1)
            def _():
                self.step(rank, 1).start()
        else:
            @pl.when(at.rank > 0)
            def _():
                self.step(rank, -1).start()
        self.spread(rank)

    def plane_event(self, rank, below=None):
        at = self.at
        self.arrived(rank, 0)

        @pl.when(lax.rem(rank, 2) == 0)
        def _():
            self.across(rank, 2).start()

        self.arrived(rank, 1)

        @pl.when(lax.rem(rank, 2) == 1)
        def _():
            self.across(rank, 3).start()


    def diagonal_event(self, rank, below=None):
        self.arrived(rank, 2)
        self.near(self.at.core, rank).start()

    def away(self, k, event):
        at = self.at

        @pl.when(at.rank >= k)
        def _():
            event(at.rank - k, True)

        @pl.when(at.rank + k < at.line)
        def _():
            event(at.rank + k, False)

    def events(self):
        at, out = self.at, []
        for k in range(at.line + 2):
            if k == 0:
                out.append(self.own)
            elif k < at.line:
                out.append(functools.partial(self.away, k, self.line_event))
            if k == 1:
                out.append(functools.partial(self.plane_event, at.rank))
            elif 1 < k <= at.line:
                out.append(functools.partial(self.away, k - 1, self.plane_event))
            if k == 2:
                out.append(functools.partial(self.diagonal_event, at.rank))
            elif k > 2:
                out.append(functools.partial(self.away, k - 2, self.diagonal_event))
        return out

    def finish(self):
        at = self.at
        loop(at.line, lambda rank: self.near(1 - at.core, rank).wait_recv())

    def drain(self):
        at = self.at
        loop(at.line, lambda rank: self.near(at.core, rank).wait_send())

        def ranks(rank):
            for kind in range(3):
                self.across(rank, kind).wait_send()

            @pl.when((at.rank < at.line - 1) & (rank <= at.rank))
            def _():
                self.step(rank, 1).wait_send()

            @pl.when((at.rank > 0) & (rank >= at.rank))
            def _():
                self.step(rank, -1).wait_send()

        loop(at.line, ranks)


class Reduce:
    def __init__(self, at, index, refs, send, recv):
        self.at, self.index = at, index
        self.part, self.near_in, self.x1, self.y1, self.x2, self.y2 = refs[:6]
        self.out, self.line_in, self.total, self.last_in = refs[6:]
        self.send, self.recv = send, recv

    def copy(self, k, src, dst, device):
        return remote(src, dst, self.send.at[self.index, k], self.recv.at[self.index, k], device)

    def near(self, k):
        at = self.at
        spot = (at.d, at.y, at.x, at.spot)[k]
        return self.copy(k, self.part.at[1 - at.core, :, spot], self.near_in.at[:, spot], at.partner)

    def start(self):
        for k in range(4):
            self.near(k).start()

    def first(self, side):
        at, half = self.at, self.at.line // 2
        src = self.part.at[at.core, pl.ds(side * half, half), at.d]
        to = at.device(at.rank, (at.x, at.y)[side])
        return self.copy(4 + side, src, (self.x1, self.y1)[side], to)

    def second(self, side):
        at = self.at
        spot = (at.x, at.y)[side]
        src = self.part.at[at.core, :, spot]
        return self.copy(6 + side, src, (self.x2, self.y2)[side], at.device(at.rank, spot))

    def along(self, k):
        at = self.at
        rank = lax.rem(at.rank + 1 + k, at.line)
        return self.copy(9 + k, self.out.at[rank], self.line_in.at[k], at.device(rank, at.spot))

    def last(self):
        at = self.at
        rows = self.last_in.shape[0]
        return self.copy(8, self.total.at[lower(1 - at.core, rows)], self.last_in, at.partner)

    def pair(self, k, ranks=slice(None)):
        at = self.at
        spot = (at.d, at.y, at.x, at.spot)[k]
        return self.part[at.core, ranks, spot].astype(F32) + self.near_in[ranks, spot].astype(F32)

    def pairs(self):
        at = self.at
        self.near(0).wait_recv()
        self.part[at.core, :, at.d] = self.pair(0).astype(BF16)
        self.first(0).start()
        self.first(1).start()

    def planes(self):
        at, half = self.at, self.at.line // 2
        for side, spot in ((0, at.y), (1, at.x)):
            self.near(1 + side).wait_recv()
            self.first(side).wait_recv()
            for part in range(2):
                ranks = slice(part * half, (part + 1) * half)
                mine = self.pair(1 + side, ranks)
                if part == side:
                    mine = mine + (self.x1, self.y1)[side][...].astype(F32)
                self.part[at.core, ranks, spot] = mine.astype(BF16)
            self.second(1 - side).start()

    def lines(self):
        at = self.at
        self.near(3).wait_recv()
        self.second(0).wait_recv()
        self.second(1).wait_recv()
        mine = self.pair(3) + self.x2[...].astype(F32) + self.y2[...].astype(F32)
        self.out[...] = mine.astype(BF16)
        for k in range(at.line - 1):
            self.along(k).start()
        mine = self.part[at.core, at.rank, at.spot].astype(F32)
        mine = mine + self.near_in[at.rank, at.spot].astype(F32)
        self.total[...] = mine + self.x2[at.rank].astype(F32) + self.y2[at.rank].astype(F32)

    def ends(self):
        at = self.at
        for k in range(at.line - 1):
            self.along(k).wait_recv()
        total = self.total[...]
        for k in range(at.line - 1):
            total = total + self.line_in[k].astype(F32)
        self.total[...] = total
        self.last().start()

    def halves(self):
        at = self.at
        self.last().wait_recv()
        rows = self.last_in.shape[0]
        mine, other = self.total[lower(at.core, rows), :], self.last_in[...]
        first = at.core == 0
        return jnp.where(first, mine, other), jnp.where(first, other, mine)

    def drain(self):
        for k in range(4):
            self.near(k).wait_send()
        for side in range(2):
            self.first(side).wait_send()
            self.second(side).wait_send()
        for k in range(self.at.line - 1):
            self.along(k).wait_send()
        self.last().wait_send()


def owner_mask(n, count):
    share = count // n
    rows = lax.broadcasted_iota(jnp.int32, (n, count), 0) * share
    cols = lax.broadcasted_iota(jnp.int32, (n, count), 1)
    return (cols >= rows) & (cols < rows + share)


def lane_pick(share, count):
    lane = lax.broadcasted_iota(jnp.int32, (LANES, count), 0).astype(F32)
    col = lax.broadcasted_iota(jnp.int32, (LANES, count), 1).astype(F32)
    owner = jnp.floor((col + 0.5) * (1.0 / share))
    return jnp.where(col - owner * share == lane, 1.0, 0.0)


def fused_scratch(n, length, width, share, rows, chunks):
    _, line = split(n)
    wide, half_out, half_z = CONV, width // 2, DI // 2
    conv_w = half_z + 2 * LANES
    shapes = dict(
        stage_c=((2, share, conv_w), F32), staged_c=((share, conv_w), F32),
        stage_z=((2, share, half_z), F32), staged_z=((share, half_z), F32),
        own=((2, rows, half_out), BF16), win_c=((2, n * share, conv_w), BF16),
        win_z=((2, n * share, half_z), BF16), wout=((2, n * rows, half_out), BF16),
        mask=((length, length), F32), neg=((length, length), F32),
        shift=((KCONV - 1, length, LANES), F32), unit=((length, width), F32),
        inv=((length, LANES), F32), masked=((length, width), BF16),
        normed=((length, width), BF16), normt=((width, length), BF16),
        enorm=((LANES, width), BF16), econv=((LANES, CONV), BF16), egate=((LANES, DI), BF16),
        eskip=((LANES, DI), F32), psel=((SECTIONS * n, n * share), BF16),
        cw=((8, CONV), F32), gate=((8, DI), F32), skip=((8, DI), F32), gain=((8, width), F32),
        proj=((length, 2 * wide), F32), pre=((length, CONV), F32), scan=((length, DI), F32),
        gated=((length, DI), F32), low=((length, DI), BF16), gm=((length, DI), F32),
        glow=((length, 2 * wide), BF16),
        run=((length, LANES), F32), runt=((LANES, length), F32), stept=((LANES, length), F32),
        inter=((length, length), F32), dinter=((length, length), F32),
        row=((length, LANES), F32), col=((LANES, length), F32),
        gconv=((8, CONV), F32), gdi=((8, DI), F32), misc=((8, LANES), F32),
    )
    names = list(shapes)
    specs = [pltpu.VMEM(*v) for v in shapes.values()]
    for tall, w in chunks:
        for dims, kind in (
            ((2, line, 4, tall, w), BF16), ((line, 4, tall, w), BF16),
            ((line // 2, tall, w), BF16), ((line // 2, tall, w), BF16),
            ((line, tall, w), BF16), ((line, tall, w), BF16),
            ((line, tall, w), BF16), ((line - 1, tall, w), BF16),
            ((tall, w), F32), ((tall // 2, w), F32),
        ):
            specs.append(pltpu.VMEM(dims, kind))
    sems = [
        (3, 2, line), (3, line), (3, 3, line), (3, 3, line), (3, line), (3, line),
        (3,), (3,), (len(chunks), 8 + line), (len(chunks), 8 + line),
    ]
    return names, specs + [pltpu.SemaphoreType.DMA(s) for s in sems]


def fused_kernel(n, names, chunks, x_ref, ct_ref, inw_ref, outw_ref,
                 norm_ref, taps_ref, cbias_ref, gated_ref, bias_ref, rate_ref, skip_ref, seg_ref, live_ref,
                 out_ref, gx_ref, gi_ref, go_ref, gs_ref, *scratch):
    at = Spot(n)
    core = at.core
    v = dict(zip(names, scratch))
    rest = scratch[len(names):]
    items_refs = [rest[10 * i : 10 * i + 10] for i in range(len(chunks))]
    sems = rest[10 * len(chunks):]
    s_own, r_own, s_red, r_red = sems[6:]
    length, width = x_ref.shape
    share, proj_width = inw_ref.shape
    rows = outw_ref.shape[0]
    chip = at.rank * at.plane + at.spot
    tail = DI + CONV
    wout, win_c, win_z, stage_c, stage_z = (
        v[k] for k in ("wout", "win_c", "win_z", "stage_c", "stage_z")
    )
    hz = DI // 2
    spare = hz + LANES

    def put(ref, row, lane, values):
        ref[..., row : row + values.shape[0], lane : lane + values.shape[1]] = values.astype(F32)

    for half in range(2):
        stage_c[half, :, :hz] = inw_ref[:, DI + half * hz : DI + (half + 1) * hz].astype(F32)
    stage_c[0, :, hz:] = inw_ref[:, 2 * DI : tail].astype(F32)
    stage_c[1, :, hz:] = jnp.zeros((share, 2 * LANES), F32)
    tile = stage_c.at[1]
    put(tile, 0, hz, inw_ref[:, tail:])
    put(tile, 0, spare, norm_ref[...][None])
    put(tile, 1, spare, taps_ref[...])
    put(tile, 1 + KCONV, spare, cbias_ref[...][None])
    put(tile, 2 + KCONV, spare, gated_ref[...][None])
    at.greet()

    def exchange(g, src, dst):
        return remote(src, dst, s_own.at[g], r_own.at[g], at.partner)

    my_rows = pl.ds(pl.multiple_of((2 * chip + core) * rows, rows), rows)
    near_c = exchange(0, stage_c.at[1 - core], v["staged_c"])
    near_z = exchange(1, stage_z.at[1 - core], v["staged_z"])
    near_out = exchange(2, v["own"].at[1 - core], wout.at[1 - core, my_rows])
    near_c.start()
    for half in range(2):
        stage_z[half] = inw_ref[:, half * hz : (half + 1) * hz].astype(F32)
        v["own"][half] = outw_ref[:, half * (width // 2) : (half + 1) * (width // 2)]
    near_z.start()
    near_out.start()
    wout[core, my_rows, :] = v["own"][core]
    first = core == 0

    def settle(near, stage, staged, win):
        near.wait_recv()
        mine, other = stage[core], staged[...]
        pair = jnp.concatenate(
            [jnp.where(first, mine, other), jnp.where(first, other, mine)], axis=0
        )
        win[core, lower(chip, 2 * share), :] = pair.astype(BF16)

    settle(near_c, stage_c, v["staged_c"], win_c)
    gathers = [
        Gather(at, buf, tall, g, *sems[:6])
        for g, (buf, tall) in enumerate(((win_c, 2 * share), (win_z, 2 * share), (wout, 2 * rows)))
    ]
    events = [g.events() for g in gathers]

    def run_events(order):
        for g, k in order:
            events[g][k]()

    run_events([(0, 0)])
    settle(near_z, stage_z, v["staged_z"], win_z)
    misc = v["misc"]
    misc[...] = jnp.zeros_like(misc)
    put(misc, 0, 0, bias_ref[...][None])
    put(misc, 1, 0, rate_ref[...][None])
    put(misc, 2, 0, skip_ref[...][None])

    segr = seg_ref[...][None].astype(F32)
    segc = jnp.broadcast_to(segr, (LANES, length)).T
    slots = lax.broadcasted_iota(jnp.int32, (length, LANES), 0)
    for j in range(1, KCONV):
        same = (slots >= j) & (pltpu.roll(segc, j, 0) == segc)
        v["shift"][j - 1] = jnp.where(same, 1.0, 0.0)
    below = lax.broadcasted_iota(jnp.int32, (length, length), 0) >= lax.broadcasted_iota(
        jnp.int32, (length, length), 1
    )
    seg_wide = jnp.concatenate([segc] * (length // LANES), axis=1)
    linked = below & (seg_wide == segr)
    v["mask"][...] = jnp.where(linked, 1.0, 0.0)
    v["neg"][...] = jnp.where(linked, 0.0, -1e30)
    x = x_ref[...].astype(F32)
    inv = lax.rsqrt(jnp.mean(x * x, axis=-1, keepdims=True) + EPSILON)
    v["inv"][...] = jnp.broadcast_to(inv, (length, LANES))
    v["unit"][...] = x * inv
    live = slots[:, :1] < live_ref[...][None]
    v["masked"][...] = jnp.where(live, ct_ref[...].astype(F32), 0.0).astype(BF16)
    v["enorm"][...] = lane_pick(width // n, width).astype(BF16)
    v["econv"][...] = lane_pick(CONV // n, CONV).astype(BF16)
    v["egate"][...] = lane_pick(DI // n, DI).astype(BF16)
    head = lax.broadcasted_iota(jnp.int32, (LANES, DI), 0) * HDIM
    channel = lax.broadcasted_iota(jnp.int32, (LANES, DI), 1)
    v["eskip"][...] = jnp.where((channel >= head) & (channel < head + HDIM), 1.0, 0.0)
    place_col = lax.broadcasted_iota(jnp.int32, (n, n * share), 1)
    place_row = lax.broadcasted_iota(jnp.int32, (n, n * share), 0) * share
    for k in range(SECTIONS):
        v["psel"][k * n : (k + 1) * n, :] = jnp.where(place_col == place_row + k, 1.0, 0.0).astype(BF16)
    v["skip"][...] = jnp.dot(
        jnp.broadcast_to(misc[2:3, :], (8, LANES)), v["eskip"][...],
        precision=HIGHEST, preferred_element_type=F32,
    )
    bias_row = misc[0:1, :]
    rate_row = jnp.exp(misc[1:2, :])

    run_events(
        [(0, 1), (0, 2), (1, 0), (0, 3), (0, 4), (0, 5), (1, 1), (1, 2), (0, 6), (0, 7), (0, 8)]
        + [(1, 3), (1, 4), (0, 9), (0, 10), (1, 5)]
    )
    near_out.wait_recv()
    run_events([(2, 0), (0, 11), (1, 6)])
    gathers[0].finish()
    left = [(1, 7), (1, 8), (2, 1), (1, 9), (2, 2), (1, 10), (2, 3), (1, 11), (2, 4)]
    left += [(2, k) for k in range(5, 12)]

    def pump(count):
        run_events(left[:count])
        del left[:count]

    vectors = dot(v["psel"][: 8 * n, :], win_c[1, :, spare:])

    def spread_vector(k, pick, count):
        wide = dot(vectors[k * n : (k + 1) * n, :], pick)
        return jnp.sum(jnp.where(owner_mask(n, count), wide, 0.0), axis=0, keepdims=True)

    gain = spread_vector(0, v["enorm"][...], width)
    v["gain"][0:1, :] = gain
    exact = v["unit"][...] * gain
    v["normed"][...] = exact.astype(BF16)
    normed = v["normed"]
    part = dot(normed[...], win_c[0])
    v["proj"][:, CONV : CONV + hz] = part[:, :hz]
    v["proj"][:, DI:CONV] = part[:, hz:]
    v["proj"][:, CONV + hz : CONV + DI + LANES] = dot(normed[...], win_c[1, :, :spare])
    pump(2)
    for k in range(KCONV + 1):
        v["cw"][k : k + 1, :] = spread_vector(1 + k, v["econv"][...], CONV)
    v["gate"][0:1, :] = spread_vector(KCONV + 2, v["egate"][...], DI)
    proj, pre, scan, low = v["proj"], v["pre"], v["scan"], v["low"]
    cw, gate, skip = v["cw"], v["gate"], v["skip"]
    shifted = proj[:, 2 * CONV - 2 * LANES : 2 * CONV - LANES] + bias_row
    step = softplus(shifted)
    decay = -step * rate_row
    running = jnp.dot(v["mask"][...], decay, precision=HIGHEST, preferred_element_type=F32)
    v["run"][...] = running
    v["runt"][...] = running.T
    v["stept"][...] = step.T
    inter, stept, run, runt, neg = v["inter"], v["stept"], v["run"], v["runt"], v["neg"]

    def conv_tile(i):
        return chunk_ds(i + CONV // LANES) if not isinstance(i, int) else slice(i * LANES, (i + 1) * LANES)

    def conv(ds, wide):
        xs = proj[:, wide]
        total = cw[KCONV : KCONV + 1, ds] + cw[KCONV - 1 : KCONV, ds] * xs
        for j in range(1, KCONV):
            moved = pltpu.roll(xs, j, 0) * v["shift"][j - 1]
            total = total + cw[KCONV - 1 - j : KCONV - j, ds] * moved
        pre[:, ds] = total
        return total

    pre_k = conv(slice(DI, DI + LANES), slice(DI, DI + LANES))
    pre_q = conv(slice(DI + LANES, CONV), slice(DI + LANES, CONV))
    keys = (pre_k * sigmoid(pre_k)).astype(BF16)
    queries = (pre_q * sigmoid(pre_q)).astype(BF16)
    inter[...] = dot(queries, keys, NT)
    lane = lax.broadcasted_iota(jnp.int32, (length, LANES), 1)

    def factor_of(h):
        spread = column(run[...], h) - runt[pl.ds(h, 1), :]
        return jnp.exp(spread + neg[...])

    def forward_pair(i):
        ds = chunk_ds(i)
        total = conv(ds, conv_tile(i))
        values = total * sigmoid(total)
        low_values = values.astype(BF16)
        outs = []
        for side in range(2):
            h = 2 * i + side
            weights = factor_of(h) * inter[...] * stept[pl.ds(h, 1), :]
            outs.append(dot(weights, low_values))
        scan[:, ds] = jnp.where(lane < HDIM, outs[0], outs[1]) + skip[0:1, ds] * values

    pairs = DI // LANES
    cuts = 4
    for k in range(cuts):
        pump(2)
        loop(pairs // cuts, lambda i, k=k: forward_pair(i + k * (pairs // cuts)))
    while (1, 11) in left:
        pump(1)
    gathers[1].finish()
    for half in range(2):
        proj[:, half * hz : (half + 1) * hz] = dot(normed[...], win_z[half])
    pump(2)

    def gate_tile(i, sumsq):
        ds = chunk_ds(i)
        z = proj[:, ds]
        gated = scan[:, ds] * (z * sigmoid(z))
        v["gated"][:, ds] = gated
        return sumsq + gated * gated

    sumsq = lax.fori_loop(0, pairs, gate_tile, jnp.zeros((length, LANES), F32))
    pump(2)
    scale = lax.rsqrt(jnp.sum(sumsq, axis=1, keepdims=True) / DI + EPSILON)

    def finish(i, _):
        ds = chunk_ds(i)
        low[:, ds] = (v["gated"][:, ds] * scale * gate[0:1, ds]).astype(BF16)
        return 0

    lax.fori_loop(0, pairs, finish, 0)
    items = [Reduce(at, k, refs, s_red, r_red) for k, refs in enumerate(items_refs)]
    weights_item, columns = items[0], items[1:]
    for half in range(2):
        part = dot(low[...], v["masked"][:, half * (width // 2) : (half + 1) * (width // 2)], TN)
        weights_item.part[half] = part.astype(BF16).reshape(weights_item.part.shape[1:])
    weights_item.start()
    pump(99)
    gathers[2].finish()
    weights_item.pairs()
    for half in range(2):
        term = dot(v["masked"][:, half * (width // 2) : (half + 1) * (width // 2)], wout[half], NT)
        v["gm"][...] = term if half == 0 else v["gm"][...] + term
    v["normt"][...] = (v["unit"][...] * v["gain"][0:1, :]).T.astype(BF16)

    dinter, row_s, col_s, gconv, gdi = v["dinter"], v["row"], v["col"], v["gconv"], v["gdi"]
    glow, gm = v["glow"], v["gm"]
    for ref in (dinter, row_s, col_s, gconv, gdi):
        ref[...] = jnp.zeros_like(ref)

    def sums(i, inner):
        ds = chunk_ds(i)
        return inner + v["gated"][:, ds] * gm[:, ds] * gate[0:1, ds]

    inner = lax.fori_loop(0, pairs, sums, jnp.zeros((length, LANES), F32))
    coef = scale * scale * scale * (jnp.sum(inner, axis=1, keepdims=True) / DI)

    def conv_back(ds, wide, grad_act):
        pre_c = pre[:, ds]
        sg = sigmoid(pre_c)
        gpre = grad_act * (sg * (1.0 + pre_c * (1.0 - sg)))
        xs = proj[:, wide]
        total = cw[KCONV - 1 : KCONV, ds] * gpre
        gconv[KCONV : KCONV + 1, ds] = jnp.sum(gpre, axis=0, keepdims=True)
        gconv[KCONV - 1 : KCONV, ds] = jnp.sum(gpre * xs, axis=0, keepdims=True)
        for j in range(1, KCONV):
            back = pltpu.roll(gpre * v["shift"][j - 1], length - j, 0)
            total = total + cw[KCONV - 1 - j : KCONV - j, ds] * back
            gconv[KCONV - 1 - j : KCONV - j, ds] = jnp.sum(back * xs, axis=0, keepdims=True)
        glow[:, wide] = total.astype(BF16)

    def backward_pair(i):
        ds = chunk_ds(i)
        z = proj[:, ds]
        sz = sigmoid(z)
        silu_z = z * sz
        scanned = scan[:, ds]
        gated = v["gated"][:, ds]
        grad_out = gm[:, ds]
        gdi[0:1, ds] = jnp.sum(grad_out * gated * scale, axis=0, keepdims=True)
        dgated = scale * (grad_out * gate[0:1, ds]) - gated * coef
        dscan = dgated * silu_z
        glow[:, ds] = (dgated * scanned * (sz * (1.0 + z * (1.0 - sz)))).astype(BF16)
        pre_c = pre[:, ds]
        values = pre_c * sigmoid(pre_c)
        gdi[1:2, ds] = jnp.sum(dscan * values, axis=0, keepdims=True)
        low_values = values.astype(BF16)
        dlow = dscan.astype(BF16)
        outs = []
        for side in range(2):
            h = 2 * i + side
            here = (lane < HDIM) if side == 0 else (lane >= HDIM)
            mine = jnp.where(here, dscan, 0.0).astype(BF16)
            until = column(run[...], h)
            until_row, step_all = runt[pl.ds(h, 1), :], stept[pl.ds(h, 1), :]
            parts, cols, sums_of_rows = [], [], []
            for begin, end in ((0, length // 2), (length // 2, length)):
                here_rows, seen = slice(begin, end), slice(0, end)
                spread = until[here_rows] - until_row[:, seen]
                factor = jnp.exp(spread + neg[here_rows, seen])
                step_row = step_all[:, seen]
                scaled = factor * step_row
                inter_part = inter[here_rows, seen]
                parts.append(dot(scaled * inter_part, dlow[here_rows], TN))
                dweights = dot(mine[here_rows], low_values[seen], NT)
                dinter[here_rows, seen] += dweights * scaled
                products = dweights * factor * inter_part
                cols.append(jnp.sum(products, axis=0, keepdims=True))
                sums_of_rows.append(jnp.sum(products * step_row, axis=1, keepdims=True))
            half = length // 2
            outs.append(jnp.concatenate([parts[0] + parts[1][:half], parts[1][half:]], axis=0))
            col_s[pl.ds(h, 1), :] = jnp.concatenate(
                [cols[0] + cols[1][:, :half], cols[1][:, half:]], axis=1
            )
            row = jnp.concatenate(sums_of_rows, axis=0)
            row_s[...] += jnp.where(lane == h, row, 0.0)
        grad_values = jnp.where(lane < HDIM, outs[0], outs[1]) + skip[0:1, ds] * dscan
        conv_back(ds, conv_tile(i), grad_values)

    def launch(k):
        item = columns[k]
        w = item.part.shape[-1]
        for half in range(2):
            cols = slice(half * CONV + k * w, half * CONV + (k + 1) * w)
            part = dot(v["normt"][...], glow[:, cols])
            item.part[half] = part.astype(BF16).reshape(item.part.shape[1:])
        item.start()

    schedule = {
        2: [lambda: launch(0)],
        3: [columns[0].pairs],
        4: [weights_item.planes],
        5: [lambda: launch(1)],
        6: [columns[1].pairs],
        7: [columns[0].planes],
        8: [lambda: launch(2)],
        9: [columns[2].pairs],
        11: [lambda: launch(3)],
    }

    def backward_step(i):
        backward_pair(i)
        for when, todo in schedule.items():
            @pl.when(i == when)
            def _(todo=todo):
                for event in todo:
                    event()

    loop(pairs, backward_step)
    columns[1].planes()
    low_dinter = dinter[...].astype(BF16)
    conv_back(slice(DI, DI + LANES), slice(DI, DI + LANES), dot(low_dinter, queries, TN))
    conv_back(slice(DI + LANES, CONV), slice(DI + LANES, CONV), dot(low_dinter, keys))
    columns[3].pairs()
    weights_item.lines()
    dstep = col_s[...].T
    drun = row_s[...] - dstep * step
    ddecay = lax.dot_general(v["mask"][...], drun, TN, precision=HIGHEST, preferred_element_type=F32)
    dstep = dstep - ddecay * rate_row
    graw = dstep * sigmoid(shifted)
    glow[:, 2 * CONV - 2 * LANES : 2 * CONV - LANES] = graw.astype(BF16)
    columns[0].lines()
    columns[2].planes()
    grad_normed = dot(glow[:, :hz], win_z[0], NT) + dot(glow[:, hz:DI], win_z[1], NT)
    grad_normed = grad_normed + dot(glow[:, CONV : CONV + hz], win_c[0, :, :hz], NT)
    grad_normed = grad_normed + dot(glow[:, DI:CONV], win_c[0, :, hz:], NT)
    grad_normed = grad_normed + dot(
        glow[:, CONV + hz : 2 * CONV - LANES], win_c[1, :, :spare], NT
    )
    unit = v["unit"][...]
    grad_gain = jnp.sum(grad_normed * unit, axis=0, keepdims=True)
    columns[1].lines()

    def owners(vector, pick):
        wide = jnp.where(owner_mask(n, vector.shape[1]), vector, 0.0)
        return dot(wide, pick, NT)

    skip_part = lax.dot_general(
        gdi[...], v["eskip"][...], NT, precision=HIGHEST, preferred_element_type=F32
    )
    per_head = [
        jnp.sum(graw, axis=0, keepdims=True), jnp.sum(ddecay * decay, axis=0, keepdims=True),
        skip_part[1:2, :],
    ]
    stacked = [owners(grad_gain, v["enorm"][...])]
    stacked += [owners(gconv[k : k + 1, :], v["econv"][...]) for k in range(KCONV + 1)]
    stacked += [owners(gdi[0:1, :], v["egate"][...])]
    stacked += [jnp.broadcast_to(row, (n, LANES)) for row in per_head]
    stacked += [jnp.zeros((n, LANES), F32)] * (SECTIONS - len(stacked))
    spread_rows = dot(v["psel"][...], jnp.concatenate(stacked, axis=0), TN)
    final = columns[4]
    shape = final.part.shape[1:]
    final.part[0] = dot(v["normt"][...], glow[:, DI:CONV]).astype(BF16).reshape(shape)
    raw_part = dot(v["normt"][...], glow[:, 2 * CONV - 2 * LANES : 2 * CONV - LANES])
    final.part[1] = jnp.concatenate([raw_part, spread_rows], axis=1).astype(BF16).reshape(shape)
    final.start()
    columns[3].planes()
    final.pairs()
    weights_item.ends()
    grad_unit = grad_normed * v["gain"][0:1, :]
    mean = jnp.mean(grad_unit * unit, axis=-1, keepdims=True)
    gx_ref[...] = ct_ref[...].astype(F32) + v["inv"][:, :1] * (grad_unit - unit * mean)
    columns[2].lines()
    final.planes()
    columns[0].ends()
    columns[3].lines()
    for half in range(2):
        cols = slice(half * (width // 2), (half + 1) * (width // 2))
        branch = dot(low[...], wout[half])
        out_ref[:, cols] = (
            x_ref[:, cols].astype(F32) + jnp.where(live, branch, 0.0)
        ).astype(BF16)
    columns[1].ends()
    columns[2].ends()
    final.lines()
    columns[3].ends()
    final.ends()
    go_ref[:, : width // 2], go_ref[:, width // 2 :] = weights_item.halves()
    for k in range(4):
        w = columns[k].part.shape[-1]
        gi_ref[:, k * w : (k + 1) * w], gi_ref[:, DI + k * w : DI + (k + 1) * w] = columns[k].halves()
    gi_ref[:, 2 * DI : tail], ends = final.halves()
    gi_ref[:, tail:] = ends[:, : proj_width - tail]
    gs_ref[...] = ends[:, LANES:]
    for near in (near_c, near_z, near_out):
        near.wait_send()
    for gather in gathers:
        gather.drain()
    for item in items:
        item.drain()


def finish_kernel(
    out_ref, gx_ref, gi_ref, go_ref, gs_ref,
    output, grad_input, norm, in_share, taps, bias, step, decay, skip, gated, out_share, done,
):
    moves = ((gx_ref, grad_input), (out_ref, output), (gi_ref, in_share), (go_ref, out_share))
    copies = [pltpu.make_async_copy(src, dst, done.at[k]) for k, (src, dst) in enumerate(moves)]
    for copy in copies:
        copy.start()
    norm[...] = gs_ref[0, : norm.shape[0]]
    taps[...] = gs_ref[1 : 1 + KCONV, : taps.shape[1]]
    bias[...] = gs_ref[1 + KCONV, : bias.shape[0]]
    gated[...] = gs_ref[2 + KCONV, : gated.shape[0]]
    step[...] = gs_ref[3 + KCONV, :HEADS]
    decay[...] = gs_ref[4 + KCONV, :HEADS]
    skip[...] = gs_ref[5 + KCONV, :HEADS]
    for copy in copies:
        copy.wait()


def fused_device(
    block_in, segment_ids, live_count, norm_gain, in_weight, conv_weight, conv_bias, step_bias,
    decay_log, skip_gain, gated_gain, out_weight, out_cotangent,
):
    n = lax.axis_size("fsdp")
    length, width = block_in.shape
    share, proj_width = in_weight.shape
    rows = out_weight.shape[0]
    chunks = [(2 * rows, width // 2)] + [(2 * share, DI // 4)] * 4 + [(2 * share, 2 * LANES)]
    names, scratch = fused_scratch(n, length, width, share, rows, chunks)
    vmem = pl.BlockSpec(memory_space=pltpu.VMEM)
    output, grad_input, in_share, out_share, mine = pl.pallas_call(
        functools.partial(fused_kernel, n, names, chunks),
        out_shape=(
            jax.ShapeDtypeStruct((length, width), BF16),
            jax.ShapeDtypeStruct((length, width), F32),
            jax.ShapeDtypeStruct((share, proj_width), F32),
            jax.ShapeDtypeStruct((rows, width), F32),
            jax.ShapeDtypeStruct((share, LANES), F32),
        ),
        in_specs=[vmem] * 13,
        out_specs=[vmem] * 5,
        scratch_shapes=scratch,
        compiler_params=pltpu.CompilerParams(
            collective_id=2, has_side_effects=True, vmem_limit_bytes=60 * 2**20
        ),
        name="layer",
    )(
        block_in, out_cotangent, in_weight, out_weight, norm_gain, conv_weight.T, conv_bias,
        gated_gain, step_bias, decay_log, skip_gain, segment_ids, live_count,
    )
    taps, gated_share = conv_weight.shape[0], gated_gain.shape[0]
    vector = lambda size: jax.ShapeDtypeStruct((size,), F32)
    whole = pl.BlockSpec(memory_space=pl.ANY)
    results = pl.pallas_call(
        finish_kernel,
        out_shape=(
            jax.ShapeDtypeStruct((length, width), BF16),
            jax.ShapeDtypeStruct((length, width), F32),
            vector(norm_gain.shape[0]),
            jax.ShapeDtypeStruct((share, proj_width), F32),
            jax.ShapeDtypeStruct((KCONV, taps), F32),
            vector(taps), vector(HEADS), vector(HEADS), vector(HEADS), vector(gated_share),
            jax.ShapeDtypeStruct((rows, width), F32),
        ),
        in_specs=[whole] * 4 + [vmem],
        out_specs=[whole] * 2 + [vmem, whole] + [vmem] * 6 + [whole],
        scratch_shapes=[pltpu.SemaphoreType.DMA((4,))],
        name="finish",
    )(output, grad_input, in_share, out_share, mine)
    return results[:4] + (results[4].T,) + results[5:]


def fits(block_in, in_weight, out_weight, n):
    plane, line = split(n)
    share, rows = in_weight.shape[0], out_weight.shape[0]
    return (
        plane == 4 and line % 2 == 0 and share % 8 == 0 and rows % 16 == 0
        and block_in.shape[0] % (2 * LANES) == 0 and share >= SECTIONS
    )


def either(*args):
    n = lax.axis_size("fsdp")
    chosen = fused_device if fits(args[0], args[4], args[11], n) else per_device
    return chosen(*args)


def solution(mesh):
    rows, vec, whole = P("fsdp", None), P("fsdp"), P()
    in_specs = (rows, vec, vec, vec, rows, rows, vec, whole, whole, whole, vec, rows, rows)
    out_specs = (rows, rows, vec, rows, rows, vec, whole, whole, whole, vec, rows)
    return jax.shard_map(
        either, mesh=mesh, in_specs=in_specs, out_specs=out_specs, check_vma=False
    )
```
